32 devices in a mesh: facet: 4 (over x, core), col: 8 (over z, y).
Axes of the slice: x: 2, y: 2, z: 4, core: 2. Of those that a mesh axis runs over, the one named last changes fastest.
Arguments:
- facet_spectra: bfloat16 [2, 4, 2, 512, 8192], P(None, 'facet', None, None, 'col'), may hold values from -6 to 6
- facet_offsets: int32 [4, 2], P('facet'), may hold values from 0 to 65535
- column_index: int32 [2], replicated, may hold values from 0 to 145
- subgrid_offsets: int32 [2, 8], P(None, 'col'), may hold values from 0 to 65528, as said below
- weights: bfloat16 [2, 8, 512, 512], P(None, 'col', 'facet'), may hold values from 0.25 to 4
Outputs:
- subgrids: bfloat16 [2, 8, 2, 512, 512], P(None, 'col', None, 'facet')
- facet_updates: bfloat16 [2, 4, 2, 512, 8192], P(None, 'facet', None, None, 'col')
The draws below stay inside these ranges and needn't reach their ends.
Inputs may be any that keep to these rules, and one draw needn't show every extreme that they name: `subgrid_offsets`: every offset is a multiple of 8; subgrid s of a column has position p = offset / 8 with (s // 1) * 1024 <= p < (s + 1) * 1024. In every column some subgrid has p exactly at such a lower end, and some subgrid has p at (s + 1) * 1024 - 128 // 2 + 1 or above.
All inputs are finite; a program needn't handle non-finite values.
Results may differ from the reference program's by a relative error of at most 0.015.
Values may be sent and summed in bfloat16 or wider, within the bound.
No kernel may reach another device: no remote copies, remote signals or barrier semaphores. Data moves between devices by JAX's collectives and lax.ppermute only.
A program may use at most 64 MiB of HBM per device.

```python
import math
import jax
import jax.numpy as jnp
from jax import lax

IMAGE = 65536
XM = 512
WM = 128
YP_DEV = 1024
YP = 8192
XA = 448
COLS = 2
SUB_DEV = 1
SUBS = 8
FACETS = 4
N_FACET = 4
N_COL = 8


def draw_subgrid_offsets(key, part):
    half = WM // 2
    span = YP_DEV // SUB_DEV
    key_inner, key_first, key_last, key_variety, key_pick, key_opposite = jax.random.split(key, 6)
    slots = jnp.arange(SUB_DEV, dtype=jnp.int32)[None, None, :]
    shards = jnp.arange(N_COL, dtype=jnp.int32)[None, :, None]
    inner = slots * span + jax.random.randint(key_inner, (COLS, N_COL, SUB_DEV), 0, span)
    first = jax.random.randint(key_first, (COLS, N_COL, SUB_DEV), 0, half)
    last = YP_DEV - half + 1 + jax.random.randint(key_last, (COLS, N_COL, SUB_DEV), 0, half - 1)
    variety = jax.random.randint(key_variety, (COLS, N_COL, SUB_DEV), 0, 3)
    places = jnp.where(variety == 0, first, jnp.where(variety == 1, last, inner))
    chosen = jax.random.randint(key_pick, (COLS, 1, 1), 0, N_COL)
    opposite = (chosen + 1 + jax.random.randint(key_opposite, (COLS, 1, 1), 0, N_COL - 1)) % N_COL
    places = jnp.where((shards == chosen) & (slots == 0), 0, places)
    places = jnp.where((shards == opposite) & (slots == SUB_DEV - 1), last, places)
    centres = places + shards * YP_DEV
    return (centres * (IMAGE // (YP_DEV * N_COL))).reshape(COLS, SUB_DEV * N_COL).astype(jnp.int32)


def place_ends(entries, stream_key, low, high):
    longest = entries.shape.index(max(entries.shape))
    spots = []
    for shift in (0, 1):
        where = [jax.random.randint(jax.random.fold_in(stream_key, axis), (), 0, length) for axis, length in enumerate(entries.shape)]
        where[longest] = (where[longest] + shift) % entries.shape[longest]
        spots.append(tuple(where))
    return entries.at[spots[0]].set(low).at[spots[1]].set(high)


def levels(key, extent, cuts, least, largest):
    loudness, own = 1.0, jax.random.fold_in(key, 6)
    for position, blocks in cuts:
        steps = jnp.exp(jax.random.uniform(jax.random.fold_in(own, position), (blocks,), jnp.float32, least / len(cuts), largest / len(cuts)))
        loudness = loudness * jnp.repeat(steps, extent[position] // blocks).reshape([-1 if axis == position else 1 for axis in range(len(extent))])
    return loudness


def noise(own_key, extent, deviation, limit, cuts=(), kind=jnp.bfloat16):
    entries = deviation * jax.random.normal(own_key, extent, jnp.float32)
    if cuts:
        entries = entries * levels(own_key, extent, cuts, -0.22, 0.18)
    return jnp.clip(entries, -limit, limit).astype(kind)


def setup_inputs(seed: int = 0) -> dict:
    arg_keys = jax.random.split(jax.random.key(seed), 6)
    return {
        "facet_spectra": noise(arg_keys[0], (COLS, FACETS, 2, XM, YP), 1.0, 6.0, ((1, 4), (4, 8))),
        "facet_offsets": place_ends(jax.random.randint(arg_keys[1], (FACETS, 2), 0, IMAGE), jax.random.fold_in(arg_keys[1], 1), 0, IMAGE - 1).astype(jnp.int32),
        "column_index": jax.random.randint(arg_keys[2], (COLS,), 0, IMAGE // XA).astype(jnp.int32),
        "subgrid_offsets": draw_subgrid_offsets(jax.random.fold_in(arg_keys[5], 71), 0),
        "weights": jnp.clip(jnp.exp(math.log(4.0) - 2.7725887 * jax.random.uniform(arg_keys[4], (COLS, SUBS, XM, XM), jnp.float32) ** levels(arg_keys[4], (COLS, SUBS, XM, XM), ((1, 8), (2, 4)), -0.2, 0.2)), 0.25, 4.0).astype(jnp.bfloat16),
    }


TAU = 2.0 * math.pi

def modular(first, second, image):
    upper = second // 256
    lower = second % 256
    return (first * upper % (image // 256) * 256 + first * lower) % image

def make_table(facets):
    place = jnp.arange(WM, dtype=jnp.int32)
    cell = jnp.arange(XM, dtype=jnp.int32)
    turns = (place[:, None] - WM // 2) * (cell[None, :] - XM // 2) % XM
    angle = TAU * turns.astype(jnp.float32) / XM
    relative = (place.astype(jnp.float32) + 0.5 - WM / 2.0) / (WM / 2.0)
    taper = (0.3 + 0.7 * (1.0 - relative * relative)) / jnp.sqrt(jnp.float32(WM * facets))
    return ((taper[:, None] * jnp.cos(angle)).astype(jnp.bfloat16), (taper[:, None] * jnp.sin(angle)).astype(jnp.bfloat16))

def phases(column_pos, offsets, indices):
    first = modular(column_pos, offsets[0], IMAGE)
    second = indices * offsets[1] % YP
    return TAU * (first.astype(jnp.float32) / IMAGE + second.astype(jnp.float32) / YP)

def mult(form, left, right):
    return jnp.einsum(form, left.astype(jnp.float32), right.astype(jnp.float32), precision=lax.Precision.HIGHEST)

def reference(facet_spectra, facet_offsets, column_index, subgrid_offsets, weights):
    real_tab, imag_tab = make_table(N_FACET)
    grids = []
    updates = []
    for column in range(COLS):
        centres = subgrid_offsets[column] // (IMAGE // YP)
        indices = ((centres[:, None] - WM // 2 + jnp.arange(WM, dtype=jnp.int32)[None, :]) % YP).astype(jnp.int32)
        column_pos = column_index[column] * XA

        def add_facet(total, items):
            spectrum, offsets = items
            angle = phases(column_pos, offsets, indices)
            cosine = jnp.cos(angle)
            sine = jnp.sin(angle)
            window = spectrum[:, :, indices].astype(jnp.float32)
            real_part = (window[0] * cosine + window[1] * sine).astype(jnp.bfloat16)
            imag_part = (window[1] * cosine - window[0] * sine).astype(jnp.bfloat16)
            return (total + jnp.stack([real_part, imag_part]).astype(jnp.float32), None)
        start = jnp.zeros((2, XM, SUBS, WM), jnp.float32)
        summed, _ = lax.scan(add_facet, start, (facet_spectra[column], facet_offsets))
        grid_real = mult('xsm,ml->sxl', summed[0], real_tab) - mult('xsm,ml->sxl', summed[1], imag_tab)
        grid_imag = mult('xsm,ml->sxl', summed[0], imag_tab) + mult('xsm,ml->sxl', summed[1], real_tab)
        grid = jnp.stack([grid_real, grid_imag], axis=1).astype(jnp.bfloat16)
        grids.append(grid)
        scaled = (grid.astype(jnp.float32) * weights[column].astype(jnp.float32)[:, None]).astype(jnp.bfloat16)
        back_real = mult('sxl,ml->sxm', scaled[:, 0], real_tab) + mult('sxl,ml->sxm', scaled[:, 1], imag_tab)
        back_imag = mult('sxl,ml->sxm', scaled[:, 1], real_tab) - mult('sxl,ml->sxm', scaled[:, 0], imag_tab)

        def spread(offsets):
            angle = phases(column_pos, offsets, indices)
            cosine = jnp.cos(angle)[:, None, :]
            sine = jnp.sin(angle)[:, None, :]
            upd_real = back_real * cosine - back_imag * sine
            upd_imag = back_imag * cosine + back_real * sine
            pieces = jnp.stack([upd_real, upd_imag]).transpose(0, 2, 1, 3)
            target = jnp.zeros((2, XM, YP), jnp.float32)
            return target.at[:, :, indices].add(pieces).astype(jnp.bfloat16)
        updates.append(lax.map(spread, facet_offsets))
    return (jnp.stack(grids), jnp.stack(updates))
```

```python
import functools
import math

import jax
import jax.numpy as jnp
from jax import lax
from jax.experimental import pallas as pl
from jax.experimental.pallas import tpu as pltpu
from jax.sharding import PartitionSpec as P

IMAGE = 65536
XM = 512
WM = 128
XA = 448
LANES = 128
HALF = WM // 2

TAU = 2.0 * math.pi

VMEM = pl.BlockSpec(memory_space=pltpu.VMEM)
SMEM = pl.BlockSpec(memory_space=pltpu.SMEM)
ANY = pl.BlockSpec(memory_space=pl.ANY)


def make_table(facets):
    place = jnp.arange(WM, dtype=jnp.int32)
    cell = jnp.arange(XM, dtype=jnp.int32)
    turns = (place[:, None] - WM // 2) * (cell[None, :] - XM // 2) % XM
    angle = TAU * turns.astype(jnp.float32) / XM
    relative = (place.astype(jnp.float32) + 0.5 - WM / 2.0) / (WM / 2.0)
    taper = (0.3 + 0.7 * (1.0 - relative * relative)) / jnp.sqrt(jnp.float32(WM * facets))
    return (
        (taper[:, None] * jnp.cos(angle)).astype(jnp.bfloat16),
        (taper[:, None] * jnp.sin(angle)).astype(jnp.bfloat16),
    )


def remainder(value, modulus):
    if modulus & (modulus - 1) == 0:
        return value & (modulus - 1)
    return lax.rem(value, jnp.int32(modulus))


def modular(first, second, image):
    upper = second // 256
    lower = remainder(second, 256)
    return remainder(remainder(first * upper, image // 256) * 256 + first * lower, image)


def place_of(subgrid_offset, here, shard, length):
    start = subgrid_offset // (IMAGE // length) - here * shard - HALF + LANES
    return lax.div(start, jnp.int32(LANES)) - 1, remainder(start, LANES)


def lanes_of(shape):
    return lax.broadcasted_iota(jnp.int32, shape, len(shape) - 1)


def spectrum_kernel(
    cols, facets, length, offsets, column, subgrid, spectra, send, keep, turn, buf, sems
):
    shard = spectra.shape[4]
    tiles = shard // LANES
    block = XM // facets
    here = lax.axis_index("col")
    facet = lax.axis_index("facet")
    copies = []
    places = []
    for c in range(cols):
        tile, lane = place_of(subgrid[c, 0], here, shard, length)
        places.append((tile, lane))
        low = jnp.maximum(tile, 0)
        high = jnp.minimum(tile + 1, tiles - 1)
        for slot, which in enumerate((low, high, 0, tiles - 1)):
            at = which * LANES
            if not isinstance(at, int):
                at = pl.multiple_of(at, LANES)
            copy = pltpu.make_async_copy(
                spectra.at[c, 0, :, :, pl.ds(at, LANES)], buf.at[c, slot], sems.at[c, slot]
            )
            copy.start()
            copies.append(copy)
    lanes = lanes_of((1, LANES))
    base = here * shard
    for c in range(cols):
        tile, lane = places[c]
        first = modular(column[c] * XA, offsets[0, 0], IMAGE).astype(jnp.float32)
        at = base + lanes + jnp.where(lanes >= lane, tile, tile + 1) * LANES
        at = remainder(at + length, length)
        edge = base + lanes + jnp.where(lanes < HALF, 0, shard - LANES)
        for kind, index in enumerate((at, edge)):
            second = remainder(index * offsets[0, 1], length)
            angle = TAU * (first / IMAGE + second.astype(jnp.float32) / length)
            row = (c * 2 + kind) * 2
            turn[row : row + 1, :] = jnp.cos(angle)
            turn[row + 1 : row + 2, :] = jnp.sin(angle)
    for c in range(cols):
        tile, lane = places[c]
        for slot in range(4):
            copies[c * 4 + slot].wait()
        from_low = jnp.logical_and(lanes >= lane, tile >= 0)
        from_high = jnp.logical_and(lanes < lane, tile + 1 < tiles)
        for s in range(facets):
            rows = pl.ds(pl.multiple_of((facet ^ s) * block, block), block)
            target = send if s % 2 else keep
            parts = []
            for part in range(2):
                zero = jnp.zeros((block, LANES), jnp.float32)
                parts.append(
                    jnp.where(from_low, buf[c, 0, part, rows, :].astype(jnp.float32), zero)
                    + jnp.where(from_high, buf[c, 1, part, rows, :].astype(jnp.float32), zero)
                )
            row = c * 4
            cosine = turn[row : row + 1, :]
            sine = turn[row + 1 : row + 2, :]
            target[0, s // 2, c, 0] = (parts[0] * cosine + parts[1] * sine).astype(jnp.bfloat16)
            target[0, s // 2, c, 1] = (parts[1] * cosine - parts[0] * sine).astype(jnp.bfloat16)
            cosine = turn[row + 2 : row + 3, :]
            sine = turn[row + 3 : row + 4, :]
            parts = []
            for part in range(2):
                parts.append(
                    jnp.where(
                        lanes < HALF,
                        buf[c, 2, part, rows, :].astype(jnp.float32),
                        buf[c, 3, part, rows, :].astype(jnp.float32),
                    )
                )
            real = parts[0] * cosine + parts[1] * sine
            imag = parts[1] * cosine - parts[0] * sine
            real_turned = pltpu.roll(real, HALF, 1)
            imag_turned = pltpu.roll(imag, HALF, 1)
            target[1, s // 2, c, 0] = jnp.where(lanes < HALF, real, imag_turned).astype(
                jnp.bfloat16
            )
            target[1, s // 2, c, 1] = jnp.where(lanes < HALF, real_turned, imag).astype(
                jnp.bfloat16
            )


def subgrid_kernel(
    cols,
    length,
    shard,
    subgrid,
    main,
    from_prev,
    from_next,
    table,
    weights,
    grids,
    back,
    to_prev,
    to_next,
    stack,
    scaled,
):
    tiles = shard // LANES
    block = main.shape[2]
    here = lax.axis_index("col")
    lanes = lanes_of((1, LANES))
    for c in range(cols):
        tile, lane = place_of(subgrid[c, 0], here, shard, length)
        low = jnp.logical_and(lanes >= lane, tile < 0)
        high = jnp.logical_and(lanes < lane, tile + 1 >= tiles)
        prev = from_prev[c].astype(jnp.float32)
        nxt = from_next[c].astype(jnp.float32)
        shift = remainder(LANES - lane, LANES)
        zero = jnp.zeros((block, LANES), jnp.float32)
        real = main[c, 0].astype(jnp.float32)
        real = real + jnp.where(low, pltpu.roll(prev, HALF, 1), zero)
        real = real + jnp.where(high, nxt, zero)
        imag = main[c, 1].astype(jnp.float32)
        imag = imag + jnp.where(low, prev, zero)
        imag = imag + jnp.where(high, pltpu.roll(nxt, HALF, 1), zero)
        rows = slice(c * block, (c + 1) * block)
        stack[rows, :WM] = pltpu.roll(real, shift, 1).astype(jnp.bfloat16)
        stack[rows, WM:] = pltpu.roll(imag, shift, 1).astype(jnp.bfloat16)
    for part in range(2):
        span = slice(part * XM, (part + 1) * XM)
        product = jnp.dot(stack[...], table[:, span], preferred_element_type=jnp.float32)
        rounded = product.astype(jnp.bfloat16)
        for c in range(cols):
            rows = slice(c * block, (c + 1) * block)
            piece = rounded[rows]
            grids[c, 0, part] = piece
            scaled[rows, span] = (
                piece.astype(jnp.float32) * weights[c, 0].astype(jnp.float32)
            ).astype(jnp.bfloat16)
    result = lax.dot_general(
        scaled[...],
        table[...],
        (((1,), (1,)), ((), ())),
        preferred_element_type=jnp.float32,
    )
    for c in range(cols):
        tile, lane = place_of(subgrid[c, 0], here, shard, length)
        rows = slice(c * block, (c + 1) * block)
        low = jnp.logical_and(lanes >= lane, tile < 0)
        high = jnp.logical_and(lanes < lane, tile + 1 >= tiles)
        zero = jnp.zeros((block, LANES), jnp.float32)
        real = pltpu.roll(result[rows, :WM], lane, 1)
        imag = pltpu.roll(result[rows, WM:], lane, 1)
        back[c, 0] = real.astype(jnp.bfloat16)
        back[c, 1] = imag.astype(jnp.bfloat16)
        real_low = jnp.where(low, real, zero)
        imag_low = jnp.where(low, imag, zero)
        real_high = jnp.where(high, real, zero)
        imag_high = jnp.where(high, imag, zero)
        to_prev[c] = (pltpu.roll(real_low, HALF, 1) + imag_low).astype(jnp.bfloat16)
        to_next[c] = (real_high + pltpu.roll(imag_high, HALF, 1)).astype(jnp.bfloat16)


def update_kernel(
    cols, facets, length, subgrid, turn, even, odd, even_edge, odd_edge, out
):
    shard = out.shape[4]
    tiles = shard // LANES
    block = XM // facets
    here = lax.axis_index("col")
    facet = lax.axis_index("facet")
    lanes = lanes_of((1, LANES))
    c = pl.program_id(0)
    tile, lane = place_of(subgrid[c, 0], here, shard, length)
    out[...] = jnp.zeros(out.shape, jnp.bfloat16)
    low_at = pl.ds(pl.multiple_of(jnp.maximum(tile, 0) * LANES, LANES), LANES)
    high_at = pl.ds(pl.multiple_of(jnp.minimum(tile + 1, tiles - 1) * LANES, LANES), LANES)
    row = c * 4
    cosine = turn[pl.ds(row, 1), :]
    sine = turn[pl.ds(row + 1, 1), :]
    edge_cosine = turn[pl.ds(row + 2, 1), :]
    edge_sine = turn[pl.ds(row + 3, 1), :]
    is_low = lanes >= lane
    is_left = lanes < HALF
    first_low = jnp.logical_and(is_low, tile == 0)
    first_high = jnp.logical_and(jnp.logical_not(is_low), tile == -1)
    last_low = jnp.logical_and(is_low, tile == tiles - 1)
    last_high = jnp.logical_and(jnp.logical_not(is_low), tile == tiles - 2)
    in_first = jnp.logical_or(first_low, first_high)
    in_last = jnp.logical_or(last_low, last_high)
    for s in range(facets):
        source = odd if s % 2 else even
        edges = odd_edge if s % 2 else even_edge
        rows = pl.ds(pl.multiple_of((facet ^ s) * block, block), block)
        zero = jnp.zeros((block, LANES), jnp.float32)
        real = source[s // 2, c, 0].astype(jnp.float32)
        imag = source[s // 2, c, 1].astype(jnp.float32)
        whole = (real * cosine - imag * sine, imag * cosine + real * sine)
        prev = edges[s // 2, 0, c].astype(jnp.float32)
        nxt = edges[s // 2, 1, c].astype(jnp.float32)
        real = jnp.where(is_left, prev, pltpu.roll(nxt, HALF, 1))
        imag = jnp.where(is_left, pltpu.roll(prev, HALF, 1), nxt)
        ends = (
            real * edge_cosine - imag * edge_sine,
            imag * edge_cosine + real * edge_sine,
        )
        for part in range(2):
            value = whole[part]
            end = ends[part]
            out[0, 0, part, rows, low_at] = jnp.where(is_low, value, zero).astype(jnp.bfloat16)
            out[0, 0, part, rows, high_at] = jnp.where(is_low, zero, value).astype(jnp.bfloat16)
            out[0, 0, part, rows, :LANES] = (
                jnp.where(is_left, end, zero) + jnp.where(in_first, value, zero)
            ).astype(jnp.bfloat16)
            out[0, 0, part, rows, shard - LANES :] = (
                jnp.where(is_left, zero, end) + jnp.where(in_last, value, zero)
            ).astype(jnp.bfloat16)


def swapped(block, bit):
    facets = lax.axis_size("facet")
    return lax.ppermute(block, "facet", [(i, i ^ bit) for i in range(facets)])


def shifted(block, distance):
    count = lax.axis_size("col")
    return lax.ppermute(block, "col", [(i, (i + distance) % count) for i in range(count)])


def added(kept, received):
    return (kept.astype(jnp.float32) + received.astype(jnp.float32)).astype(jnp.bfloat16)


def reduced(blocks, facets):
    bit = 2
    while bit < facets:
        kept, sent = blocks[0::2], blocks[1::2]
        blocks = added(kept, swapped(sent, bit))
        bit *= 2
    return blocks[0]


def gathered(block, facets):
    blocks = block[None]
    bit = facets // 2
    while bit > 1:
        received = swapped(blocks, bit)
        blocks = jnp.stack([blocks, received], axis=1).reshape((-1,) + blocks.shape[1:])
        bit //= 2
    return blocks, swapped(blocks, 1)


def per_device(facet_spectra, facet_offsets, column_index, subgrid_offsets, weights):
    cols = facet_spectra.shape[0]
    shard = facet_spectra.shape[4]
    facets = lax.axis_size("facet")
    length = shard * lax.axis_size("col")
    block = XM // facets
    bf16 = jnp.bfloat16

    pieces = jax.ShapeDtypeStruct((2, facets // 2, cols, 2, block, LANES), bf16)
    send, keep, turn = pl.pallas_call(
        functools.partial(spectrum_kernel, cols, facets, length),
        out_shape=(pieces, pieces, jax.ShapeDtypeStruct((cols * 4, LANES), jnp.float32)),
        in_specs=[SMEM, SMEM, SMEM, ANY],
        out_specs=(VMEM, VMEM, VMEM),
        scratch_shapes=[
            pltpu.VMEM((cols, 4, 2, XM, LANES), bf16),
            pltpu.SemaphoreType.DMA((cols, 4)),
        ],
        name="spectrum",
    )(facet_offsets, column_index, subgrid_offsets, facet_spectra)

    real_tab, imag_tab = make_table(facets)
    table = jnp.concatenate(
        [
            jnp.concatenate([real_tab, imag_tab], axis=1),
            jnp.concatenate([-imag_tab, real_tab], axis=1),
        ],
        axis=0,
    )

    summed = added(keep, swapped(send, 1))
    edges = reduced(summed[1], facets)
    main = reduced(summed[0], facets)
    from_next = shifted(edges[:, 0], -1)
    from_prev = shifted(edges[:, 1], 1)

    edge = jax.ShapeDtypeStruct((cols, block, LANES), bf16)
    grids, back, to_prev, to_next = pl.pallas_call(
        functools.partial(subgrid_kernel, cols, length, shard),
        out_shape=(
            jax.ShapeDtypeStruct((cols, 1, 2, block, XM), bf16),
            jax.ShapeDtypeStruct((cols, 2, block, LANES), bf16),
            edge,
            edge,
        ),
        in_specs=[SMEM, VMEM, VMEM, VMEM, VMEM, VMEM],
        out_specs=(VMEM, VMEM, VMEM, VMEM),
        scratch_shapes=[
            pltpu.VMEM((cols * block, 2 * WM), bf16),
            pltpu.VMEM((cols * block, 2 * XM), bf16),
        ],
        name="subgrid",
    )(subgrid_offsets, main, from_prev, from_next, table, weights)

    came_prev = shifted(to_next, 1)
    came_next = shifted(to_prev, -1)
    even, odd = gathered(back, facets)
    even_edge, odd_edge = gathered(jnp.stack([came_prev, came_next]), facets)

    def whole(array):
        rank = array.ndim
        return pl.BlockSpec(array.shape, lambda i: (0,) * rank)

    updates = pl.pallas_call(
        functools.partial(update_kernel, cols, facets, length),
        grid=(cols,),
        out_shape=jax.ShapeDtypeStruct((cols, 1, 2, XM, shard), bf16),
        in_specs=[SMEM, whole(turn), whole(even), whole(odd), whole(even_edge), whole(odd_edge)],
        out_specs=pl.BlockSpec((1, 1, 2, XM, shard), lambda i: (i, 0, 0, 0, 0)),
        name="update",
    )(subgrid_offsets, turn, even, odd, even_edge, odd_edge)
    return grids, updates


def solution(mesh):
    in_specs = (
        P(None, "facet", None, None, "col"),
        P("facet", None),
        P(),
        P(None, "col"),
        P(None, "col", "facet", None),
    )
    out_specs = (P(None, "col", None, "facet", None), P(None, "facet", None, None, "col"))
    return jax.shard_map(
        per_device, mesh=mesh, in_specs=in_specs, out_specs=out_specs, check_vma=False
    )
```

```python
import functools
import math

import jax
import jax.numpy as jnp
from jax import lax
from jax.experimental import pallas as pl
from jax.experimental.pallas import tpu as pltpu
from jax.sharding import PartitionSpec as P


IMAGE = 65536
XM = 512
WM = 128
XA = 448
LANES = 128
HALF = WM // 2

TAU = 2.0 * math.pi
BF16 = jnp.bfloat16
F32 = jnp.float32

VMEM = pl.BlockSpec(memory_space=pltpu.VMEM)
SMEM = pl.BlockSpec(memory_space=pltpu.SMEM)
HBM = pl.BlockSpec(memory_space=pltpu.HBM)


def make_table(facets, zero):
    place = jnp.arange(WM, dtype=jnp.int32) + zero
    cell = jnp.arange(XM, dtype=jnp.int32)
    turns = (place[:, None] - WM // 2) * (cell[None, :] - XM // 2) % XM
    angle = TAU * turns.astype(F32) / XM
    relative = (place.astype(F32) + 0.5 - WM / 2.0) / (WM / 2.0)
    taper = (0.3 + 0.7 * (1.0 - relative * relative)) / jnp.sqrt(F32(WM * facets))
    return (
        (taper[:, None] * jnp.cos(angle)).astype(BF16),
        (taper[:, None] * jnp.sin(angle)).astype(BF16),
    )


def remainder(value, modulus):
    if modulus & (modulus - 1) == 0:
        return value & (modulus - 1)
    return lax.rem(value, jnp.int32(modulus))


def modular(first, second, image):
    upper = second // 256
    lower = remainder(second, 256)
    return remainder(remainder(first * upper, image // 256) * 256 + first * lower, image)


def place_of(subgrid_offset, here, shard, length):
    start = subgrid_offset // (IMAGE // length) - here * shard - HALF + LANES
    return lax.div(start, jnp.int32(LANES)) - 1, remainder(start, LANES)


def lanes_of(shape):
    return lax.broadcasted_iota(jnp.int32, shape, len(shape) - 1)


def turns_of(turn, index, firsts, second, length):
    rows = lax.broadcasted_iota(jnp.int32, (8, LANES), 0)
    first = jnp.zeros((8, LANES), F32)
    for c, value in enumerate(firsts):
        first = jnp.where(rows == c, value.astype(F32), first)
    steps = remainder(index * second, length).astype(F32)
    angle = TAU * (first / IMAGE + steps / length)
    turn[0:8, :] = jnp.cos(angle)
    turn[8:16, :] = jnp.sin(angle)


def firsts_of(cols, offsets, column):
    return [modular(column[c] * XA, offsets[0, 0], IMAGE) for c in range(cols)]


def edge_kernel(cols, facets, length, offsets, column, spectra, send, keep, turn, buf, sems):
    shard = spectra.shape[4]
    block = XM // facets
    here = lax.axis_index("col")
    facet = lax.axis_index("facet")
    copies = []
    for c in range(cols):
        for slot, at in enumerate((0, shard - LANES)):
            copy = pltpu.make_async_copy(
                spectra.at[c, 0, :, :, pl.ds(at, LANES)], buf.at[c, slot], sems.at[c, slot]
            )
            copy.start()
            copies.append(copy)
    lanes = lanes_of((8, LANES))
    index = here * shard + lanes + jnp.where(lanes < HALF, 0, shard - LANES)
    turns_of(turn, index, firsts_of(cols, offsets, column), offsets[0, 1], length)
    left = lanes_of((1, LANES)) < HALF
    for c in range(cols):
        copies[c * 2].wait()
        copies[c * 2 + 1].wait()
        cosine = turn[c : c + 1, :]
        sine = turn[8 + c : 9 + c, :]
        for s in range(facets):
            rows = pl.ds(pl.multiple_of((facet ^ s) * block, block), block)
            target = send if s % 2 else keep
            parts = [
                jnp.where(
                    left,
                    buf[c, 0, part, rows, :].astype(F32),
                    buf[c, 1, part, rows, :].astype(F32),
                )
                for part in range(2)
            ]
            real = parts[0] * cosine + parts[1] * sine
            imag = parts[1] * cosine - parts[0] * sine
            low = jnp.where(left, real, pltpu.roll(imag, HALF, 1))
            high = jnp.where(left, pltpu.roll(real, HALF, 1), imag)
            target[0, s // 2, c] = low.astype(BF16)
            target[1, s // 2, c] = high.astype(BF16)


def main_kernel(
    cols, facets, length, offsets, column, subgrid, spectra, after, send, keep, turn, buf, sems
):
    del after
    shard = spectra.shape[4]
    tiles = shard // LANES
    block = XM // facets
    here = lax.axis_index("col")
    facet = lax.axis_index("facet")
    copies = []
    places = []
    for c in range(cols):
        tile, lane = place_of(subgrid[0, c], here, shard, length)
        places.append((tile, lane))
        low = jnp.maximum(tile, 0)
        high = jnp.minimum(tile + 1, tiles - 1)
        for slot, which in enumerate((low, high)):
            at = pl.multiple_of(which * LANES, LANES)
            copy = pltpu.make_async_copy(
                spectra.at[c, 0, :, :, pl.ds(at, LANES)], buf.at[c, slot], sems.at[c, slot]
            )
            copy.start()
            copies.append(copy)
    lanes = lanes_of((8, LANES))
    rows = lax.broadcasted_iota(jnp.int32, (8, LANES), 0)
    index = jnp.zeros((8, LANES), jnp.int32)
    for c in range(cols):
        tile, lane = places[c]
        at = here * shard + lanes + jnp.where(lanes >= lane, tile, tile + 1) * LANES
        index = jnp.where(rows == c, remainder(at + length, length), index)
    turns_of(turn, index, firsts_of(cols, offsets, column), offsets[0, 1], length)
    lanes = lanes_of((1, LANES))
    for c in range(cols):
        tile, lane = places[c]
        copies[c * 2].wait()
        copies[c * 2 + 1].wait()
        from_low = jnp.logical_and(lanes >= lane, tile >= 0)
        from_high = jnp.logical_and(lanes < lane, tile + 1 < tiles)
        zero = jnp.zeros((1, LANES), F32)
        cosine = turn[c : c + 1, :]
        sine = turn[8 + c : 9 + c, :]
        for s in range(facets):
            rows = pl.ds(pl.multiple_of((facet ^ s) * block, block), block)
            target = send if s % 2 else keep
            parts = [
                jnp.where(
                    from_low,
                    buf[c, 0, part, rows, :].astype(F32),
                    jnp.where(from_high, buf[c, 1, part, rows, :].astype(F32), zero),
                )
                for part in range(2)
            ]
            target[0, s // 2, c] = (parts[0] * cosine + parts[1] * sine).astype(BF16)
            target[1, s // 2, c] = (parts[1] * cosine - parts[0] * sine).astype(BF16)


def subgrid_kernel(
    cols,
    length,
    shard,
    subgrid,
    kept,
    received,
    from_prev,
    from_next,
    table,
    weights,
    grids,
    back,
    to_prev,
    to_next,
    stack,
    scaled,
):
    tiles = shard // LANES
    block = kept.shape[3]
    here = lax.axis_index("col")
    lanes = lanes_of((1, LANES))
    zero = jnp.zeros((1, LANES), F32)
    for c in range(cols):
        tile, lane = place_of(subgrid[0, c], here, shard, length)
        low = jnp.logical_and(lanes >= lane, tile < 0)
        high = jnp.logical_and(lanes < lane, tile + 1 >= tiles)
        prev = from_prev[0, c].astype(F32)
        nxt = from_next[0, c].astype(F32)
        shift = remainder(LANES - lane, LANES)
        real = kept[0, 0, c].astype(F32) + received[0, 0, c].astype(F32)
        real = real + jnp.where(low, pltpu.roll(prev, HALF, 1), jnp.where(high, nxt, zero))
        imag = kept[1, 0, c].astype(F32) + received[1, 0, c].astype(F32)
        imag = imag + jnp.where(low, prev, jnp.where(high, pltpu.roll(nxt, HALF, 1), zero))
        rows = slice(c * block, (c + 1) * block)
        stack[rows, :WM] = pltpu.roll(real, shift, 1).astype(BF16)
        stack[rows, WM:] = pltpu.roll(imag, shift, 1).astype(BF16)
    for part in range(2):
        span = slice(part * XM, (part + 1) * XM)
        product = jnp.dot(stack[...], table[:, span], preferred_element_type=F32)
        rounded = product.astype(BF16)
        for c in range(cols):
            rows = slice(c * block, (c + 1) * block)
            piece = rounded[rows]
            grids[c, 0, part] = piece
            scaled[rows, span] = (piece.astype(F32) * weights[c, 0].astype(F32)).astype(BF16)
    result = lax.dot_general(
        scaled[...],
        table[...],
        (((1,), (1,)), ((), ())),
        preferred_element_type=F32,
    )
    for c in range(cols):
        tile, lane = place_of(subgrid[0, c], here, shard, length)
        rows = slice(c * block, (c + 1) * block)
        low = jnp.logical_and(lanes >= lane, tile < 0)
        high = jnp.logical_and(lanes < lane, tile + 1 >= tiles)
        real = pltpu.roll(result[rows, :WM], lane, 1)
        imag = pltpu.roll(result[rows, WM:], lane, 1)
        back[0, 0, c] = real.astype(BF16)
        back[1, 0, c] = imag.astype(BF16)
        real_low = jnp.where(low, real, zero)
        imag_low = jnp.where(low, imag, zero)
        real_high = jnp.where(high, real, zero)
        imag_high = jnp.where(high, imag, zero)
        to_prev[0, c] = (pltpu.roll(real_low, HALF, 1) + imag_low).astype(BF16)
        to_next[0, c] = (real_high + pltpu.roll(imag_high, HALF, 1)).astype(BF16)


def phased(source, s, c, cosine, sine):
    real = source[0, s // 2, c].astype(F32)
    imag = source[1, s // 2, c].astype(F32)
    return real * cosine - imag * sine, imag * cosine + real * sine


def update_kernel(facets, length, subgrid, turn, even, odd, out):
    shard = out.shape[4]
    tiles = shard // LANES
    block = XM // facets
    here = lax.axis_index("col")
    facet = lax.axis_index("facet")
    lanes = lanes_of((1, LANES))
    zero = jnp.zeros((1, LANES), F32)
    c = pl.program_id(0)
    tile, lane = place_of(subgrid[0, c], here, shard, length)
    out[...] = jnp.zeros(out.shape, BF16)
    low_at = pl.ds(pl.multiple_of(jnp.maximum(tile, 0) * LANES, LANES), LANES)
    high_at = pl.ds(pl.multiple_of(jnp.minimum(tile + 1, tiles - 1) * LANES, LANES), LANES)
    cosine = turn[pl.ds(c, 1), :]
    sine = turn[pl.ds(8 + c, 1), :]
    is_low = lanes >= lane
    for s in range(facets):
        rows = pl.ds(pl.multiple_of((facet ^ s) * block, block), block)
        whole = phased(odd if s % 2 else even, s, c, cosine, sine)
        for part in range(2):
            value = whole[part]
            out[0, 0, part, rows, low_at] = jnp.where(is_low, value, zero).astype(BF16)
            out[0, 0, part, rows, high_at] = jnp.where(is_low, zero, value).astype(BF16)


def end_kernel(
    cols,
    facets,
    length,
    subgrid,
    turn,
    edge_turn,
    even,
    odd,
    even_edge,
    odd_edge,
    whole,
    out,
    buf,
    sems,
):
    shard = out.shape[4]
    tiles = shard // LANES
    block = XM // facets
    here = lax.axis_index("col")
    facet = lax.axis_index("facet")
    lanes = lanes_of((1, LANES))
    left = lanes < HALF
    zero = jnp.zeros((1, LANES), F32)
    copies = []
    for c in range(cols):
        tile, lane = place_of(subgrid[0, c], here, shard, length)
        cosine = turn[c : c + 1, :]
        sine = turn[8 + c : 9 + c, :]
        edge_cosine = edge_turn[c : c + 1, :]
        edge_sine = edge_turn[8 + c : 9 + c, :]
        at = jnp.where(lanes >= lane, tile, tile + 1)
        in_first = at == 0
        in_last = at == tiles - 1
        for s in range(facets):
            rows = pl.ds(pl.multiple_of((facet ^ s) * block, block), block)
            values = phased(odd if s % 2 else even, s, c, cosine, sine)
            edges = odd_edge if s % 2 else even_edge
            prev = edges[0, s // 2, c].astype(F32)
            nxt = edges[1, s // 2, c].astype(F32)
            real = jnp.where(left, prev, pltpu.roll(nxt, HALF, 1))
            imag = jnp.where(left, pltpu.roll(prev, HALF, 1), nxt)
            ends = (
                real * edge_cosine - imag * edge_sine,
                imag * edge_cosine + real * edge_sine,
            )
            for part in range(2):
                value = values[part]
                end = ends[part]
                buf[c, 0, part, rows, :] = (
                    jnp.where(left, end, zero) + jnp.where(in_first, value, zero)
                ).astype(BF16)
                buf[c, 1, part, rows, :] = (
                    jnp.where(left, zero, end) + jnp.where(in_last, value, zero)
                ).astype(BF16)
        for slot, start in enumerate((0, shard - LANES)):
            copy = pltpu.make_async_copy(
                buf.at[c, slot], out.at[c, 0, :, :, pl.ds(start, LANES)], sems.at[c, slot]
            )
            copy.start()
            copies.append(copy)
    for copy in copies:
        copy.wait()


def swapped(block, bit):
    facets = lax.axis_size("facet")
    return lax.ppermute(block, "facet", [(i, i ^ bit) for i in range(facets)])


def shifted(block, distance):
    count = lax.axis_size("col")
    return lax.ppermute(block, "col", [(i, (i + distance) % count) for i in range(count)])


def added(kept, received):
    return (kept.astype(F32) + received.astype(F32)).astype(BF16)


def reduced(kept, sent, facets):
    received = swapped(sent, 1)
    bit = 2
    while bit < facets:
        blocks = added(kept, received)
        kept, sent = blocks[:, 0::2], blocks[:, 1::2]
        received = swapped(sent, bit)
        bit *= 2
    return kept, received


def gathered(blocks, facets):
    bit = facets // 2
    while bit > 1:
        received = swapped(blocks, bit)
        shape = (blocks.shape[0], -1) + blocks.shape[2:]
        blocks = jnp.stack([blocks, received], axis=2).reshape(shape)
        bit //= 2
    return blocks, swapped(blocks, 1)


def params(mib):
    return pltpu.CompilerParams(vmem_limit_bytes=mib * 1024 * 1024)


def computed(facet_spectra, facet_offsets, column_index, subgrid_offsets, weights):
    cols = facet_spectra.shape[0]
    shard = facet_spectra.shape[4]
    facets = lax.axis_size("facet")
    length = shard * lax.axis_size("col")
    block = XM // facets
    facet_spectra, facet_offsets, column_index, places = (
        pltpu.with_memory_space_constraint(array, pltpu.HBM)
        for array in (facet_spectra, facet_offsets, column_index, subgrid_offsets.T)
    )

    pieces = jax.ShapeDtypeStruct((2, facets // 2, cols, block, LANES), BF16)
    turns = jax.ShapeDtypeStruct((16, LANES), F32)
    scratch = [pltpu.VMEM((cols, 2, 2, XM, LANES), BF16), pltpu.SemaphoreType.DMA((cols, 2))]
    edge_send, edge_keep, edge_turn = pl.pallas_call(
        functools.partial(edge_kernel, cols, facets, length),
        out_shape=(pieces, pieces, turns),
        in_specs=[SMEM, SMEM, HBM],
        out_specs=(VMEM, VMEM, VMEM),
        scratch_shapes=scratch,
        compiler_params=params(12),
        name="edge",
    )(facet_offsets, column_index, facet_spectra)
    main_send, main_keep, turn = pl.pallas_call(
        functools.partial(main_kernel, cols, facets, length),
        out_shape=(pieces, pieces, turns),
        in_specs=[SMEM, SMEM, SMEM, HBM, VMEM],
        out_specs=(VMEM, VMEM, VMEM),
        scratch_shapes=scratch,
        compiler_params=params(12),
        name="main",
    )(facet_offsets, column_index, places, facet_spectra, edge_turn)

    edges = added(*reduced(edge_keep, edge_send, facets))
    main_kept, main_received = reduced(main_keep, main_send, facets)
    from_prev = shifted(edges[1], 1)
    from_next = shifted(edges[0], -1)

    real_tab, imag_tab = make_table(facets, 0)
    table = jnp.concatenate(
        [
            jnp.concatenate([real_tab, imag_tab], axis=1),
            jnp.concatenate([-imag_tab, real_tab], axis=1),
        ],
        axis=0,
    )

    edge = jax.ShapeDtypeStruct((1, cols, block, LANES), BF16)
    grids, back, to_prev, to_next = pl.pallas_call(
        functools.partial(subgrid_kernel, cols, length, shard),
        out_shape=(
            jax.ShapeDtypeStruct((cols, 1, 2, block, XM), BF16),
            jax.ShapeDtypeStruct((2, 1, cols, block, LANES), BF16),
            edge,
            edge,
        ),
        in_specs=[SMEM] + [VMEM] * 6,
        out_specs=(VMEM, VMEM, VMEM, VMEM),
        scratch_shapes=[
            pltpu.VMEM((cols * block, 2 * WM), BF16),
            pltpu.VMEM((cols * block, 2 * XM), BF16),
        ],
        compiler_params=params(12),
        name="subgrid",
    )(places, main_kept, main_received, from_prev, from_next, table, weights)

    came_prev = shifted(to_next, 1)
    came_next = shifted(to_prev, -1)
    even, odd = gathered(back, facets)
    even_edge, odd_edge = gathered(jnp.stack([came_prev, came_next]), facets)

    def all_of(array):
        rank = array.ndim
        return pl.BlockSpec(array.shape, lambda i: (0,) * rank)

    updates = pl.pallas_call(
        functools.partial(update_kernel, facets, length),
        grid=(cols,),
        out_shape=jax.ShapeDtypeStruct((cols, 1, 2, XM, shard), BF16),
        in_specs=[SMEM, all_of(turn), all_of(even), all_of(odd)],
        out_specs=pl.BlockSpec((1, 1, 2, XM, shard), lambda i: (i, 0, 0, 0, 0)),
        compiler_params=params(16),
        name="update",
    )(places, turn, even, odd)
    updates = pl.pallas_call(
        functools.partial(end_kernel, cols, facets, length),
        out_shape=jax.ShapeDtypeStruct((cols, 1, 2, XM, shard), BF16),
        in_specs=[SMEM] + [VMEM] * 6 + [HBM],
        out_specs=HBM,
        scratch_shapes=scratch,
        input_output_aliases={7: 0},
        compiler_params=params(12),
        name="end",
    )(places, turn, edge_turn, even, odd, even_edge, odd_edge, updates)
    return grids, updates


def solution(mesh):
    in_specs = (
        P(None, "facet", None, None, "col"),
        P("facet", None),
        P(),
        P(None, "col"),
        P(None, "col", "facet", None),
    )
    out_specs = (P(None, "col", None, "facet", None), P(None, "facet", None, None, "col"))
    return jax.shard_map(
        computed, mesh=mesh, in_specs=in_specs, out_specs=out_specs, check_vma=False
    )
```

```python
import functools
import math

import jax
import jax.numpy as jnp
from jax import lax
from jax.experimental import pallas as pl
from jax.experimental.pallas import tpu as pltpu
from jax.sharding import PartitionSpec as P


IMAGE = 65536
XM = 512
WM = 128
XA = 448
LANES = 128
HALF = WM // 2

TAU = 2.0 * math.pi
BF16 = jnp.bfloat16
F32 = jnp.float32

VMEM = pl.BlockSpec(memory_space=pltpu.VMEM)
SMEM = pl.BlockSpec(memory_space=pltpu.SMEM)
HBM = pl.BlockSpec(memory_space=pltpu.HBM)


def remainder(value, modulus):
    if modulus & (modulus - 1) == 0:
        return value & (modulus - 1)
    return lax.rem(value, jnp.int32(modulus))


def modular(first, second, image):
    upper = second // 256
    lower = remainder(second, 256)
    return remainder(remainder(first * upper, image // 256) * 256 + first * lower, image)


def place_of(subgrid_offset, here, shard, length):
    start = subgrid_offset // (IMAGE // length) - here * shard - HALF + LANES
    return lax.div(start, jnp.int32(LANES)) - 1, remainder(start, LANES)


def lanes_of(shape):
    return lax.broadcasted_iota(jnp.int32, shape, len(shape) - 1)


def turns_of(turn, index, firsts, second, length):
    rows = lax.broadcasted_iota(jnp.int32, (8, LANES), 0)
    first = jnp.zeros((8, LANES), F32)
    for c, value in enumerate(firsts):
        first = jnp.where(rows == c, value.astype(F32), first)
    steps = remainder(index * second, length).astype(F32)
    angle = TAU * (first / IMAGE + steps / length)
    turn[0:8, :] = jnp.cos(angle)
    turn[8:16, :] = jnp.sin(angle)


def firsts_of(cols, offsets, column):
    return [modular(column[c] * XA, offsets[0, 0], IMAGE) for c in range(cols)]


def rows_of(facet, s, block):
    return pl.ds(pl.multiple_of((facet ^ s) * block, block), block)


def fetched(spectra, buf, sems, c, s, rows, places):
    copies = []
    for slot, at in enumerate(places):
        copy = pltpu.make_async_copy(
            spectra.at[c, 0, :, rows, pl.ds(at, LANES)],
            buf.at[c, slot, :, rows, :],
            sems.at[c, slot, s],
        )
        copy.start()
        copies.append(copy)
    return copies


def turned(parts, cosine, sine):
    return parts[0] * cosine + parts[1] * sine, parts[1] * cosine - parts[0] * sine


def edge_kernel(
    cols, facets, length, offsets, column, spectra, send, keep, turn, buf, sems, own, held, small
):
    shard = spectra.shape[4]
    block = XM // facets
    here = lax.axis_index("col")
    facet = lax.axis_index("facet")
    scalars = [
        pltpu.make_async_copy(offsets, own, small.at[0]),
        pltpu.make_async_copy(column, held, small.at[1]),
    ]
    for copy in scalars:
        copy.start()
    copies = {}
    order = [s for s in range(facets) if s % 2] + [s for s in range(facets) if s % 2 == 0]
    for c in range(cols):
        for s in order:
            rows = rows_of(facet, s, block)
            copies[c, s] = fetched(spectra, buf, sems, c, s, rows, (0, shard - LANES))
    for copy in scalars:
        copy.wait()
    lanes = lanes_of((8, LANES))
    index = here * shard + lanes + jnp.where(lanes < HALF, 0, shard - LANES)
    turns_of(turn, index, firsts_of(cols, own, held), own[0, 1], length)
    left = lanes_of((1, LANES)) < HALF
    for c in range(cols):
        cosine = turn[c : c + 1, :]
        sine = turn[8 + c : 9 + c, :]
        for s in order:
            for copy in copies[c, s]:
                copy.wait()
            rows = rows_of(facet, s, block)
            target = send if s % 2 else keep
            parts = [
                jnp.where(
                    left,
                    buf[c, 0, part, rows, :].astype(F32),
                    buf[c, 1, part, rows, :].astype(F32),
                )
                for part in range(2)
            ]
            real, imag = turned(parts, cosine, sine)
            low = jnp.where(left, real, pltpu.roll(imag, HALF, 1))
            high = jnp.where(left, pltpu.roll(real, HALF, 1), imag)
            target[0, s // 2, c] = low.astype(BF16)
            target[1, s // 2, c] = high.astype(BF16)


def main_kernel(
    cols, facets, length, offsets, column, subgrid, spectra, after, send, keep, turn, buf, sems
):
    del after
    shard = spectra.shape[4]
    tiles = shard // LANES
    block = XM // facets
    here = lax.axis_index("col")
    facet = lax.axis_index("facet")
    copies = {}
    places = []
    for c in range(cols):
        tile, lane = place_of(subgrid[0, c], here, shard, length)
        places.append((tile, lane))
        low = pl.multiple_of(jnp.maximum(tile, 0) * LANES, LANES)
        high = pl.multiple_of(jnp.minimum(tile + 1, tiles - 1) * LANES, LANES)
        for s in range(facets):
            rows = rows_of(facet, s, block)
            copies[c, s] = fetched(spectra, buf, sems, c, s, rows, (low, high))
    lanes = lanes_of((8, LANES))
    rows = lax.broadcasted_iota(jnp.int32, (8, LANES), 0)
    held = jnp.zeros((8, LANES), jnp.int32)
    begins = jnp.zeros((8, LANES), jnp.int32)
    for c in range(cols):
        tile, lane = places[c]
        held = jnp.where(rows == c, jnp.where(lanes >= lane, tile, tile + 1), held)
        begins = jnp.where(rows == c, lane, begins)
    index = remainder(here * shard + lanes + held * LANES + length, length)
    turns_of(turn, index, firsts_of(cols, offsets, column), offsets[0, 1], length)
    turn[16:24, :] = held.astype(F32)
    turn[24:32, :] = begins.astype(F32)
    lanes = lanes_of((1, LANES))
    zero = jnp.zeros((1, LANES), F32)
    for c in range(cols):
        tile, lane = places[c]
        from_low = jnp.logical_and(lanes >= lane, tile >= 0)
        from_high = jnp.logical_and(lanes < lane, tile + 1 < tiles)
        cosine = turn[c : c + 1, :]
        sine = turn[8 + c : 9 + c, :]
        for s in range(facets):
            for copy in copies[c, s]:
                copy.wait()
            rows = rows_of(facet, s, block)
            target = send if s % 2 else keep
            parts = [
                jnp.where(
                    from_low,
                    buf[c, 0, part, rows, :].astype(F32),
                    jnp.where(from_high, buf[c, 1, part, rows, :].astype(F32), zero),
                )
                for part in range(2)
            ]
            real, imag = turned(parts, cosine, sine)
            target[0, s // 2, c] = real.astype(BF16)
            target[1, s // 2, c] = imag.astype(BF16)


def table_kernel(facets, after, table):
    del after
    place = lax.broadcasted_iota(jnp.int32, (WM, LANES), 0)
    cell = lanes_of((WM, LANES))
    angle = TAU * remainder((place - HALF) * cell + HALF * XM, XM).astype(F32) / XM
    relative = (place.astype(F32) + 0.5 - WM / 2.0) / (WM / 2.0)
    taper = (0.3 + 0.7 * (1.0 - relative * relative)) / jnp.sqrt(
        jnp.full((1, LANES), WM * facets, F32)
    )
    cosine = taper * jnp.cos(angle)
    sine = taper * jnp.sin(angle)
    for tile in range(XM // LANES):
        first = tile * LANES - XM // 2
        quarter = remainder((place - HALF) * (first * 4 // XM) + HALF * 4, 4)
        odd = remainder(quarter, 2) == 1
        real = jnp.where(odd, sine, cosine)
        imag = jnp.where(odd, cosine, sine)
        real = jnp.where(jnp.logical_or(quarter == 1, quarter == 2), -real, real).astype(BF16)
        imag = jnp.where(quarter >= 2, -imag, imag)
        span = slice(tile * LANES, (tile + 1) * LANES)
        other = slice(XM + tile * LANES, XM + (tile + 1) * LANES)
        table[:WM, span] = real
        table[WM:, other] = real
        table[:WM, other] = imag.astype(BF16)
        table[WM:, span] = (-imag).astype(BF16)


def zero_kernel(after, out, buf, sems):
    del after
    cols, _, _, height, _ = out.shape
    block = buf.shape[0]
    buf[...] = jnp.zeros(buf.shape, BF16)
    copies = []
    for c in range(cols):
        for part in range(2):
            for i in range(height // block):
                rows = pl.ds(i * block, block)
                copies.append(
                    pltpu.make_async_copy(buf, out.at[c, 0, part, rows, :], sems.at[c, part, i])
                )
    for copy in copies:
        copy.start()
    for copy in copies:
        copy.wait()


def subgrid_kernel(
    cols,
    shard,
    turn,
    kept,
    received,
    from_prev,
    from_next,
    table,
    weights,
    grids,
    back,
    to_prev,
    to_next,
    stack,
    scaled,
    stage,
    sems,
):
    tiles = shard // LANES
    block = kept.shape[3]
    zero = jnp.zeros((1, LANES), F32)
    begins = [jnp.max(turn[24 + c : 25 + c, :].astype(jnp.int32)) for c in range(cols)]
    for c in range(cols):
        held = turn[16 + c : 17 + c, :]
        low = held < 0
        high = held > tiles - 1
        prev = from_prev[0, c].astype(F32)
        nxt = from_next[0, c].astype(F32)
        shift = remainder(LANES - begins[c], LANES)
        real = kept[0, 0, c].astype(F32) + received[0, 0, c].astype(F32)
        real = real + jnp.where(low, pltpu.roll(prev, HALF, 1), jnp.where(high, nxt, zero))
        imag = kept[1, 0, c].astype(F32) + received[1, 0, c].astype(F32)
        imag = imag + jnp.where(low, prev, jnp.where(high, pltpu.roll(nxt, HALF, 1), zero))
        rows = slice(c * block, (c + 1) * block)
        stack[rows, :WM] = pltpu.roll(real, shift, 1).astype(BF16)
        stack[rows, WM:] = pltpu.roll(imag, shift, 1).astype(BF16)
    copies = []
    for part in range(2):
        span = slice(part * XM, (part + 1) * XM)
        product = jnp.dot(stack[...], table[:, span], preferred_element_type=F32)
        rounded = product.astype(BF16)
        for c in range(cols):
            rows = slice(c * block, (c + 1) * block)
            piece = rounded[rows]
            stage[c, part] = piece
            scaled[rows, span] = (piece.astype(F32) * weights[c, 0].astype(F32)).astype(BF16)
        copy = pltpu.make_async_copy(stage.at[:, part], grids.at[:, 0, part], sems.at[part])
        copy.start()
        copies.append(copy)
    result = lax.dot_general(
        scaled[...],
        table[...],
        (((1,), (1,)), ((), ())),
        preferred_element_type=F32,
    )
    for c in range(cols):
        held = turn[16 + c : 17 + c, :]
        rows = slice(c * block, (c + 1) * block)
        low = held < 0
        high = held > tiles - 1
        real = pltpu.roll(result[rows, :WM], begins[c], 1)
        imag = pltpu.roll(result[rows, WM:], begins[c], 1)
        back[0, 0, c] = real.astype(BF16)
        back[1, 0, c] = imag.astype(BF16)
        real_low = jnp.where(low, real, zero)
        imag_low = jnp.where(low, imag, zero)
        real_high = jnp.where(high, real, zero)
        imag_high = jnp.where(high, imag, zero)
        to_prev[0, c] = (pltpu.roll(real_low, HALF, 1) + imag_low).astype(BF16)
        to_next[0, c] = (real_high + pltpu.roll(imag_high, HALF, 1)).astype(BF16)
    for copy in copies:
        copy.wait()


def phased(source, s, c, cosine, sine):
    real = source[0, s // 2, c].astype(F32)
    imag = source[1, s // 2, c].astype(F32)
    return real * cosine - imag * sine, imag * cosine + real * sine


def window_kernel(cols, facets, length, subgrid, turn, even, odd, whole, out, buf, sems):
    shard = out.shape[4]
    tiles = shard // LANES
    block = XM // facets
    here = lax.axis_index("col")
    facet = lax.axis_index("facet")
    lanes = lanes_of((1, LANES))
    zero = jnp.zeros((1, LANES), F32)
    copies = []
    for c in range(cols):
        tile, lane = place_of(subgrid[0, c], here, shard, length)
        cosine = turn[c : c + 1, :]
        sine = turn[8 + c : 9 + c, :]
        is_low = lanes >= lane
        for s in range(facets):
            rows = rows_of(facet, s, block)
            values = phased(odd if s % 2 else even, s, c, cosine, sine)
            for part in range(2):
                buf[c, 0, part, rows, :] = jnp.where(is_low, values[part], zero).astype(BF16)
                buf[c, 1, part, rows, :] = jnp.where(is_low, zero, values[part]).astype(BF16)
        for slot in range(2):
            which = tile + slot
            at = pl.multiple_of(jnp.clip(which, 0, tiles - 1) * LANES, LANES)
            copy = pltpu.make_async_copy(
                buf.at[c, slot], out.at[c, 0, :, :, pl.ds(at, LANES)], sems.at[c, slot]
            )
            inside = jnp.logical_and(which > 0, which < tiles - 1)
            pl.when(inside)(copy.start)
            copies.append((inside, copy))
    for inside, copy in copies:
        pl.when(inside)(copy.wait)


def end_kernel(
    cols, facets, turn, edge_turn, even, odd, even_edge, odd_edge, whole, out, buf, sems
):
    shard = out.shape[4]
    tiles = shard // LANES
    block = XM // facets
    facet = lax.axis_index("facet")
    left = lanes_of((1, LANES)) < HALF
    zero = jnp.zeros((1, LANES), F32)
    copies = []
    for c in range(cols):
        cosine = turn[c : c + 1, :]
        sine = turn[8 + c : 9 + c, :]
        edge_cosine = edge_turn[c : c + 1, :]
        edge_sine = edge_turn[8 + c : 9 + c, :]
        held = turn[16 + c : 17 + c, :]
        in_first = held == 0
        in_last = held == tiles - 1
        for s in range(facets):
            rows = rows_of(facet, s, block)
            values = phased(odd if s % 2 else even, s, c, cosine, sine)
            edges = odd_edge if s % 2 else even_edge
            prev = edges[0, s // 2, c].astype(F32)
            nxt = edges[1, s // 2, c].astype(F32)
            real = jnp.where(left, prev, pltpu.roll(nxt, HALF, 1))
            imag = jnp.where(left, pltpu.roll(prev, HALF, 1), nxt)
            ends = (
                real * edge_cosine - imag * edge_sine,
                imag * edge_cosine + real * edge_sine,
            )
            for part in range(2):
                value = values[part]
                end = ends[part]
                buf[c, 0, part, rows, :] = (
                    jnp.where(left, end, zero) + jnp.where(in_first, value, zero)
                ).astype(BF16)
                buf[c, 1, part, rows, :] = (
                    jnp.where(left, zero, end) + jnp.where(in_last, value, zero)
                ).astype(BF16)
            for slot, start in enumerate((0, shard - LANES)):
                copy = pltpu.make_async_copy(
                    buf.at[c, slot, :, rows, :],
                    out.at[c, 0, :, rows, pl.ds(start, LANES)],
                    sems.at[c, slot, s],
                )
                copy.start()
                copies.append(copy)
    for copy in copies:
        copy.wait()


def swapped(block, bit):
    facets = lax.axis_size("facet")
    return lax.ppermute(block, "facet", [(i, i ^ bit) for i in range(facets)])


def shifted(block, distance):
    count = lax.axis_size("col")
    return lax.ppermute(block, "col", [(i, (i + distance) % count) for i in range(count)])


def added(kept, received):
    return (kept.astype(F32) + received.astype(F32)).astype(BF16)


def reduced(kept, sent, facets):
    received = swapped(sent, 1)
    bit = 2
    while bit < facets:
        blocks = added(kept, received)
        kept, sent = blocks[:, 0::2], blocks[:, 1::2]
        received = swapped(sent, bit)
        bit *= 2
    return kept, received


def gathered(blocks, facets):
    bit = facets // 2
    while bit > 1:
        received = swapped(blocks, bit)
        shape = (blocks.shape[0], -1) + blocks.shape[2:]
        blocks = jnp.stack([blocks, received], axis=2).reshape(shape)
        bit //= 2
    return blocks, swapped(blocks, 1)


def params(mib):
    return pltpu.CompilerParams(vmem_limit_bytes=mib * 1024 * 1024)


def computed(facet_spectra, facet_offsets, column_index, subgrid_offsets, weights):
    cols = facet_spectra.shape[0]
    shard = facet_spectra.shape[4]
    facets = lax.axis_size("facet")
    length = shard * lax.axis_size("col")
    block = XM // facets
    facet_spectra, facet_offsets, column_index, places = (
        pltpu.with_memory_space_constraint(array, pltpu.HBM)
        for array in (facet_spectra, facet_offsets, column_index, subgrid_offsets.T)
    )

    pieces = jax.ShapeDtypeStruct((2, facets // 2, cols, block, LANES), BF16)
    tile_pair = pltpu.VMEM((cols, 2, 2, XM, LANES), BF16)
    pair_sems = pltpu.SemaphoreType.DMA((cols, 2, facets))
    edge_send, edge_keep, edge_turn = pl.pallas_call(
        functools.partial(edge_kernel, cols, facets, length),
        out_shape=(pieces, pieces, jax.ShapeDtypeStruct((16, LANES), F32)),
        in_specs=[HBM, HBM, HBM],
        out_specs=(VMEM, VMEM, VMEM),
        scratch_shapes=[
            tile_pair,
            pair_sems,
            pltpu.SMEM(facet_offsets.shape, jnp.int32),
            pltpu.SMEM(column_index.shape, jnp.int32),
            pltpu.SemaphoreType.DMA((2,)),
        ],
        compiler_params=params(12),
        name="edge",
    )(facet_offsets, column_index, facet_spectra)
    edges = added(*reduced(edge_keep, edge_send, facets))

    main_send, main_keep, turn = pl.pallas_call(
        functools.partial(main_kernel, cols, facets, length),
        out_shape=(pieces, pieces, jax.ShapeDtypeStruct((32, LANES), F32)),
        in_specs=[SMEM, SMEM, SMEM, HBM, VMEM],
        out_specs=(VMEM, VMEM, VMEM),
        scratch_shapes=[tile_pair, pair_sems],
        compiler_params=params(12),
        name="main",
    )(facet_offsets, column_index, places, facet_spectra, edge_turn)
    main_kept, main_received = reduced(main_keep, main_send, facets)
    from_prev = shifted(edges[1], 1)
    from_next = shifted(edges[0], -1)

    table = pl.pallas_call(
        functools.partial(table_kernel, facets),
        out_shape=jax.ShapeDtypeStruct((2 * WM, 2 * XM), BF16),
        in_specs=[VMEM],
        out_specs=VMEM,
        compiler_params=params(12),
        name="table",
    )(edge_turn)
    shape = jax.ShapeDtypeStruct((cols, 1, 2, XM, shard), BF16)
    updates = pl.pallas_call(
        zero_kernel,
        out_shape=shape,
        in_specs=[VMEM],
        out_specs=HBM,
        scratch_shapes=[
            pltpu.VMEM((LANES, shard), BF16),
            pltpu.SemaphoreType.DMA((cols, 2, XM // LANES)),
        ],
        compiler_params=params(12),
        name="zero",
    )(turn)

    edge = jax.ShapeDtypeStruct((1, cols, block, LANES), BF16)
    grids, back, to_prev, to_next = pl.pallas_call(
        functools.partial(subgrid_kernel, cols, shard),
        out_shape=(
            jax.ShapeDtypeStruct((cols, 1, 2, block, XM), BF16),
            jax.ShapeDtypeStruct((2, 1, cols, block, LANES), BF16),
            edge,
            edge,
        ),
        in_specs=[VMEM] * 7,
        out_specs=(HBM, VMEM, VMEM, VMEM),
        scratch_shapes=[
            pltpu.VMEM((cols * block, 2 * WM), BF16),
            pltpu.VMEM((cols * block, 2 * XM), BF16),
            pltpu.VMEM((cols, 2, block, XM), BF16),
            pltpu.SemaphoreType.DMA((2,)),
        ],
        compiler_params=params(12),
        name="subgrid",
    )(turn, main_kept, main_received, from_prev, from_next, table, weights)

    came_prev = shifted(to_next, 1)
    came_next = shifted(to_prev, -1)
    even, odd = gathered(back, facets)
    even_edge, odd_edge = gathered(jnp.stack([came_prev, came_next]), facets)

    updates = pl.pallas_call(
        functools.partial(window_kernel, cols, facets, length),
        out_shape=shape,
        in_specs=[SMEM, VMEM, VMEM, VMEM, HBM],
        out_specs=HBM,
        scratch_shapes=[tile_pair, pltpu.SemaphoreType.DMA((cols, 2))],
        input_output_aliases={4: 0},
        compiler_params=params(12),
        name="window",
    )(places, turn, even, odd, updates)
    updates = pl.pallas_call(
        functools.partial(end_kernel, cols, facets),
        out_shape=shape,
        in_specs=[VMEM] * 6 + [HBM],
        out_specs=HBM,
        scratch_shapes=[tile_pair, pair_sems],
        input_output_aliases={6: 0},
        compiler_params=params(12),
        name="end",
    )(turn, edge_turn, even, odd, even_edge, odd_edge, updates)
    return grids, updates


def solution(mesh):
    in_specs = (
        P(None, "facet", None, None, "col"),
        P("facet", None),
        P(),
        P(None, "col"),
        P(None, "col", "facet", None),
    )
    out_specs = (P(None, "col", None, "facet", None), P(None, "facet", None, None, "col"))
    return jax.shard_map(
        computed, mesh=mesh, in_specs=in_specs, out_specs=out_specs, check_vma=False
    )
```

```python
import functools
import math

import jax
import jax.numpy as jnp
from jax import lax
from jax.experimental import pallas as pl
from jax.experimental.pallas import tpu as pltpu
from jax.sharding import PartitionSpec as P


IMAGE = 65536
XM = 512
WM = 128
XA = 448
LANES = 128
HALF = WM // 2

TAU = 2.0 * math.pi
BF16 = jnp.bfloat16
F32 = jnp.float32

VMEM = pl.BlockSpec(memory_space=pltpu.VMEM)
SMEM = pl.BlockSpec(memory_space=pltpu.SMEM)
HBM = pl.BlockSpec(memory_space=pltpu.HBM)


def remainder(value, modulus):
    if modulus & (modulus - 1) == 0:
        return value & (modulus - 1)
    return lax.rem(value, jnp.int32(modulus))


def modular(first, second, image):
    upper = second // 256
    lower = remainder(second, 256)
    return remainder(remainder(first * upper, image // 256) * 256 + first * lower, image)


def place_of(subgrid_offset, here, shard, length):
    start = subgrid_offset // (IMAGE // length) - here * shard - HALF + LANES
    return lax.div(start, jnp.int32(LANES)) - 1, remainder(start, LANES)


def lanes_of(shape):
    return lax.broadcasted_iota(jnp.int32, shape, len(shape) - 1)


def turns_of(turn, index, firsts, second, length):
    rows = lax.broadcasted_iota(jnp.int32, (8, LANES), 0)
    first = jnp.zeros((8, LANES), F32)
    for c, value in enumerate(firsts):
        first = jnp.where(rows == c, value.astype(F32), first)
    steps = remainder(index * second, length).astype(F32)
    angle = TAU * (first / IMAGE + steps / length)
    turn[0:8, :] = jnp.cos(angle)
    turn[8:16, :] = jnp.sin(angle)


def firsts_of(cols, offsets, column):
    return [modular(column[c] * XA, offsets[0, 0], IMAGE) for c in range(cols)]


def rows_of(facet, s, block):
    return pl.ds(pl.multiple_of((facet ^ s) * block, block), block)


def fetched(spectra, buf, sems, c, s, rows, places):
    copies = []
    for slot, at in enumerate(places):
        copy = pltpu.make_async_copy(
            spectra.at[c, 0, :, rows, pl.ds(at, LANES)],
            buf.at[c, slot, :, rows, :],
            sems.at[c, slot, s],
        )
        copy.start()
        copies.append(copy)
    return copies


def turned(parts, cosine, sine):
    return parts[0] * cosine + parts[1] * sine, parts[1] * cosine - parts[0] * sine


def places_of(turn, cols):
    tiles = [jnp.min(turn[16 + c : 17 + c, :]).astype(jnp.int32) for c in range(cols)]
    lanes = [jnp.max(turn[24 + c : 25 + c, :]).astype(jnp.int32) for c in range(cols)]
    return tiles, lanes


def edges_of(target, buf, copies, turn, order, cols, block, facet):
    left = lanes_of((1, LANES)) < HALF
    for c in range(cols):
        cosine = turn[c : c + 1, :]
        sine = turn[8 + c : 9 + c, :]
        for s in order:
            for copy in copies[c, s]:
                copy.wait()
            rows = rows_of(facet, s, block)
            parts = [
                jnp.where(
                    left,
                    buf[c, 0, part, rows, :].astype(F32),
                    buf[c, 1, part, rows, :].astype(F32),
                )
                for part in range(2)
            ]
            real, imag = turned(parts, cosine, sine)
            low = jnp.where(left, real, pltpu.roll(imag, HALF, 1))
            high = jnp.where(left, pltpu.roll(real, HALF, 1), imag)
            target[0, s // 2, c] = low.astype(BF16)
            target[1, s // 2, c] = high.astype(BF16)


def edge_kernel(
    cols, facets, length, offsets, column, spectra, send, turn, buf, sems, own, held, small
):
    shard = spectra.shape[4]
    block = XM // facets
    here = lax.axis_index("col")
    facet = lax.axis_index("facet")
    scalars = [
        pltpu.make_async_copy(offsets, own, small.at[0]),
        pltpu.make_async_copy(column, held, small.at[1]),
    ]
    for copy in scalars:
        copy.start()
    copies = {}
    order = range(1, facets, 2)
    for c in range(cols):
        for s in order:
            rows = rows_of(facet, s, block)
            copies[c, s] = fetched(spectra, buf, sems, c, s, rows, (0, shard - LANES))
    for copy in scalars:
        copy.wait()
    lanes = lanes_of((8, LANES))
    index = here * shard + lanes + jnp.where(lanes < HALF, 0, shard - LANES)
    turns_of(turn, index, firsts_of(cols, own, held), own[0, 1], length)
    edges_of(send, buf, copies, turn, order, cols, block, facet)


def hold_kernel(
    cols,
    facets,
    length,
    offsets,
    column,
    subgrid,
    spectra,
    edge_turn,
    keep,
    turn,
    buf,
    sems,
    own,
    held,
    spots,
    small,
):
    shard = spectra.shape[4]
    block = XM // facets
    here = lax.axis_index("col")
    facet = lax.axis_index("facet")
    scalars = [
        pltpu.make_async_copy(offsets, own, small.at[0]),
        pltpu.make_async_copy(column, held, small.at[1]),
        pltpu.make_async_copy(subgrid, spots, small.at[2]),
    ]
    for copy in scalars:
        copy.start()
    copies = {}
    order = range(0, facets, 2)
    for c in range(cols):
        for s in order:
            rows = rows_of(facet, s, block)
            copies[c, s] = fetched(spectra, buf, sems, c, s, rows, (0, shard - LANES))
    for copy in scalars:
        copy.wait()
    lanes = lanes_of((8, LANES))
    rows = lax.broadcasted_iota(jnp.int32, (8, LANES), 0)
    tile_at = jnp.zeros((8, LANES), jnp.int32)
    begins = jnp.zeros((8, LANES), jnp.int32)
    for c in range(cols):
        tile, lane = place_of(spots[0, c], here, shard, length)
        tile_at = jnp.where(rows == c, jnp.where(lanes >= lane, tile, tile + 1), tile_at)
        begins = jnp.where(rows == c, lane, begins)
    index = remainder(here * shard + lanes + tile_at * LANES + length, length)
    turns_of(turn, index, firsts_of(cols, own, held), own[0, 1], length)
    turn[16:24, :] = tile_at.astype(F32)
    turn[24:32, :] = begins.astype(F32)
    edges_of(keep, buf, copies, edge_turn, order, cols, block, facet)


def main_kernel(cols, facets, spectra, turn, after, send, keep, buf, sems):
    del after
    shard = spectra.shape[4]
    tiles = shard // LANES
    block = XM // facets
    facet = lax.axis_index("facet")
    copies = {}
    first_tiles, _ = places_of(turn, cols)
    for c in range(cols):
        tile = first_tiles[c]
        low = pl.multiple_of(jnp.maximum(tile, 0) * LANES, LANES)
        high = pl.multiple_of(jnp.minimum(tile + 1, tiles - 1) * LANES, LANES)
        for s in range(facets):
            rows = rows_of(facet, s, block)
            copies[c, s] = fetched(spectra, buf, sems, c, s, rows, (low, high))
    zero = jnp.zeros((1, LANES), F32)
    for c in range(cols):
        tile_at = turn[16 + c : 17 + c, :]
        is_low = lanes_of((1, LANES)).astype(F32) >= turn[24 + c : 25 + c, :]
        inside = jnp.logical_and(tile_at >= 0, tile_at <= tiles - 1)
        cosine = jnp.where(inside, turn[c : c + 1, :], zero)
        sine = jnp.where(inside, turn[8 + c : 9 + c, :], zero)
        for s in range(facets):
            for copy in copies[c, s]:
                copy.wait()
            rows = rows_of(facet, s, block)
            target = send if s % 2 else keep
            parts = [
                jnp.where(
                    is_low,
                    buf[c, 0, part, rows, :].astype(F32),
                    buf[c, 1, part, rows, :].astype(F32),
                )
                for part in range(2)
            ]
            real, imag = turned(parts, cosine, sine)
            target[0, s // 2, c] = real.astype(BF16)
            target[1, s // 2, c] = imag.astype(BF16)


def table_kernel(facets, after, table):
    del after
    place = lax.broadcasted_iota(jnp.int32, (WM, LANES), 0)
    cell = lanes_of((WM, LANES))
    angle = TAU * remainder((place - HALF) * cell + HALF * XM, XM).astype(F32) / XM
    relative = (place.astype(F32) + 0.5 - WM / 2.0) / (WM / 2.0)
    taper = (0.3 + 0.7 * (1.0 - relative * relative)) / jnp.sqrt(
        jnp.full((1, LANES), WM * facets, F32)
    )
    cosine = taper * jnp.cos(angle)
    sine = taper * jnp.sin(angle)
    for tile in range(XM // LANES):
        first = tile * LANES - XM // 2
        quarter = remainder((place - HALF) * (first * 4 // XM) + HALF * 4, 4)
        odd = remainder(quarter, 2) == 1
        real = jnp.where(odd, sine, cosine)
        imag = jnp.where(odd, cosine, sine)
        real = jnp.where(jnp.logical_or(quarter == 1, quarter == 2), -real, real).astype(BF16)
        imag = jnp.where(quarter >= 2, -imag, imag)
        span = slice(tile * LANES, (tile + 1) * LANES)
        other = slice(XM + tile * LANES, XM + (tile + 1) * LANES)
        table[:WM, span] = real
        table[WM:, other] = real
        table[:WM, other] = imag.astype(BF16)
        table[WM:, span] = (-imag).astype(BF16)


def zero_kernel(after, out, buf, sems):
    del after
    cols, _, _, height, _ = out.shape
    block = buf.shape[0]
    buf[...] = jnp.zeros(buf.shape, BF16)
    copies = []
    for c in range(cols):
        for part in range(2):
            for i in range(height // block):
                rows = pl.ds(i * block, block)
                copies.append(
                    pltpu.make_async_copy(buf, out.at[c, 0, part, rows, :], sems.at[c, part, i])
                )
    for copy in copies:
        copy.start()
    for copy in copies:
        copy.wait()


def subgrid_kernel(
    cols,
    shard,
    turn,
    kept,
    received,
    from_prev,
    from_next,
    table,
    weights,
    grids,
    back,
    to_prev,
    to_next,
    stack,
    scaled,
    stage,
    sems,
):
    tiles = shard // LANES
    block = kept.shape[3]
    zero = jnp.zeros((1, LANES), F32)
    _, begins = places_of(turn, cols)
    for c in range(cols):
        held = turn[16 + c : 17 + c, :]
        low = held < 0
        high = held > tiles - 1
        prev = from_prev[0, c].astype(F32)
        nxt = from_next[0, c].astype(F32)
        shift = remainder(LANES - begins[c], LANES)
        real = kept[0, 0, c].astype(F32) + received[0, 0, c].astype(F32)
        real = real + jnp.where(low, pltpu.roll(prev, HALF, 1), jnp.where(high, nxt, zero))
        imag = kept[1, 0, c].astype(F32) + received[1, 0, c].astype(F32)
        imag = imag + jnp.where(low, prev, jnp.where(high, pltpu.roll(nxt, HALF, 1), zero))
        rows = slice(c * block, (c + 1) * block)
        stack[rows, :WM] = pltpu.roll(real, shift, 1).astype(BF16)
        stack[rows, WM:] = pltpu.roll(imag, shift, 1).astype(BF16)
    copies = []
    for part in range(2):
        span = slice(part * XM, (part + 1) * XM)
        product = jnp.dot(stack[...], table[:, span], preferred_element_type=F32)
        rounded = product.astype(BF16)
        for c in range(cols):
            rows = slice(c * block, (c + 1) * block)
            piece = rounded[rows]
            stage[c, part] = piece
            scaled[rows, span] = (piece.astype(F32) * weights[c, 0].astype(F32)).astype(BF16)
        copy = pltpu.make_async_copy(stage.at[:, part], grids.at[:, 0, part], sems.at[part])
        copy.start()
        copies.append(copy)
    result = lax.dot_general(
        scaled[...],
        table[...],
        (((1,), (1,)), ((), ())),
        preferred_element_type=F32,
    )
    for c in range(cols):
        held = turn[16 + c : 17 + c, :]
        rows = slice(c * block, (c + 1) * block)
        low = held < 0
        high = held > tiles - 1
        real = pltpu.roll(result[rows, :WM], begins[c], 1)
        imag = pltpu.roll(result[rows, WM:], begins[c], 1)
        back[0, 0, c] = real.astype(BF16)
        back[1, 0, c] = imag.astype(BF16)
        real_low = jnp.where(low, real, zero)
        imag_low = jnp.where(low, imag, zero)
        real_high = jnp.where(high, real, zero)
        imag_high = jnp.where(high, imag, zero)
        to_prev[0, c] = (pltpu.roll(real_low, HALF, 1) + imag_low).astype(BF16)
        to_next[0, c] = (real_high + pltpu.roll(imag_high, HALF, 1)).astype(BF16)
    for copy in copies:
        copy.wait()


def phased(source, s, c, cosine, sine):
    real = source[0, s // 2, c].astype(F32)
    imag = source[1, s // 2, c].astype(F32)
    return real * cosine - imag * sine, imag * cosine + real * sine


def window_kernel(cols, facets, turn, even, odd, whole, out, buf, sems):
    shard = out.shape[4]
    tiles = shard // LANES
    block = XM // facets
    facet = lax.axis_index("facet")
    zero = jnp.zeros((1, LANES), F32)
    first_tiles, _ = places_of(turn, cols)
    copies = []
    for c in range(cols):
        cosine = turn[c : c + 1, :]
        sine = turn[8 + c : 9 + c, :]
        is_low = lanes_of((1, LANES)).astype(F32) >= turn[24 + c : 25 + c, :]
        for s in range(facets):
            rows = rows_of(facet, s, block)
            values = phased(odd if s % 2 else even, s, c, cosine, sine)
            for part in range(2):
                buf[c, 0, part, rows, :] = jnp.where(is_low, values[part], zero).astype(BF16)
                buf[c, 1, part, rows, :] = jnp.where(is_low, zero, values[part]).astype(BF16)
        for slot in range(2):
            which = first_tiles[c] + slot
            at = pl.multiple_of(jnp.clip(which, 0, tiles - 1) * LANES, LANES)
            copy = pltpu.make_async_copy(
                buf.at[c, slot], out.at[c, 0, :, :, pl.ds(at, LANES)], sems.at[c, slot]
            )
            inside = jnp.logical_and(which > 0, which < tiles - 1)
            pl.when(inside)(copy.start)
            copies.append((inside, copy))
    for inside, copy in copies:
        pl.when(inside)(copy.wait)


def end_kernel(cols, facets, odd, turn, edge_turn, main, edges, whole, out, buf, sems):
    shard = out.shape[4]
    tiles = shard // LANES
    block = XM // facets
    facet = lax.axis_index("facet")
    left = lanes_of((1, LANES)) < HALF
    zero = jnp.zeros((1, LANES), F32)
    copies = []
    for c in range(cols):
        cosine = turn[c : c + 1, :]
        sine = turn[8 + c : 9 + c, :]
        edge_cosine = edge_turn[c : c + 1, :]
        edge_sine = edge_turn[8 + c : 9 + c, :]
        tile_at = turn[16 + c : 17 + c, :]
        in_first = tile_at == 0
        in_last = tile_at == tiles - 1
        for s in range(odd, facets, 2):
            rows = rows_of(facet, s, block)
            values = phased(main, s, c, cosine, sine)
            prev = edges[0, s // 2, c].astype(F32)
            nxt = edges[1, s // 2, c].astype(F32)
            real = jnp.where(left, prev, pltpu.roll(nxt, HALF, 1))
            imag = jnp.where(left, pltpu.roll(prev, HALF, 1), nxt)
            ends = (
                real * edge_cosine - imag * edge_sine,
                imag * edge_cosine + real * edge_sine,
            )
            for part in range(2):
                value = values[part]
                end = ends[part]
                buf[c, 0, part, s // 2] = (
                    jnp.where(left, end, zero) + jnp.where(in_first, value, zero)
                ).astype(BF16)
                buf[c, 1, part, s // 2] = (
                    jnp.where(left, zero, end) + jnp.where(in_last, value, zero)
                ).astype(BF16)
            for slot, start in enumerate((0, shard - LANES)):
                copy = pltpu.make_async_copy(
                    buf.at[c, slot, :, s // 2],
                    out.at[c, 0, :, rows, pl.ds(start, LANES)],
                    sems.at[c, slot, s // 2],
                )
                copy.start()
                copies.append(copy)
    for copy in copies:
        copy.wait()


def swapped(block, bit):
    facets = lax.axis_size("facet")
    return lax.ppermute(block, "facet", [(i, i ^ bit) for i in range(facets)])


def shifted(block, distance):
    count = lax.axis_size("col")
    return lax.ppermute(block, "col", [(i, (i + distance) % count) for i in range(count)])


def added(kept, received):
    return (kept.astype(F32) + received.astype(F32)).astype(BF16)


def reduced(kept, sent, facets):
    received = swapped(sent, 1)
    bit = 2
    while bit < facets:
        blocks = added(kept, received)
        kept, sent = blocks[:, 0::2], blocks[:, 1::2]
        received = swapped(sent, bit)
        bit *= 2
    return kept, received


def gathered(blocks, facets):
    bit = facets // 2
    while bit > 1:
        received = swapped(blocks, bit)
        shape = (blocks.shape[0], -1) + blocks.shape[2:]
        blocks = jnp.stack([blocks, received], axis=2).reshape(shape)
        bit //= 2
    return blocks, swapped(blocks, 1)


def params(mib):
    return pltpu.CompilerParams(vmem_limit_bytes=mib * 1024 * 1024)


def computed(facet_spectra, facet_offsets, column_index, subgrid_offsets, weights):
    cols = facet_spectra.shape[0]
    shard = facet_spectra.shape[4]
    facets = lax.axis_size("facet")
    length = shard * lax.axis_size("col")
    block = XM // facets
    facet_spectra, facet_offsets, column_index, places = (
        pltpu.with_memory_space_constraint(array, pltpu.HBM)
        for array in (facet_spectra, facet_offsets, column_index, subgrid_offsets.T)
    )

    pieces = jax.ShapeDtypeStruct((2, facets // 2, cols, block, LANES), BF16)
    tile_pair = pltpu.VMEM((cols, 2, 2, XM, LANES), BF16)
    pair_sems = pltpu.SemaphoreType.DMA((cols, 2, facets))
    whole_scalars = [
        pltpu.SMEM(facet_offsets.shape, jnp.int32),
        pltpu.SMEM(column_index.shape, jnp.int32),
    ]
    edge_send, edge_turn = pl.pallas_call(
        functools.partial(edge_kernel, cols, facets, length),
        out_shape=(pieces, jax.ShapeDtypeStruct((16, LANES), F32)),
        in_specs=[HBM, HBM, HBM],
        out_specs=(VMEM, VMEM),
        scratch_shapes=[tile_pair, pair_sems, *whole_scalars, pltpu.SemaphoreType.DMA((2,))],
        compiler_params=params(12),
        name="edge",
    )(facet_offsets, column_index, facet_spectra)
    edge_keep, turn = pl.pallas_call(
        functools.partial(hold_kernel, cols, facets, length),
        out_shape=(pieces, jax.ShapeDtypeStruct((32, LANES), F32)),
        in_specs=[HBM, HBM, HBM, HBM, VMEM],
        out_specs=(VMEM, VMEM),
        scratch_shapes=[
            tile_pair,
            pair_sems,
            *whole_scalars,
            pltpu.SMEM(places.shape, jnp.int32),
            pltpu.SemaphoreType.DMA((3,)),
        ],
        compiler_params=params(12),
        name="hold",
    )(facet_offsets, column_index, places, facet_spectra, edge_turn)
    pair = reduced(edge_keep, edge_send, facets)
    edges = added(*pair)

    main_send, main_keep = pl.pallas_call(
        functools.partial(main_kernel, cols, facets),
        out_shape=(pieces, pieces),
        in_specs=[HBM, VMEM, VMEM],
        out_specs=(VMEM, VMEM),
        scratch_shapes=[tile_pair, pair_sems],
        compiler_params=params(12),
        name="main",
    )(facet_spectra, turn, edge_turn)
    main_kept, main_received = reduced(main_keep, main_send, facets)
    from_prev = shifted(edges[1], 1)
    from_next = shifted(edges[0], -1)

    table = pl.pallas_call(
        functools.partial(table_kernel, facets),
        out_shape=jax.ShapeDtypeStruct((2 * WM, 2 * XM), BF16),
        in_specs=[VMEM],
        out_specs=VMEM,
        compiler_params=params(12),
        name="table",
    )(edge_turn)
    shape = jax.ShapeDtypeStruct((cols, 1, 2, XM, shard), BF16)
    updates = pl.pallas_call(
        zero_kernel,
        out_shape=shape,
        in_specs=[VMEM],
        out_specs=HBM,
        scratch_shapes=[
            pltpu.VMEM((LANES, shard), BF16),
            pltpu.SemaphoreType.DMA((cols, 2, XM // LANES)),
        ],
        compiler_params=params(12),
        name="zero",
    )(turn)

    edge = jax.ShapeDtypeStruct((1, cols, block, LANES), BF16)
    grids, back, to_prev, to_next = pl.pallas_call(
        functools.partial(subgrid_kernel, cols, shard),
        out_shape=(
            jax.ShapeDtypeStruct((cols, 1, 2, block, XM), BF16),
            jax.ShapeDtypeStruct((2, 1, cols, block, LANES), BF16),
            edge,
            edge,
        ),
        in_specs=[VMEM] * 7,
        out_specs=(HBM, VMEM, VMEM, VMEM),
        scratch_shapes=[
            pltpu.VMEM((cols * block, 2 * WM), BF16),
            pltpu.VMEM((cols * block, 2 * XM), BF16),
            pltpu.VMEM((cols, 2, block, XM), BF16),
            pltpu.SemaphoreType.DMA((2,)),
        ],
        compiler_params=params(12),
        name="subgrid",
    )(turn, main_kept, main_received, from_prev, from_next, table, weights)

    came_prev = shifted(to_next, 1)
    came_next = shifted(to_prev, -1)
    even, odd = gathered(back, facets)
    even_edge, odd_edge = gathered(jnp.stack([came_prev, came_next]), facets)

    updates = pl.pallas_call(
        functools.partial(window_kernel, cols, facets),
        out_shape=shape,
        in_specs=[VMEM, VMEM, VMEM, HBM],
        out_specs=HBM,
        scratch_shapes=[tile_pair, pltpu.SemaphoreType.DMA((cols, 2))],
        input_output_aliases={3: 0},
        compiler_params=params(12),
        name="window",
    )(turn, even, odd, updates)
    halves = ((0, even, even_edge), (1, odd, odd_edge))
    for half, main, ends in halves:
        updates = pl.pallas_call(
            functools.partial(end_kernel, cols, facets, half),
            out_shape=shape,
            in_specs=[VMEM] * 4 + [HBM],
            out_specs=HBM,
            scratch_shapes=[
                pltpu.VMEM((cols, 2, 2, facets // 2, block, LANES), BF16),
                pltpu.SemaphoreType.DMA((cols, 2, facets // 2)),
            ],
            input_output_aliases={4: 0},
            compiler_params=params(12),
        )(turn, edge_turn, main, ends, updates)
    return grids, updates


def solution(mesh):
    in_specs = (
        P(None, "facet", None, None, "col"),
        P("facet", None),
        P(),
        P(None, "col"),
        P(None, "col", "facet", None),
    )
    out_specs = (P(None, "col", None, "facet", None), P(None, "facet", None, None, "col"))
    return jax.shard_map(
        computed, mesh=mesh, in_specs=in_specs, out_specs=out_specs, check_vma=False
    )
```

```python
import functools
import math

import jax
import jax.numpy as jnp
from jax import lax
from jax.experimental import pallas as pl
from jax.experimental.pallas import tpu as pltpu
from jax.sharding import PartitionSpec as P


IMAGE = 65536
XM = 512
WM = 128
XA = 448
LANES = 128
HALF = WM // 2

TAU = 2.0 * math.pi
BF16 = jnp.bfloat16
F32 = jnp.float32

VMEM = pl.BlockSpec(memory_space=pltpu.VMEM)
SMEM = pl.BlockSpec(memory_space=pltpu.SMEM)
HBM = pl.BlockSpec(memory_space=pltpu.HBM)


def remainder(value, modulus):
    if modulus & (modulus - 1) == 0:
        return value & (modulus - 1)
    return lax.rem(value, jnp.int32(modulus))


def modular(first, second, image):
    upper = second // 256
    lower = remainder(second, 256)
    return remainder(remainder(first * upper, image // 256) * 256 + first * lower, image)


def place_of(subgrid_offset, here, shard, length):
    start = subgrid_offset // (IMAGE // length) - here * shard - HALF + LANES
    return lax.div(start, jnp.int32(LANES)) - 1, remainder(start, LANES)


def lanes_of(shape):
    return lax.broadcasted_iota(jnp.int32, shape, len(shape) - 1)


def turns_of(turn, index, firsts, second, length):
    rows = lax.broadcasted_iota(jnp.int32, (8, LANES), 0)
    first = jnp.zeros((8, LANES), F32)
    for c, value in enumerate(firsts):
        first = jnp.where(rows == c, value.astype(F32), first)
    steps = remainder(index * second, length).astype(F32)
    angle = TAU * (first / IMAGE + steps / length)
    turn[0:8, :] = jnp.cos(angle)
    turn[8:16, :] = jnp.sin(angle)


def firsts_of(cols, offsets, column):
    return [modular(column[c] * XA, offsets[0, 0], IMAGE) for c in range(cols)]


def rows_of(facet, s, block):
    return pl.ds(pl.multiple_of((facet ^ s) * block, block), block)


def fetched(spectra, buf, sems, c, s, rows, places):
    copies = []
    for slot, at in enumerate(places):
        copy = pltpu.make_async_copy(
            spectra.at[c, 0, :, rows, pl.ds(at, LANES)],
            buf.at[c, slot, :, rows, :],
            sems.at[c, slot, s],
        )
        copy.start()
        copies.append(copy)
    return copies


def turned(parts, cosine, sine):
    return parts[0] * cosine + parts[1] * sine, parts[1] * cosine - parts[0] * sine


def places_of(turn, cols):
    tiles = [jnp.min(turn[16 + c : 17 + c, :]).astype(jnp.int32) for c in range(cols)]
    lanes = [jnp.max(turn[24 + c : 25 + c, :]).astype(jnp.int32) for c in range(cols)]
    return tiles, lanes


def edges_of(target, buf, copies, turn, order, cols, block, facet):
    left = lanes_of((1, LANES)) < HALF
    for c in range(cols):
        cosine = turn[c : c + 1, :]
        sine = turn[8 + c : 9 + c, :]
        for s in order:
            for copy in copies[c, s]:
                copy.wait()
            rows = rows_of(facet, s, block)
            parts = [
                jnp.where(
                    left,
                    buf[c, 0, part, rows, :].astype(F32),
                    buf[c, 1, part, rows, :].astype(F32),
                )
                for part in range(2)
            ]
            real, imag = turned(parts, cosine, sine)
            low = jnp.where(left, real, pltpu.roll(imag, HALF, 1))
            high = jnp.where(left, pltpu.roll(real, HALF, 1), imag)
            target[0, s // 2, c] = low.astype(BF16)
            target[1, s // 2, c] = high.astype(BF16)


def edge_kernel(
    cols, facets, length, offsets, column, spectra, send, turn, buf, sems, own, held, small
):
    shard = spectra.shape[4]
    block = XM // facets
    here = lax.axis_index("col")
    facet = lax.axis_index("facet")
    scalars = [
        pltpu.make_async_copy(offsets, own, small.at[0]),
        pltpu.make_async_copy(column, held, small.at[1]),
    ]
    for copy in scalars:
        copy.start()
    copies = {}
    order = range(1, facets, 2)
    for c in range(cols):
        for s in order:
            rows = rows_of(facet, s, block)
            copies[c, s] = fetched(spectra, buf, sems, c, s, rows, (0, shard - LANES))
    for copy in scalars:
        copy.wait()
    lanes = lanes_of((8, LANES))
    index = here * shard + lanes + jnp.where(lanes < HALF, 0, shard - LANES)
    turns_of(turn, index, firsts_of(cols, own, held), own[0, 1], length)
    edges_of(send, buf, copies, turn, order, cols, block, facet)


def hold_kernel(
    cols,
    facets,
    length,
    offsets,
    column,
    subgrid,
    spectra,
    edge_turn,
    keep,
    turn,
    buf,
    sems,
    own,
    held,
    spots,
    small,
):
    shard = spectra.shape[4]
    block = XM // facets
    here = lax.axis_index("col")
    facet = lax.axis_index("facet")
    scalars = [
        pltpu.make_async_copy(offsets, own, small.at[0]),
        pltpu.make_async_copy(column, held, small.at[1]),
        pltpu.make_async_copy(subgrid, spots, small.at[2]),
    ]
    for copy in scalars:
        copy.start()
    copies = {}
    order = range(0, facets, 2)
    for c in range(cols):
        for s in order:
            rows = rows_of(facet, s, block)
            copies[c, s] = fetched(spectra, buf, sems, c, s, rows, (0, shard - LANES))
    for copy in scalars:
        copy.wait()
    lanes = lanes_of((8, LANES))
    rows = lax.broadcasted_iota(jnp.int32, (8, LANES), 0)
    tile_at = jnp.zeros((8, LANES), jnp.int32)
    begins = jnp.zeros((8, LANES), jnp.int32)
    for c in range(cols):
        tile, lane = place_of(spots[0, c], here, shard, length)
        tile_at = jnp.where(rows == c, jnp.where(lanes >= lane, tile, tile + 1), tile_at)
        begins = jnp.where(rows == c, lane, begins)
    index = remainder(here * shard + lanes + tile_at * LANES + length, length)
    turns_of(turn, index, firsts_of(cols, own, held), own[0, 1], length)
    turn[16:24, :] = tile_at.astype(F32)
    turn[24:32, :] = begins.astype(F32)
    edges_of(keep, buf, copies, edge_turn, order, cols, block, facet)


def main_kernel(cols, facets, spectra, turn, after, send, keep, buf, sems):
    del after
    shard = spectra.shape[4]
    tiles = shard // LANES
    block = XM // facets
    facet = lax.axis_index("facet")
    copies = {}
    first_tiles, _ = places_of(turn, cols)
    for c in range(cols):
        tile = first_tiles[c]
        low = pl.multiple_of(jnp.maximum(tile, 0) * LANES, LANES)
        high = pl.multiple_of(jnp.minimum(tile + 1, tiles - 1) * LANES, LANES)
        for s in range(facets):
            rows = rows_of(facet, s, block)
            copies[c, s] = fetched(spectra, buf, sems, c, s, rows, (low, high))
    zero = jnp.zeros((1, LANES), F32)
    for c in range(cols):
        tile_at = turn[16 + c : 17 + c, :]
        is_low = lanes_of((1, LANES)).astype(F32) >= turn[24 + c : 25 + c, :]
        inside = jnp.logical_and(tile_at >= 0, tile_at <= tiles - 1)
        cosine = jnp.where(inside, turn[c : c + 1, :], zero)
        sine = jnp.where(inside, turn[8 + c : 9 + c, :], zero)
        for s in range(facets):
            for copy in copies[c, s]:
                copy.wait()
            rows = rows_of(facet, s, block)
            target = send if s % 2 else keep
            parts = [
                jnp.where(
                    is_low,
                    buf[c, 0, part, rows, :].astype(F32),
                    buf[c, 1, part, rows, :].astype(F32),
                )
                for part in range(2)
            ]
            real, imag = turned(parts, cosine, sine)
            target[0, s // 2, c] = real.astype(BF16)
            target[1, s // 2, c] = imag.astype(BF16)


def table_kernel(facets, after, table):
    del after
    place = lax.broadcasted_iota(jnp.int32, (WM, LANES), 0)
    cell = lanes_of((WM, LANES))
    angle = TAU * remainder((place - HALF) * cell + HALF * XM, XM).astype(F32) / XM
    relative = (place.astype(F32) + 0.5 - WM / 2.0) / (WM / 2.0)
    taper = (0.3 + 0.7 * (1.0 - relative * relative)) / jnp.sqrt(
        jnp.full((1, LANES), WM * facets, F32)
    )
    cosine = taper * jnp.cos(angle)
    sine = taper * jnp.sin(angle)
    for tile in range(XM // LANES):
        first = tile * LANES - XM // 2
        quarter = remainder((place - HALF) * (first * 4 // XM) + HALF * 4, 4)
        odd = remainder(quarter, 2) == 1
        real = jnp.where(odd, sine, cosine)
        imag = jnp.where(odd, cosine, sine)
        real = jnp.where(jnp.logical_or(quarter == 1, quarter == 2), -real, real).astype(BF16)
        imag = jnp.where(quarter >= 2, -imag, imag)
        span = slice(tile * LANES, (tile + 1) * LANES)
        other = slice(XM + tile * LANES, XM + (tile + 1) * LANES)
        table[:WM, span] = real
        table[WM:, other] = real
        table[:WM, other] = imag.astype(BF16)
        table[WM:, span] = (-imag).astype(BF16)


def zero_kernel(after, out, buf, sems):
    del after
    cols, _, _, height, _ = out.shape
    block = buf.shape[0]
    buf[...] = jnp.zeros(buf.shape, BF16)
    copies = []
    for c in range(cols):
        for part in range(2):
            for i in range(height // block):
                rows = pl.ds(i * block, block)
                copies.append(
                    pltpu.make_async_copy(buf, out.at[c, 0, part, rows, :], sems.at[c, part, i])
                )
    for copy in copies:
        copy.start()
    for copy in copies:
        copy.wait()


def subgrid_kernel(
    cols,
    shard,
    turn,
    kept,
    received,
    from_prev,
    from_next,
    table,
    weights,
    grids,
    back,
    to_prev,
    to_next,
    stack,
    scaled,
    stage,
    sems,
):
    tiles = shard // LANES
    block = kept.shape[3]
    zero = jnp.zeros((1, LANES), F32)
    _, begins = places_of(turn, cols)
    for c in range(cols):
        held = turn[16 + c : 17 + c, :]
        low = held < 0
        high = held > tiles - 1
        prev = from_prev[0, c].astype(F32)
        nxt = from_next[0, c].astype(F32)
        shift = remainder(LANES - begins[c], LANES)
        real = kept[0, 0, c].astype(F32) + received[0, 0, c].astype(F32)
        real = real + jnp.where(low, pltpu.roll(prev, HALF, 1), jnp.where(high, nxt, zero))
        imag = kept[1, 0, c].astype(F32) + received[1, 0, c].astype(F32)
        imag = imag + jnp.where(low, prev, jnp.where(high, pltpu.roll(nxt, HALF, 1), zero))
        rows = slice(c * block, (c + 1) * block)
        stack[rows, :WM] = pltpu.roll(real, shift, 1).astype(BF16)
        stack[rows, WM:] = pltpu.roll(imag, shift, 1).astype(BF16)
    copies = []
    for part in range(2):
        span = slice(part * XM, (part + 1) * XM)
        product = jnp.dot(stack[...], table[:, span], preferred_element_type=F32)
        rounded = product.astype(BF16)
        for c in range(cols):
            rows = slice(c * block, (c + 1) * block)
            piece = rounded[rows]
            stage[c, part] = piece
            scaled[rows, span] = (piece.astype(F32) * weights[c, 0].astype(F32)).astype(BF16)
        copy = pltpu.make_async_copy(stage.at[:, part], grids.at[:, 0, part], sems.at[part])
        copy.start()
        copies.append(copy)
    result = lax.dot_general(
        scaled[...],
        table[...],
        (((1,), (1,)), ((), ())),
        preferred_element_type=F32,
    )
    for c in range(cols):
        held = turn[16 + c : 17 + c, :]
        rows = slice(c * block, (c + 1) * block)
        low = held < 0
        high = held > tiles - 1
        real = pltpu.roll(result[rows, :WM], begins[c], 1)
        imag = pltpu.roll(result[rows, WM:], begins[c], 1)
        back[0, 0, c] = real.astype(BF16)
        back[1, 0, c] = imag.astype(BF16)
        real_low = jnp.where(low, real, zero)
        imag_low = jnp.where(low, imag, zero)
        real_high = jnp.where(high, real, zero)
        imag_high = jnp.where(high, imag, zero)
        to_prev[0, c] = (pltpu.roll(real_low, HALF, 1) + imag_low).astype(BF16)
        to_next[0, c] = (real_high + pltpu.roll(imag_high, HALF, 1)).astype(BF16)
    for copy in copies:
        copy.wait()


def windows_of(main, half, base, turn, out, buf, sems, tiles, cols, facets, facet):
    block = XM // facets
    zero = jnp.zeros((1, LANES), F32)
    first_tiles, _ = places_of(turn, cols)
    copies = []
    for c in range(cols):
        cosine = turn[c : c + 1, :]
        sine = turn[8 + c : 9 + c, :]
        is_low = lanes_of((1, LANES)).astype(F32) >= turn[24 + c : 25 + c, :]
        for i in range(facets // 2):
            rows = rows_of(facet, 2 * i + half, block)
            real = main[0, i, c].astype(F32)
            imag = main[1, i, c].astype(F32)
            values = (real * cosine - imag * sine, imag * cosine + real * sine)
            for part in range(2):
                base[part, i, c] = values[part]
                buf[c, 0, part, i] = jnp.where(is_low, values[part], zero).astype(BF16)
                buf[c, 1, part, i] = jnp.where(is_low, zero, values[part]).astype(BF16)
            for slot in range(2):
                which = first_tiles[c] + slot
                at = pl.multiple_of(jnp.clip(which, 0, tiles - 1) * LANES, LANES)
                copy = pltpu.make_async_copy(
                    buf.at[c, slot, :, i],
                    out.at[c, 0, :, rows, pl.ds(at, LANES)],
                    sems.at[c, slot, i],
                )
                inside = jnp.logical_and(which > 0, which < tiles - 1)
                pl.when(inside)(copy.start)
                copies.append((inside, copy))
    return copies


def ends_of(edges, half, base, turn, edge_turn, out, buf, sems, cols, facets, facet):
    shard = out.shape[4]
    tiles = shard // LANES
    block = XM // facets
    left = lanes_of((1, LANES)) < HALF
    zero = jnp.zeros((1, LANES), F32)
    copies = []
    for c in range(cols):
        edge_cosine = edge_turn[c : c + 1, :]
        edge_sine = edge_turn[8 + c : 9 + c, :]
        tile_at = turn[16 + c : 17 + c, :]
        in_first = tile_at == 0
        in_last = tile_at == tiles - 1
        for i in range(facets // 2):
            rows = rows_of(facet, 2 * i + half, block)
            prev = edges[0, i, c].astype(F32)
            nxt = edges[1, i, c].astype(F32)
            real = jnp.where(left, prev, pltpu.roll(nxt, HALF, 1))
            imag = jnp.where(left, pltpu.roll(prev, HALF, 1), nxt)
            ends = (
                real * edge_cosine - imag * edge_sine,
                imag * edge_cosine + real * edge_sine,
            )
            for part in range(2):
                value = base[part, i, c]
                end = ends[part]
                buf[c, 0, part, i] = (
                    jnp.where(left, end, zero) + jnp.where(in_first, value, zero)
                ).astype(BF16)
                buf[c, 1, part, i] = (
                    jnp.where(left, zero, end) + jnp.where(in_last, value, zero)
                ).astype(BF16)
            for slot, start in enumerate((0, shard - LANES)):
                copy = pltpu.make_async_copy(
                    buf.at[c, slot, :, i],
                    out.at[c, 0, :, rows, pl.ds(start, LANES)],
                    sems.at[c, slot, i],
                )
                copy.start()
                copies.append(copy)
    return copies


def finish(windows, ends):
    for inside, copy in windows:
        pl.when(inside)(copy.wait)
    for copy in ends:
        copy.wait()


def window_kernel(cols, facets, turn, even, whole, out, base, buf, sems):
    facet = lax.axis_index("facet")
    tiles = out.shape[4] // LANES
    finish(windows_of(even, 0, base, turn, out, buf, sems, tiles, cols, facets, facet), ())


def middle_kernel(
    cols,
    facets,
    turn,
    edge_turn,
    odd,
    even_edge,
    even_base,
    whole,
    out,
    base,
    buf,
    sems,
    end_buf,
    end_sems,
):
    facet = lax.axis_index("facet")
    tiles = out.shape[4] // LANES
    windows = windows_of(odd, 1, base, turn, out, buf, sems, tiles, cols, facets, facet)
    ends = ends_of(
        even_edge, 0, even_base, turn, edge_turn, out, end_buf, end_sems, cols, facets, facet
    )
    finish(windows, ends)


def end_kernel(cols, facets, turn, edge_turn, odd_edge, odd_base, whole, out, buf, sems):
    facet = lax.axis_index("facet")
    ends = ends_of(odd_edge, 1, odd_base, turn, edge_turn, out, buf, sems, cols, facets, facet)
    finish((), ends)


def swapped(block, bit):
    facets = lax.axis_size("facet")
    return lax.ppermute(block, "facet", [(i, i ^ bit) for i in range(facets)])


def shifted(block, distance):
    count = lax.axis_size("col")
    return lax.ppermute(block, "col", [(i, (i + distance) % count) for i in range(count)])


def added(kept, received):
    return (kept.astype(F32) + received.astype(F32)).astype(BF16)


def reduced(kept, sent, facets):
    received = swapped(sent, 1)
    bit = 2
    while bit < facets:
        blocks = added(kept, received)
        kept, sent = blocks[:, 0::2], blocks[:, 1::2]
        received = swapped(sent, bit)
        bit *= 2
    return kept, received


def gathered(blocks, facets):
    bit = facets // 2
    while bit > 1:
        received = swapped(blocks, bit)
        shape = (blocks.shape[0], -1) + blocks.shape[2:]
        blocks = jnp.stack([blocks, received], axis=2).reshape(shape)
        bit //= 2
    return blocks, swapped(blocks, 1)


def params(mib):
    return pltpu.CompilerParams(vmem_limit_bytes=mib * 1024 * 1024)


def computed(facet_spectra, facet_offsets, column_index, subgrid_offsets, weights):
    cols = facet_spectra.shape[0]
    shard = facet_spectra.shape[4]
    facets = lax.axis_size("facet")
    length = shard * lax.axis_size("col")
    block = XM // facets
    facet_spectra, facet_offsets, column_index, places = (
        pltpu.with_memory_space_constraint(array, pltpu.HBM)
        for array in (facet_spectra, facet_offsets, column_index, subgrid_offsets.T)
    )

    pieces = jax.ShapeDtypeStruct((2, facets // 2, cols, block, LANES), BF16)
    tile_pair = pltpu.VMEM((cols, 2, 2, XM, LANES), BF16)
    pair_sems = pltpu.SemaphoreType.DMA((cols, 2, facets))
    whole_scalars = [
        pltpu.SMEM(facet_offsets.shape, jnp.int32),
        pltpu.SMEM(column_index.shape, jnp.int32),
    ]
    edge_send, edge_turn = pl.pallas_call(
        functools.partial(edge_kernel, cols, facets, length),
        out_shape=(pieces, jax.ShapeDtypeStruct((16, LANES), F32)),
        in_specs=[HBM, HBM, HBM],
        out_specs=(VMEM, VMEM),
        scratch_shapes=[tile_pair, pair_sems, *whole_scalars, pltpu.SemaphoreType.DMA((2,))],
        compiler_params=params(12),
        name="edge",
    )(facet_offsets, column_index, facet_spectra)
    edge_keep, turn = pl.pallas_call(
        functools.partial(hold_kernel, cols, facets, length),
        out_shape=(pieces, jax.ShapeDtypeStruct((32, LANES), F32)),
        in_specs=[HBM, HBM, HBM, HBM, VMEM],
        out_specs=(VMEM, VMEM),
        scratch_shapes=[
            tile_pair,
            pair_sems,
            *whole_scalars,
            pltpu.SMEM(places.shape, jnp.int32),
            pltpu.SemaphoreType.DMA((3,)),
        ],
        compiler_params=params(12),
        name="hold",
    )(facet_offsets, column_index, places, facet_spectra, edge_turn)
    pair = reduced(edge_keep, edge_send, facets)
    edges = added(*pair)

    main_send, main_keep = pl.pallas_call(
        functools.partial(main_kernel, cols, facets),
        out_shape=(pieces, pieces),
        in_specs=[HBM, VMEM, VMEM],
        out_specs=(VMEM, VMEM),
        scratch_shapes=[tile_pair, pair_sems],
        compiler_params=params(12),
        name="main",
    )(facet_spectra, turn, edge_turn)
    main_kept, main_received = reduced(main_keep, main_send, facets)
    from_prev = shifted(edges[1], 1)
    from_next = shifted(edges[0], -1)

    table = pl.pallas_call(
        functools.partial(table_kernel, facets),
        out_shape=jax.ShapeDtypeStruct((2 * WM, 2 * XM), BF16),
        in_specs=[VMEM],
        out_specs=VMEM,
        compiler_params=params(12),
        name="table",
    )(edge_turn)
    shape = jax.ShapeDtypeStruct((cols, 1, 2, XM, shard), BF16)
    updates = pl.pallas_call(
        zero_kernel,
        out_shape=shape,
        in_specs=[VMEM],
        out_specs=HBM,
        scratch_shapes=[
            pltpu.VMEM((LANES, shard), BF16),
            pltpu.SemaphoreType.DMA((cols, 2, XM // LANES)),
        ],
        compiler_params=params(12),
        name="zero",
    )(turn)

    edge = jax.ShapeDtypeStruct((1, cols, block, LANES), BF16)
    grids, back, to_prev, to_next = pl.pallas_call(
        functools.partial(subgrid_kernel, cols, shard),
        out_shape=(
            jax.ShapeDtypeStruct((cols, 1, 2, block, XM), BF16),
            jax.ShapeDtypeStruct((2, 1, cols, block, LANES), BF16),
            edge,
            edge,
        ),
        in_specs=[VMEM] * 7,
        out_specs=(HBM, VMEM, VMEM, VMEM),
        scratch_shapes=[
            pltpu.VMEM((cols * block, 2 * WM), BF16),
            pltpu.VMEM((cols * block, 2 * XM), BF16),
            pltpu.VMEM((cols, 2, block, XM), BF16),
            pltpu.SemaphoreType.DMA((2,)),
        ],
        compiler_params=params(12),
        name="subgrid",
    )(turn, main_kept, main_received, from_prev, from_next, table, weights)

    came_prev = shifted(to_next, 1)
    came_next = shifted(to_prev, -1)
    even, odd = gathered(back, facets)
    even_edge, odd_edge = gathered(jnp.stack([came_prev, came_next]), facets)

    base = jax.ShapeDtypeStruct((2, facets // 2, cols, block, LANES), F32)
    tile_half = [
        pltpu.VMEM((cols, 2, 2, facets // 2, block, LANES), BF16),
        pltpu.SemaphoreType.DMA((cols, 2, facets // 2)),
    ]
    updates, even_base = pl.pallas_call(
        functools.partial(window_kernel, cols, facets),
        out_shape=(shape, base),
        in_specs=[VMEM, VMEM, HBM],
        out_specs=(HBM, VMEM),
        scratch_shapes=tile_half,
        input_output_aliases={2: 0},
        compiler_params=params(12),
        name="window",
    )(turn, even, updates)
    updates, odd_base = pl.pallas_call(
        functools.partial(middle_kernel, cols, facets),
        out_shape=(shape, base),
        in_specs=[VMEM] * 5 + [HBM],
        out_specs=(HBM, VMEM),
        scratch_shapes=tile_half * 2,
        input_output_aliases={5: 0},
        compiler_params=params(12),
        name="middle",
    )(turn, edge_turn, odd, even_edge, even_base, updates)
    updates = pl.pallas_call(
        functools.partial(end_kernel, cols, facets),
        out_shape=shape,
        in_specs=[VMEM] * 4 + [HBM],
        out_specs=HBM,
        scratch_shapes=tile_half,
        input_output_aliases={4: 0},
        compiler_params=params(12),
        name="end",
    )(turn, edge_turn, odd_edge, odd_base, updates)
    return grids, updates


def solution(mesh):
    in_specs = (
        P(None, "facet", None, None, "col"),
        P("facet", None),
        P(),
        P(None, "col"),
        P(None, "col", "facet", None),
    )
    out_specs = (P(None, "col", None, "facet", None), P(None, "facet", None, None, "col"))
    return jax.shard_map(
        computed, mesh=mesh, in_specs=in_specs, out_specs=out_specs, check_vma=False
    )
```

```python
import functools
import math

import jax
import jax.numpy as jnp
from jax import lax
from jax.experimental import pallas as pl
from jax.experimental.pallas import tpu as pltpu
from jax.sharding import PartitionSpec as P


IMAGE = 65536
XM = 512
WM = 128
XA = 448
LANES = 128
HALF = WM // 2

TAU = 2.0 * math.pi
BF16 = jnp.bfloat16
F32 = jnp.float32

VMEM = pl.BlockSpec(memory_space=pltpu.VMEM)
SMEM = pl.BlockSpec(memory_space=pltpu.SMEM)
HBM = pl.BlockSpec(memory_space=pltpu.HBM)


def remainder(value, modulus):
    if modulus & (modulus - 1) == 0:
        return value & (modulus - 1)
    return lax.rem(value, jnp.int32(modulus))


def modular(first, second, image):
    upper = second // 256
    lower = remainder(second, 256)
    return remainder(remainder(first * upper, image // 256) * 256 + first * lower, image)


def place_of(subgrid_offset, here, shard, length):
    start = subgrid_offset // (IMAGE // length) - here * shard - HALF + LANES
    return lax.div(start, jnp.int32(LANES)) - 1, remainder(start, LANES)


def lanes_of(shape):
    return lax.broadcasted_iota(jnp.int32, shape, len(shape) - 1)


def turns_of(turn, index, firsts, second, length):
    rows = lax.broadcasted_iota(jnp.int32, (8, LANES), 0)
    first = jnp.zeros((8, LANES), F32)
    for c, value in enumerate(firsts):
        first = jnp.where(rows == c, value.astype(F32), first)
    steps = remainder(index * second, length).astype(F32)
    angle = TAU * (first / IMAGE + steps / length)
    turn[0:8, :] = jnp.cos(angle)
    turn[8:16, :] = jnp.sin(angle)


def firsts_of(cols, offsets, column):
    return [modular(column[c] * XA, offsets[0, 0], IMAGE) for c in range(cols)]


def rows_of(facet, s, block):
    return pl.ds(pl.multiple_of((facet ^ s) * block, block), block)


def fetched(spectra, buf, sems, c, s, rows, places):
    copies = []
    for slot, at in enumerate(places):
        copy = pltpu.make_async_copy(
            spectra.at[c, 0, :, rows, pl.ds(at, LANES)],
            buf.at[c, slot, :, rows, :],
            sems.at[c, slot, s],
        )
        copy.start()
        copies.append(copy)
    return copies


def turned(parts, cosine, sine):
    return parts[0] * cosine + parts[1] * sine, parts[1] * cosine - parts[0] * sine


def places_of(turn, cols):
    tiles = [jnp.min(turn[16 + c : 17 + c, :]).astype(jnp.int32) for c in range(cols)]
    lanes = [jnp.max(turn[24 + c : 25 + c, :]).astype(jnp.int32) for c in range(cols)]
    return tiles, lanes


def edges_of(target, buf, copies, turn, order, cols, block, facet):
    left = lanes_of((1, LANES)) < HALF
    for c in range(cols):
        cosine = turn[c : c + 1, :]
        sine = turn[8 + c : 9 + c, :]
        for s in order:
            for copy in copies[c, s]:
                copy.wait()
            rows = rows_of(facet, s, block)
            parts = [
                jnp.where(
                    left,
                    buf[c, 0, part, rows, :].astype(F32),
                    buf[c, 1, part, rows, :].astype(F32),
                )
                for part in range(2)
            ]
            real, imag = turned(parts, cosine, sine)
            low = jnp.where(left, real, pltpu.roll(imag, HALF, 1))
            high = jnp.where(left, pltpu.roll(real, HALF, 1), imag)
            target[0, s // 2, c] = low.astype(BF16)
            target[1, s // 2, c] = high.astype(BF16)


def edge_kernel(
    cols, facets, length, offsets, column, spectra, send, turn, buf, sems, own, held, small
):
    shard = spectra.shape[4]
    block = XM // facets
    here = lax.axis_index("col")
    facet = lax.axis_index("facet")
    scalars = [
        pltpu.make_async_copy(offsets, own, small.at[0]),
        pltpu.make_async_copy(column, held, small.at[1]),
    ]
    for copy in scalars:
        copy.start()
    copies = {}
    order = range(1, facets, 2)
    for c in range(cols):
        for s in order:
            rows = rows_of(facet, s, block)
            copies[c, s] = fetched(spectra, buf, sems, c, s, rows, (0, shard - LANES))
    for copy in scalars:
        copy.wait()
    lanes = lanes_of((8, LANES))
    index = here * shard + lanes + jnp.where(lanes < HALF, 0, shard - LANES)
    turns_of(turn, index, firsts_of(cols, own, held), own[0, 1], length)
    edges_of(send, buf, copies, turn, order, cols, block, facet)


def hold_kernel(
    cols,
    facets,
    length,
    offsets,
    column,
    subgrid,
    spectra,
    edge_turn,
    keep,
    turn,
    buf,
    sems,
    own,
    held,
    spots,
    small,
):
    shard = spectra.shape[4]
    block = XM // facets
    here = lax.axis_index("col")
    facet = lax.axis_index("facet")
    scalars = [
        pltpu.make_async_copy(offsets, own, small.at[0]),
        pltpu.make_async_copy(column, held, small.at[1]),
        pltpu.make_async_copy(subgrid, spots, small.at[2]),
    ]
    for copy in scalars:
        copy.start()
    copies = {}
    order = range(0, facets, 2)
    for c in range(cols):
        for s in order:
            rows = rows_of(facet, s, block)
            copies[c, s] = fetched(spectra, buf, sems, c, s, rows, (0, shard - LANES))
    for copy in scalars:
        copy.wait()
    lanes = lanes_of((8, LANES))
    rows = lax.broadcasted_iota(jnp.int32, (8, LANES), 0)
    tile_at = jnp.zeros((8, LANES), jnp.int32)
    begins = jnp.zeros((8, LANES), jnp.int32)
    for c in range(cols):
        tile, lane = place_of(spots[0, c], here, shard, length)
        tile_at = jnp.where(rows == c, jnp.where(lanes >= lane, tile, tile + 1), tile_at)
        begins = jnp.where(rows == c, lane, begins)
    index = remainder(here * shard + lanes + tile_at * LANES + length, length)
    turns_of(turn, index, firsts_of(cols, own, held), own[0, 1], length)
    turn[16:24, :] = tile_at.astype(F32)
    turn[24:32, :] = begins.astype(F32)
    edges_of(keep, buf, copies, edge_turn, order, cols, block, facet)


def main_kernel(cols, facets, spectra, turn, after, send, keep, buf, sems):
    del after
    shard = spectra.shape[4]
    tiles = shard // LANES
    block = XM // facets
    facet = lax.axis_index("facet")
    copies = {}
    first_tiles, _ = places_of(turn, cols)
    for c in range(cols):
        tile = first_tiles[c]
        low = pl.multiple_of(jnp.maximum(tile, 0) * LANES, LANES)
        high = pl.multiple_of(jnp.minimum(tile + 1, tiles - 1) * LANES, LANES)
        for s in range(facets):
            rows = rows_of(facet, s, block)
            copies[c, s] = fetched(spectra, buf, sems, c, s, rows, (low, high))
    zero = jnp.zeros((1, LANES), F32)
    for c in range(cols):
        tile_at = turn[16 + c : 17 + c, :]
        is_low = lanes_of((1, LANES)).astype(F32) >= turn[24 + c : 25 + c, :]
        inside = jnp.logical_and(tile_at >= 0, tile_at <= tiles - 1)
        cosine = jnp.where(inside, turn[c : c + 1, :], zero)
        sine = jnp.where(inside, turn[8 + c : 9 + c, :], zero)
        for s in range(facets):
            for copy in copies[c, s]:
                copy.wait()
            rows = rows_of(facet, s, block)
            target = send if s % 2 else keep
            parts = [
                jnp.where(
                    is_low,
                    buf[c, 0, part, rows, :].astype(F32),
                    buf[c, 1, part, rows, :].astype(F32),
                )
                for part in range(2)
            ]
            real, imag = turned(parts, cosine, sine)
            target[0, s // 2, c] = real.astype(BF16)
            target[1, s // 2, c] = imag.astype(BF16)


def table_kernel(facets, after, table):
    del after
    place = lax.broadcasted_iota(jnp.int32, (WM, LANES), 0)
    cell = lanes_of((WM, LANES))
    angle = TAU * remainder((place - HALF) * cell + HALF * XM, XM).astype(F32) / XM
    relative = (place.astype(F32) + 0.5 - WM / 2.0) / (WM / 2.0)
    taper = (0.3 + 0.7 * (1.0 - relative * relative)) / jnp.sqrt(
        jnp.full((1, LANES), WM * facets, F32)
    )
    cosine = taper * jnp.cos(angle)
    sine = taper * jnp.sin(angle)
    for tile in range(XM // LANES):
        first = tile * LANES - XM // 2
        quarter = remainder((place - HALF) * (first * 4 // XM) + HALF * 4, 4)
        odd = remainder(quarter, 2) == 1
        real = jnp.where(odd, sine, cosine)
        imag = jnp.where(odd, cosine, sine)
        real = jnp.where(jnp.logical_or(quarter == 1, quarter == 2), -real, real).astype(BF16)
        imag = jnp.where(quarter >= 2, -imag, imag)
        span = slice(tile * LANES, (tile + 1) * LANES)
        other = slice(XM + tile * LANES, XM + (tile + 1) * LANES)
        table[:WM, span] = real
        table[WM:, other] = real
        table[:WM, other] = imag.astype(BF16)
        table[WM:, span] = (-imag).astype(BF16)


def zero_kernel(after, out, buf, sems):
    del after
    cols, _, _, height, _ = out.shape
    block = buf.shape[0]
    buf[...] = jnp.zeros(buf.shape, BF16)
    copies = []
    for c in range(cols):
        for part in range(2):
            for i in range(height // block):
                rows = pl.ds(i * block, block)
                copies.append(
                    pltpu.make_async_copy(buf, out.at[c, 0, part, rows, :], sems.at[c, part, i])
                )
    for copy in copies:
        copy.start()
    for copy in copies:
        copy.wait()


def subgrid_kernel(
    cols,
    shard,
    turn,
    kept,
    received,
    from_prev,
    from_next,
    table,
    weights,
    grids,
    back,
    to_prev,
    to_next,
    stack,
    scaled,
):
    tiles = shard // LANES
    block = kept.shape[3]
    zero = jnp.zeros((1, LANES), F32)
    _, begins = places_of(turn, cols)
    for c in range(cols):
        held = turn[16 + c : 17 + c, :]
        low = held < 0
        high = held > tiles - 1
        prev = from_prev[0, c].astype(F32)
        nxt = from_next[0, c].astype(F32)
        shift = remainder(LANES - begins[c], LANES)
        real = kept[0, 0, c].astype(F32) + received[0, 0, c].astype(F32)
        real = real + jnp.where(low, pltpu.roll(prev, HALF, 1), jnp.where(high, nxt, zero))
        imag = kept[1, 0, c].astype(F32) + received[1, 0, c].astype(F32)
        imag = imag + jnp.where(low, prev, jnp.where(high, pltpu.roll(nxt, HALF, 1), zero))
        rows = slice(c * block, (c + 1) * block)
        stack[rows, :WM] = pltpu.roll(real, shift, 1).astype(BF16)
        stack[rows, WM:] = pltpu.roll(imag, shift, 1).astype(BF16)
    for part in range(2):
        span = slice(part * XM, (part + 1) * XM)
        product = jnp.dot(stack[...], table[:, span], preferred_element_type=F32)
        rounded = product.astype(BF16)
        for c in range(cols):
            rows = slice(c * block, (c + 1) * block)
            piece = rounded[rows]
            grids[c, 0, part] = piece
            scaled[rows, span] = (piece.astype(F32) * weights[c, 0].astype(F32)).astype(BF16)
    result = lax.dot_general(
        scaled[...],
        table[...],
        (((1,), (1,)), ((), ())),
        preferred_element_type=F32,
    )
    for c in range(cols):
        held = turn[16 + c : 17 + c, :]
        rows = slice(c * block, (c + 1) * block)
        low = held < 0
        high = held > tiles - 1
        real = pltpu.roll(result[rows, :WM], begins[c], 1)
        imag = pltpu.roll(result[rows, WM:], begins[c], 1)
        back[0, 0, c] = real.astype(BF16)
        back[1, 0, c] = imag.astype(BF16)
        real_low = jnp.where(low, real, zero)
        imag_low = jnp.where(low, imag, zero)
        real_high = jnp.where(high, real, zero)
        imag_high = jnp.where(high, imag, zero)
        to_prev[0, c] = (pltpu.roll(real_low, HALF, 1) + imag_low).astype(BF16)
        to_next[0, c] = (real_high + pltpu.roll(imag_high, HALF, 1)).astype(BF16)


def windows_of(main, half, base, turn, out, buf, sems, tiles, cols, facets, facet):
    block = XM // facets
    zero = jnp.zeros((1, LANES), F32)
    first_tiles, _ = places_of(turn, cols)
    copies = []
    for c in range(cols):
        cosine = turn[c : c + 1, :]
        sine = turn[8 + c : 9 + c, :]
        is_low = lanes_of((1, LANES)).astype(F32) >= turn[24 + c : 25 + c, :]
        for i in range(facets // 2):
            rows = rows_of(facet, 2 * i + half, block)
            real = main[0, i, c].astype(F32)
            imag = main[1, i, c].astype(F32)
            values = (real * cosine - imag * sine, imag * cosine + real * sine)
            for part in range(2):
                base[part, i, c] = values[part]
                buf[c, 0, part, i] = jnp.where(is_low, values[part], zero).astype(BF16)
                buf[c, 1, part, i] = jnp.where(is_low, zero, values[part]).astype(BF16)
            for slot in range(2):
                which = first_tiles[c] + slot
                at = pl.multiple_of(jnp.clip(which, 0, tiles - 1) * LANES, LANES)
                copy = pltpu.make_async_copy(
                    buf.at[c, slot, :, i],
                    out.at[c, 0, :, rows, pl.ds(at, LANES)],
                    sems.at[c, slot, i],
                )
                inside = jnp.logical_and(which > 0, which < tiles - 1)
                pl.when(inside)(copy.start)
                copies.append((inside, copy))
    return copies


def ends_of(edges, half, base, turn, edge_turn, out, buf, sems, cols, facets, facet):
    shard = out.shape[4]
    tiles = shard // LANES
    block = XM // facets
    left = lanes_of((1, LANES)) < HALF
    zero = jnp.zeros((1, LANES), F32)
    copies = []
    for c in range(cols):
        edge_cosine = edge_turn[c : c + 1, :]
        edge_sine = edge_turn[8 + c : 9 + c, :]
        tile_at = turn[16 + c : 17 + c, :]
        in_first = tile_at == 0
        in_last = tile_at == tiles - 1
        for i in range(facets // 2):
            rows = rows_of(facet, 2 * i + half, block)
            prev = edges[0, i, c].astype(F32)
            nxt = edges[1, i, c].astype(F32)
            real = jnp.where(left, prev, pltpu.roll(nxt, HALF, 1))
            imag = jnp.where(left, pltpu.roll(prev, HALF, 1), nxt)
            ends = (
                real * edge_cosine - imag * edge_sine,
                imag * edge_cosine + real * edge_sine,
            )
            for part in range(2):
                value = base[part, i, c]
                end = ends[part]
                buf[c, 0, part, i] = (
                    jnp.where(left, end, zero) + jnp.where(in_first, value, zero)
                ).astype(BF16)
                buf[c, 1, part, i] = (
                    jnp.where(left, zero, end) + jnp.where(in_last, value, zero)
                ).astype(BF16)
            for slot, start in enumerate((0, shard - LANES)):
                copy = pltpu.make_async_copy(
                    buf.at[c, slot, :, i],
                    out.at[c, 0, :, rows, pl.ds(start, LANES)],
                    sems.at[c, slot, i],
                )
                copy.start()
                copies.append(copy)
    return copies


def finish(windows, ends):
    for inside, copy in windows:
        pl.when(inside)(copy.wait)
    for copy in ends:
        copy.wait()


def window_kernel(
    cols, facets, turn, even, held, whole, out, base, grids, buf, sems, grid_sem
):
    facet = lax.axis_index("facet")
    tiles = out.shape[4] // LANES
    store = pltpu.make_async_copy(held, grids, grid_sem)
    store.start()
    windows = windows_of(even, 0, base, turn, out, buf, sems, tiles, cols, facets, facet)
    finish(windows, (store,))


def middle_kernel(
    cols,
    facets,
    turn,
    edge_turn,
    odd,
    even_edge,
    even_base,
    whole,
    out,
    base,
    buf,
    sems,
    end_buf,
    end_sems,
):
    facet = lax.axis_index("facet")
    tiles = out.shape[4] // LANES
    windows = windows_of(odd, 1, base, turn, out, buf, sems, tiles, cols, facets, facet)
    ends = ends_of(
        even_edge, 0, even_base, turn, edge_turn, out, end_buf, end_sems, cols, facets, facet
    )
    finish(windows, ends)


def end_kernel(cols, facets, turn, edge_turn, odd_edge, odd_base, whole, out, buf, sems):
    facet = lax.axis_index("facet")
    ends = ends_of(odd_edge, 1, odd_base, turn, edge_turn, out, buf, sems, cols, facets, facet)
    finish((), ends)


def swapped(block, bit):
    facets = lax.axis_size("facet")
    return lax.ppermute(block, "facet", [(i, i ^ bit) for i in range(facets)])


def shifted(block, distance):
    count = lax.axis_size("col")
    return lax.ppermute(block, "col", [(i, (i + distance) % count) for i in range(count)])


def added(kept, received):
    return (kept.astype(F32) + received.astype(F32)).astype(BF16)


def reduced(kept, sent, facets):
    received = swapped(sent, 1)
    bit = 2
    while bit < facets:
        blocks = added(kept, received)
        kept, sent = blocks[:, 0::2], blocks[:, 1::2]
        received = swapped(sent, bit)
        bit *= 2
    return kept, received


def gathered(blocks, facets):
    bit = facets // 2
    while bit > 1:
        received = swapped(blocks, bit)
        shape = (blocks.shape[0], -1) + blocks.shape[2:]
        blocks = jnp.stack([blocks, received], axis=2).reshape(shape)
        bit //= 2
    return blocks, swapped(blocks, 1)


def params(mib):
    return pltpu.CompilerParams(vmem_limit_bytes=mib * 1024 * 1024)


def computed(facet_spectra, facet_offsets, column_index, subgrid_offsets, weights):
    cols = facet_spectra.shape[0]
    shard = facet_spectra.shape[4]
    facets = lax.axis_size("facet")
    length = shard * lax.axis_size("col")
    block = XM // facets
    facet_spectra, facet_offsets, column_index, places = (
        pltpu.with_memory_space_constraint(array, pltpu.HBM)
        for array in (facet_spectra, facet_offsets, column_index, subgrid_offsets.T)
    )

    pieces = jax.ShapeDtypeStruct((2, facets // 2, cols, block, LANES), BF16)
    tile_pair = pltpu.VMEM((cols, 2, 2, XM, LANES), BF16)
    pair_sems = pltpu.SemaphoreType.DMA((cols, 2, facets))
    whole_scalars = [
        pltpu.SMEM(facet_offsets.shape, jnp.int32),
        pltpu.SMEM(column_index.shape, jnp.int32),
    ]
    edge_send, edge_turn = pl.pallas_call(
        functools.partial(edge_kernel, cols, facets, length),
        out_shape=(pieces, jax.ShapeDtypeStruct((16, LANES), F32)),
        in_specs=[HBM, HBM, HBM],
        out_specs=(VMEM, VMEM),
        scratch_shapes=[tile_pair, pair_sems, *whole_scalars, pltpu.SemaphoreType.DMA((2,))],
        compiler_params=params(12),
        name="edge",
    )(facet_offsets, column_index, facet_spectra)
    edge_keep, turn = pl.pallas_call(
        functools.partial(hold_kernel, cols, facets, length),
        out_shape=(pieces, jax.ShapeDtypeStruct((32, LANES), F32)),
        in_specs=[HBM, HBM, HBM, HBM, VMEM],
        out_specs=(VMEM, VMEM),
        scratch_shapes=[
            tile_pair,
            pair_sems,
            *whole_scalars,
            pltpu.SMEM(places.shape, jnp.int32),
            pltpu.SemaphoreType.DMA((3,)),
        ],
        compiler_params=params(12),
        name="hold",
    )(facet_offsets, column_index, places, facet_spectra, edge_turn)
    pair = reduced(edge_keep, edge_send, facets)
    edges = added(*pair)

    main_send, main_keep = pl.pallas_call(
        functools.partial(main_kernel, cols, facets),
        out_shape=(pieces, pieces),
        in_specs=[HBM, VMEM, VMEM],
        out_specs=(VMEM, VMEM),
        scratch_shapes=[tile_pair, pair_sems],
        compiler_params=params(12),
        name="main",
    )(facet_spectra, turn, edge_turn)
    main_kept, main_received = reduced(main_keep, main_send, facets)
    from_prev = shifted(edges[1], 1)
    from_next = shifted(edges[0], -1)

    table = pl.pallas_call(
        functools.partial(table_kernel, facets),
        out_shape=jax.ShapeDtypeStruct((2 * WM, 2 * XM), BF16),
        in_specs=[VMEM],
        out_specs=VMEM,
        compiler_params=params(12),
        name="table",
    )(edge_turn)
    shape = jax.ShapeDtypeStruct((cols, 1, 2, XM, shard), BF16)
    updates = pl.pallas_call(
        zero_kernel,
        out_shape=shape,
        in_specs=[VMEM],
        out_specs=HBM,
        scratch_shapes=[
            pltpu.VMEM((LANES, shard), BF16),
            pltpu.SemaphoreType.DMA((cols, 2, XM // LANES)),
        ],
        compiler_params=params(12),
        name="zero",
    )(turn)

    edge = jax.ShapeDtypeStruct((1, cols, block, LANES), BF16)
    grid_shape = jax.ShapeDtypeStruct((cols, 1, 2, block, XM), BF16)
    held, back, to_prev, to_next = pl.pallas_call(
        functools.partial(subgrid_kernel, cols, shard),
        out_shape=(
            grid_shape,
            jax.ShapeDtypeStruct((2, 1, cols, block, LANES), BF16),
            edge,
            edge,
        ),
        in_specs=[VMEM] * 7,
        out_specs=(VMEM, VMEM, VMEM, VMEM),
        scratch_shapes=[
            pltpu.VMEM((cols * block, 2 * WM), BF16),
            pltpu.VMEM((cols * block, 2 * XM), BF16),
        ],
        compiler_params=params(12),
        name="subgrid",
    )(turn, main_kept, main_received, from_prev, from_next, table, weights)

    came_prev = shifted(to_next, 1)
    came_next = shifted(to_prev, -1)
    even, odd = gathered(back, facets)
    even_edge, odd_edge = gathered(jnp.stack([came_prev, came_next]), facets)

    base = jax.ShapeDtypeStruct((2, facets // 2, cols, block, LANES), F32)
    tile_half = [
        pltpu.VMEM((cols, 2, 2, facets // 2, block, LANES), BF16),
        pltpu.SemaphoreType.DMA((cols, 2, facets // 2)),
    ]
    updates, even_base, grids = pl.pallas_call(
        functools.partial(window_kernel, cols, facets),
        out_shape=(shape, base, grid_shape),
        in_specs=[VMEM, VMEM, VMEM, HBM],
        out_specs=(HBM, VMEM, HBM),
        scratch_shapes=[*tile_half, pltpu.SemaphoreType.DMA(())],
        input_output_aliases={3: 0},
        compiler_params=params(12),
        name="window",
    )(turn, even, held, updates)
    updates, odd_base = pl.pallas_call(
        functools.partial(middle_kernel, cols, facets),
        out_shape=(shape, base),
        in_specs=[VMEM] * 5 + [HBM],
        out_specs=(HBM, VMEM),
        scratch_shapes=tile_half * 2,
        input_output_aliases={5: 0},
        compiler_params=params(12),
        name="middle",
    )(turn, edge_turn, odd, even_edge, even_base, updates)
    updates = pl.pallas_call(
        functools.partial(end_kernel, cols, facets),
        out_shape=shape,
        in_specs=[VMEM] * 4 + [HBM],
        out_specs=HBM,
        scratch_shapes=tile_half,
        input_output_aliases={4: 0},
        compiler_params=params(12),
        name="end",
    )(turn, edge_turn, odd_edge, odd_base, updates)
    return grids, updates


def solution(mesh):
    in_specs = (
        P(None, "facet", None, None, "col"),
        P("facet", None),
        P(),
        P(None, "col"),
        P(None, "col", "facet", None),
    )
    out_specs = (P(None, "col", None, "facet", None), P(None, "facet", None, None, "col"))
    return jax.shard_map(
        computed, mesh=mesh, in_specs=in_specs, out_specs=out_specs, check_vma=False
    )
```

```python
import functools
import math

import jax
import jax.numpy as jnp
from jax import lax
from jax.experimental import pallas as pl
from jax.experimental.pallas import tpu as pltpu
from jax.sharding import PartitionSpec as P


IMAGE = 65536
XM = 512
WM = 128
XA = 448
LANES = 128
HALF = WM // 2

TAU = 2.0 * math.pi
BF16 = jnp.bfloat16
F32 = jnp.float32

VMEM = pl.BlockSpec(memory_space=pltpu.VMEM)
SMEM = pl.BlockSpec(memory_space=pltpu.SMEM)
HBM = pl.BlockSpec(memory_space=pltpu.HBM)


def remainder(value, modulus):
    if modulus & (modulus - 1) == 0:
        return value & (modulus - 1)
    return lax.rem(value, jnp.int32(modulus))


def modular(first, second, image):
    upper = second // 256
    lower = remainder(second, 256)
    return remainder(remainder(first * upper, image // 256) * 256 + first * lower, image)


def place_of(subgrid_offset, here, shard, length):
    start = subgrid_offset // (IMAGE // length) - here * shard - HALF + LANES
    return lax.div(start, jnp.int32(LANES)) - 1, remainder(start, LANES)


def lanes_of(shape):
    return lax.broadcasted_iota(jnp.int32, shape, len(shape) - 1)


def turns_of(turn, index, firsts, second, length):
    rows = lax.broadcasted_iota(jnp.int32, (8, LANES), 0)
    first = jnp.zeros((8, LANES), F32)
    for c, value in enumerate(firsts):
        first = jnp.where(rows == c, value.astype(F32), first)
    steps = remainder(index * second, length).astype(F32)
    angle = TAU * (first / IMAGE + steps / length)
    turn[0:8, :] = jnp.cos(angle)
    turn[8:16, :] = jnp.sin(angle)


def firsts_of(cols, offsets, column):
    return [modular(column[c] * XA, offsets[0, 0], IMAGE) for c in range(cols)]


def rows_of(facet, s, block):
    return pl.ds(pl.multiple_of((facet ^ s) * block, block), block)


def fetched(spectra, buf, sems, c, s, rows, places):
    copies = []
    for slot, at in enumerate(places):
        copy = pltpu.make_async_copy(
            spectra.at[c, 0, :, rows, pl.ds(at, LANES)],
            buf.at[c, slot, :, rows, :],
            sems.at[c, slot, s],
        )
        copy.start()
        copies.append(copy)
    return copies


def turned(parts, cosine, sine):
    return parts[0] * cosine + parts[1] * sine, parts[1] * cosine - parts[0] * sine


def places_of(turn, cols):
    tiles = [jnp.min(turn[16 + c : 17 + c, :]).astype(jnp.int32) for c in range(cols)]
    lanes = [jnp.max(turn[24 + c : 25 + c, :]).astype(jnp.int32) for c in range(cols)]
    return tiles, lanes


def edges_of(target, buf, copies, turn, order, cols, block, facet):
    left = lanes_of((1, LANES)) < HALF
    for c in range(cols):
        cosine = turn[c : c + 1, :]
        sine = turn[8 + c : 9 + c, :]
        for s in order:
            for copy in copies[c, s]:
                copy.wait()
            rows = rows_of(facet, s, block)
            parts = [
                jnp.where(
                    left,
                    buf[c, 0, part, rows, :].astype(F32),
                    buf[c, 1, part, rows, :].astype(F32),
                )
                for part in range(2)
            ]
            real, imag = turned(parts, cosine, sine)
            low = jnp.where(left, real, pltpu.roll(imag, HALF, 1))
            high = jnp.where(left, pltpu.roll(real, HALF, 1), imag)
            target[0, s // 2, c] = low.astype(BF16)
            target[1, s // 2, c] = high.astype(BF16)


def edge_kernel(
    cols, facets, length, offsets, column, spectra, send, turn, buf, sems, own, held, small
):
    shard = spectra.shape[4]
    block = XM // facets
    here = lax.axis_index("col")
    facet = lax.axis_index("facet")
    scalars = [
        pltpu.make_async_copy(offsets, own, small.at[0]),
        pltpu.make_async_copy(column, held, small.at[1]),
    ]
    for copy in scalars:
        copy.start()
    copies = {}
    order = range(1, facets, 2)
    for c in range(cols):
        for s in order:
            rows = rows_of(facet, s, block)
            copies[c, s] = fetched(spectra, buf, sems, c, s, rows, (0, shard - LANES))
    for copy in scalars:
        copy.wait()
    lanes = lanes_of((8, LANES))
    index = here * shard + lanes + jnp.where(lanes < HALF, 0, shard - LANES)
    turns_of(turn, index, firsts_of(cols, own, held), own[0, 1], length)
    edges_of(send, buf, copies, turn, order, cols, block, facet)


def hold_kernel(
    cols,
    facets,
    length,
    offsets,
    column,
    subgrid,
    spectra,
    edge_turn,
    keep,
    turn,
    buf,
    sems,
    own,
    held,
    spots,
    small,
):
    shard = spectra.shape[4]
    block = XM // facets
    here = lax.axis_index("col")
    facet = lax.axis_index("facet")
    scalars = [
        pltpu.make_async_copy(offsets, own, small.at[0]),
        pltpu.make_async_copy(column, held, small.at[1]),
        pltpu.make_async_copy(subgrid, spots, small.at[2]),
    ]
    for copy in scalars:
        copy.start()
    copies = {}
    order = range(0, facets, 2)
    for c in range(cols):
        for s in order:
            rows = rows_of(facet, s, block)
            copies[c, s] = fetched(spectra, buf, sems, c, s, rows, (0, shard - LANES))
    for copy in scalars:
        copy.wait()
    lanes = lanes_of((8, LANES))
    rows = lax.broadcasted_iota(jnp.int32, (8, LANES), 0)
    tile_at = jnp.zeros((8, LANES), jnp.int32)
    begins = jnp.zeros((8, LANES), jnp.int32)
    for c in range(cols):
        tile, lane = place_of(spots[0, c], here, shard, length)
        tile_at = jnp.where(rows == c, jnp.where(lanes >= lane, tile, tile + 1), tile_at)
        begins = jnp.where(rows == c, lane, begins)
    index = remainder(here * shard + lanes + tile_at * LANES + length, length)
    turns_of(turn, index, firsts_of(cols, own, held), own[0, 1], length)
    turn[16:24, :] = tile_at.astype(F32)
    turn[24:32, :] = begins.astype(F32)
    edges_of(keep, buf, copies, edge_turn, order, cols, block, facet)


def main_kernel(cols, facets, spectra, turn, after, send, keep, buf, sems):
    del after
    shard = spectra.shape[4]
    tiles = shard // LANES
    block = XM // facets
    facet = lax.axis_index("facet")
    copies = {}
    first_tiles, _ = places_of(turn, cols)
    for c in range(cols):
        tile = first_tiles[c]
        low = pl.multiple_of(jnp.maximum(tile, 0) * LANES, LANES)
        high = pl.multiple_of(jnp.minimum(tile + 1, tiles - 1) * LANES, LANES)
        for s in range(facets):
            rows = rows_of(facet, s, block)
            copies[c, s] = fetched(spectra, buf, sems, c, s, rows, (low, high))
    zero = jnp.zeros((1, LANES), F32)
    for c in range(cols):
        tile_at = turn[16 + c : 17 + c, :]
        is_low = lanes_of((1, LANES)).astype(F32) >= turn[24 + c : 25 + c, :]
        inside = jnp.logical_and(tile_at >= 0, tile_at <= tiles - 1)
        cosine = jnp.where(inside, turn[c : c + 1, :], zero)
        sine = jnp.where(inside, turn[8 + c : 9 + c, :], zero)
        for s in range(facets):
            for copy in copies[c, s]:
                copy.wait()
            rows = rows_of(facet, s, block)
            target = send if s % 2 else keep
            parts = [
                jnp.where(
                    is_low,
                    buf[c, 0, part, rows, :].astype(F32),
                    buf[c, 1, part, rows, :].astype(F32),
                )
                for part in range(2)
            ]
            real, imag = turned(parts, cosine, sine)
            target[0, s // 2, c] = real.astype(BF16)
            target[1, s // 2, c] = imag.astype(BF16)


def table_kernel(facets, after, table):
    del after
    place = lax.broadcasted_iota(jnp.int32, (WM, LANES), 0)
    cell = lanes_of((WM, LANES))
    angle = TAU * remainder((place - HALF) * cell + HALF * XM, XM).astype(F32) / XM
    relative = (place.astype(F32) + 0.5 - WM / 2.0) / (WM / 2.0)
    taper = (0.3 + 0.7 * (1.0 - relative * relative)) / jnp.sqrt(
        jnp.full((1, LANES), WM * facets, F32)
    )
    cosine = taper * jnp.cos(angle)
    sine = taper * jnp.sin(angle)
    for tile in range(XM // LANES):
        first = tile * LANES - XM // 2
        quarter = remainder((place - HALF) * (first * 4 // XM) + HALF * 4, 4)
        odd = remainder(quarter, 2) == 1
        real = jnp.where(odd, sine, cosine)
        imag = jnp.where(odd, cosine, sine)
        real = jnp.where(jnp.logical_or(quarter == 1, quarter == 2), -real, real).astype(BF16)
        imag = jnp.where(quarter >= 2, -imag, imag)
        span = slice(tile * LANES, (tile + 1) * LANES)
        other = slice(XM + tile * LANES, XM + (tile + 1) * LANES)
        table[:WM, span] = real
        table[WM:, other] = real
        table[:WM, other] = imag.astype(BF16)
        table[WM:, span] = (-imag).astype(BF16)


def zero_kernel(after, out, buf, sems):
    del after
    cols, _, _, height, _ = out.shape
    block = buf.shape[0]
    buf[...] = jnp.zeros(buf.shape, BF16)
    copies = []
    for c in range(cols):
        for part in range(2):
            for i in range(height // block):
                rows = pl.ds(i * block, block)
                copies.append(
                    pltpu.make_async_copy(buf, out.at[c, 0, part, rows, :], sems.at[c, part, i])
                )
    for copy in copies:
        copy.start()
    for copy in copies:
        copy.wait()


def subgrid_kernel(
    cols,
    shard,
    turn,
    kept,
    received,
    from_prev,
    from_next,
    table,
    weights,
    grids,
    back,
    to_prev,
    to_next,
    stack,
    scaled,
):
    tiles = shard // LANES
    block = kept.shape[3]
    zero = jnp.zeros((1, LANES), F32)
    _, begins = places_of(turn, cols)
    for c in range(cols):
        held = turn[16 + c : 17 + c, :]
        low = held < 0
        high = held > tiles - 1
        prev = from_prev[0, c].astype(F32)
        nxt = from_next[0, c].astype(F32)
        shift = remainder(LANES - begins[c], LANES)
        real = kept[0, 0, c].astype(F32) + received[0, 0, c].astype(F32)
        real = real + jnp.where(low, pltpu.roll(prev, HALF, 1), jnp.where(high, nxt, zero))
        imag = kept[1, 0, c].astype(F32) + received[1, 0, c].astype(F32)
        imag = imag + jnp.where(low, prev, jnp.where(high, pltpu.roll(nxt, HALF, 1), zero))
        rows = slice(c * block, (c + 1) * block)
        stack[rows, :WM] = pltpu.roll(real, shift, 1).astype(BF16)
        stack[rows, WM:] = pltpu.roll(imag, shift, 1).astype(BF16)
    for part in range(2):
        span = slice(part * XM, (part + 1) * XM)
        product = jnp.dot(stack[...], table[:, span], preferred_element_type=F32)
        rounded = product.astype(BF16)
        for c in range(cols):
            rows = slice(c * block, (c + 1) * block)
            piece = rounded[rows]
            grids[c, 0, part] = piece
            scaled[rows, span] = (piece.astype(F32) * weights[c, 0].astype(F32)).astype(BF16)
    result = lax.dot_general(
        scaled[...],
        table[...],
        (((1,), (1,)), ((), ())),
        preferred_element_type=F32,
    )
    for c in range(cols):
        held = turn[16 + c : 17 + c, :]
        rows = slice(c * block, (c + 1) * block)
        low = held < 0
        high = held > tiles - 1
        real = pltpu.roll(result[rows, :WM], begins[c], 1)
        imag = pltpu.roll(result[rows, WM:], begins[c], 1)
        back[0, 0, c] = real.astype(BF16)
        back[1, 0, c] = imag.astype(BF16)
        real_low = jnp.where(low, real, zero)
        imag_low = jnp.where(low, imag, zero)
        real_high = jnp.where(high, real, zero)
        imag_high = jnp.where(high, imag, zero)
        to_prev[0, c] = (pltpu.roll(real_low, HALF, 1) + imag_low).astype(BF16)
        to_next[0, c] = (real_high + pltpu.roll(imag_high, HALF, 1)).astype(BF16)


def window_of(main, i, c, turn):
    cosine = turn[c : c + 1, :]
    sine = turn[8 + c : 9 + c, :]
    real = main[0, i, c].astype(F32)
    imag = main[1, i, c].astype(F32)
    return real * cosine - imag * sine, imag * cosine + real * sine


def windows_of(mains, slots, base, turn, out, buf, sems, cols, block):
    tiles = out.shape[4] // LANES
    facet = lax.axis_index("facet")
    zero = jnp.zeros((1, LANES), F32)
    first_tiles, _ = places_of(turn, cols)
    copies = []
    for c in range(cols):
        is_low = lanes_of((1, LANES)).astype(F32) >= turn[24 + c : 25 + c, :]
        for i, slot in enumerate(slots):
            rows = rows_of(facet, slot, block)
            main, at_main = mains[i]
            values = window_of(main, at_main, c, turn)
            for part in range(2):
                base[part, i, c] = values[part]
                buf[c, 0, part, i] = jnp.where(is_low, values[part], zero).astype(BF16)
                buf[c, 1, part, i] = jnp.where(is_low, zero, values[part]).astype(BF16)
            for side in range(2):
                which = first_tiles[c] + side
                at = pl.multiple_of(jnp.clip(which, 0, tiles - 1) * LANES, LANES)
                copy = pltpu.make_async_copy(
                    buf.at[c, side, :, i],
                    out.at[c, 0, :, rows, pl.ds(at, LANES)],
                    sems.at[c, side, i],
                )
                inside = jnp.logical_and(which > 0, which < tiles - 1)
                pl.when(inside)(copy.start)
                copies.append((inside, copy))
    return copies


def ends_of(edges, slots, base, turn, edge_turn, out, buf, sems, cols, block):
    shard = out.shape[4]
    tiles = shard // LANES
    facet = lax.axis_index("facet")
    left = lanes_of((1, LANES)) < HALF
    zero = jnp.zeros((1, LANES), F32)
    copies = []
    for c in range(cols):
        edge_cosine = edge_turn[c : c + 1, :]
        edge_sine = edge_turn[8 + c : 9 + c, :]
        tile_at = turn[16 + c : 17 + c, :]
        in_first = tile_at == 0
        in_last = tile_at == tiles - 1
        for i, slot in enumerate(slots):
            rows = rows_of(facet, slot, block)
            edge, at_edge = edges[i]
            prev = edge[0, at_edge, c].astype(F32)
            nxt = edge[1, at_edge, c].astype(F32)
            real = jnp.where(left, prev, pltpu.roll(nxt, HALF, 1))
            imag = jnp.where(left, pltpu.roll(prev, HALF, 1), nxt)
            ends = (
                real * edge_cosine - imag * edge_sine,
                imag * edge_cosine + real * edge_sine,
            )
            for part in range(2):
                value = base[part, i, c]
                end = ends[part]
                buf[c, 0, part, i] = (
                    jnp.where(left, end, zero) + jnp.where(in_first, value, zero)
                ).astype(BF16)
                buf[c, 1, part, i] = (
                    jnp.where(left, zero, end) + jnp.where(in_last, value, zero)
                ).astype(BF16)
            for side, start in enumerate((0, shard - LANES)):
                copy = pltpu.make_async_copy(
                    buf.at[c, side, :, i],
                    out.at[c, 0, :, rows, pl.ds(start, LANES)],
                    sems.at[c, side, i],
                )
                copy.start()
                copies.append(copy)
    return copies


def finish(windows, ends):
    for inside, copy in windows:
        pl.when(inside)(copy.wait)
    for copy in ends:
        copy.wait()


def each(array, count):
    return [(array, i) for i in range(count)]


def early_kernel(
    cols,
    turn,
    edge_turn,
    own,
    near,
    own_edge,
    held,
    whole,
    out,
    grids,
    near_base,
    base,
    buf,
    sems,
    end_buf,
    end_sems,
    grid_sem,
):
    block = own.shape[3]
    store = pltpu.make_async_copy(held, grids, grid_sem)
    store.start()
    first = buf.at[:, :, :, 0:1], sems.at[:, :, 0:1]
    second = buf.at[:, :, :, 1:2], sems.at[:, :, 1:2]
    windows = windows_of(((own, 0),), (0,), base, turn, out, *first, cols, block)
    ends = ends_of(((own_edge, 0),), (0,), base, turn, edge_turn, out, end_buf, end_sems, cols, block)
    windows += windows_of(((near, 0),), (1,), near_base, turn, out, *second, cols, block)
    finish(windows, (*ends, store))


def window_kernel(
    cols,
    slots,
    turn,
    edge_turn,
    main,
    near_edge,
    near_base,
    whole,
    out,
    base,
    buf,
    sems,
    end_buf,
    end_sems,
):
    block = main.shape[3]
    mains = each(main, len(slots))
    windows = windows_of(mains, slots, base, turn, out, buf, sems, cols, block)
    edges = ((near_edge, 0),)
    ends = ends_of(edges, (1,), near_base, turn, edge_turn, out, end_buf, end_sems, cols, block)
    finish(windows, ends)


def middle_kernel(
    cols,
    slots,
    end_slots,
    turn,
    edge_turn,
    main,
    edge,
    edge_base,
    whole,
    out,
    base,
    buf,
    sems,
    end_buf,
    end_sems,
):
    block = main.shape[3]
    count = len(slots)
    windows = windows_of(each(main, count), slots, base, turn, out, buf, sems, cols, block)
    ends = ends_of(
        each(edge, count),
        end_slots,
        edge_base,
        turn,
        edge_turn,
        out,
        end_buf,
        end_sems,
        cols,
        block,
    )
    finish(windows, ends)


def end_kernel(cols, slots, turn, edge_turn, edge, base, whole, out, buf, sems):
    block = edge.shape[3]
    edges = each(edge, len(slots))
    finish((), ends_of(edges, slots, base, turn, edge_turn, out, buf, sems, cols, block))


def swapped(block, bit):
    facets = lax.axis_size("facet")
    return lax.ppermute(block, "facet", [(i, i ^ bit) for i in range(facets)])


def shifted(block, distance):
    count = lax.axis_size("col")
    return lax.ppermute(block, "col", [(i, (i + distance) % count) for i in range(count)])


def added(kept, received):
    return (kept.astype(F32) + received.astype(F32)).astype(BF16)


def reduced(kept, sent, facets):
    received = swapped(sent, 1)
    bit = 2
    while bit < facets:
        blocks = added(kept, received)
        kept, sent = blocks[:, 0::2], blocks[:, 1::2]
        received = swapped(sent, bit)
        bit *= 2
    return kept, received


def gathered(blocks, facets):
    bit = facets // 2
    while bit > 2:
        received = swapped(blocks, bit)
        shape = (blocks.shape[0], -1) + blocks.shape[2:]
        blocks = jnp.stack([blocks, received], axis=2).reshape(shape)
        bit //= 2
    received = swapped(blocks, bit)
    if blocks.shape[1] == 1:
        return received
    shape = (blocks.shape[0], -1) + blocks.shape[2:]
    return jnp.stack([blocks, received], axis=2).reshape(shape)[:, 1:]


def params(mib):
    return pltpu.CompilerParams(vmem_limit_bytes=mib * 1024 * 1024)


def computed(facet_spectra, facet_offsets, column_index, subgrid_offsets, weights):
    cols = facet_spectra.shape[0]
    shard = facet_spectra.shape[4]
    facets = lax.axis_size("facet")
    length = shard * lax.axis_size("col")
    block = XM // facets
    facet_spectra, facet_offsets, column_index, places = (
        pltpu.with_memory_space_constraint(array, pltpu.HBM)
        for array in (facet_spectra, facet_offsets, column_index, subgrid_offsets.T)
    )

    pieces = jax.ShapeDtypeStruct((2, facets // 2, cols, block, LANES), BF16)
    tile_pair = pltpu.VMEM((cols, 2, 2, XM, LANES), BF16)
    pair_sems = pltpu.SemaphoreType.DMA((cols, 2, facets))
    whole_scalars = [
        pltpu.SMEM(facet_offsets.shape, jnp.int32),
        pltpu.SMEM(column_index.shape, jnp.int32),
    ]
    edge_send, edge_turn = pl.pallas_call(
        functools.partial(edge_kernel, cols, facets, length),
        out_shape=(pieces, jax.ShapeDtypeStruct((16, LANES), F32)),
        in_specs=[HBM, HBM, HBM],
        out_specs=(VMEM, VMEM),
        scratch_shapes=[tile_pair, pair_sems, *whole_scalars, pltpu.SemaphoreType.DMA((2,))],
        compiler_params=params(12),
        name="edge",
    )(facet_offsets, column_index, facet_spectra)
    edge_keep, turn = pl.pallas_call(
        functools.partial(hold_kernel, cols, facets, length),
        out_shape=(pieces, jax.ShapeDtypeStruct((32, LANES), F32)),
        in_specs=[HBM, HBM, HBM, HBM, VMEM],
        out_specs=(VMEM, VMEM),
        scratch_shapes=[
            tile_pair,
            pair_sems,
            *whole_scalars,
            pltpu.SMEM(places.shape, jnp.int32),
            pltpu.SemaphoreType.DMA((3,)),
        ],
        compiler_params=params(12),
        name="hold",
    )(facet_offsets, column_index, places, facet_spectra, edge_turn)
    pair = reduced(edge_keep, edge_send, facets)
    edges = added(*pair)

    main_send, main_keep = pl.pallas_call(
        functools.partial(main_kernel, cols, facets),
        out_shape=(pieces, pieces),
        in_specs=[HBM, VMEM, VMEM],
        out_specs=(VMEM, VMEM),
        scratch_shapes=[tile_pair, pair_sems],
        compiler_params=params(12),
        name="main",
    )(facet_spectra, turn, edge_turn)
    main_kept, main_received = reduced(main_keep, main_send, facets)
    from_prev = shifted(edges[1], 1)
    from_next = shifted(edges[0], -1)

    table = pl.pallas_call(
        functools.partial(table_kernel, facets),
        out_shape=jax.ShapeDtypeStruct((2 * WM, 2 * XM), BF16),
        in_specs=[VMEM],
        out_specs=VMEM,
        compiler_params=params(12),
        name="table",
    )(edge_turn)
    shape = jax.ShapeDtypeStruct((cols, 1, 2, XM, shard), BF16)
    updates = pl.pallas_call(
        zero_kernel,
        out_shape=shape,
        in_specs=[VMEM],
        out_specs=HBM,
        scratch_shapes=[
            pltpu.VMEM((LANES, shard), BF16),
            pltpu.SemaphoreType.DMA((cols, 2, XM // LANES)),
        ],
        compiler_params=params(12),
        name="zero",
    )(turn)

    edge = jax.ShapeDtypeStruct((1, cols, block, LANES), BF16)
    grid_shape = jax.ShapeDtypeStruct((cols, 1, 2, block, XM), BF16)
    held, back, to_prev, to_next = pl.pallas_call(
        functools.partial(subgrid_kernel, cols, shard),
        out_shape=(
            grid_shape,
            jax.ShapeDtypeStruct((2, 1, cols, block, LANES), BF16),
            edge,
            edge,
        ),
        in_specs=[VMEM] * 7,
        out_specs=(VMEM, VMEM, VMEM, VMEM),
        scratch_shapes=[
            pltpu.VMEM((cols * block, 2 * WM), BF16),
            pltpu.VMEM((cols * block, 2 * XM), BF16),
        ],
        compiler_params=params(12),
        name="subgrid",
    )(turn, main_kept, main_received, from_prev, from_next, table, weights)

    came_prev = shifted(to_next, 1)
    came_next = shifted(to_prev, -1)
    near = swapped(back, 1)
    rest = gathered(back, facets)
    far = swapped(rest, 1)
    came = jnp.stack([came_prev, came_next])
    near_edge = swapped(came, 1)
    rest_edge = gathered(came, facets)
    far_edge = swapped(rest_edge, 1)
    evens = tuple(range(2, facets, 2))
    odds = tuple(range(3, facets, 2))

    def tiles_for(count):
        return [
            pltpu.VMEM((cols, 2, 2, count, block, LANES), BF16),
            pltpu.SemaphoreType.DMA((cols, 2, count)),
        ]

    base = jax.ShapeDtypeStruct((2, len(evens), cols, block, LANES), F32)
    single = jax.ShapeDtypeStruct((2, 1, cols, block, LANES), F32)
    updates, grids, near_base = pl.pallas_call(
        functools.partial(early_kernel, cols),
        out_shape=(shape, grid_shape, single),
        in_specs=[VMEM] * 6 + [HBM],
        out_specs=(HBM, HBM, VMEM),
        scratch_shapes=[
            pltpu.VMEM(single.shape, F32),
            *tiles_for(2),
            *tiles_for(1),
            pltpu.SemaphoreType.DMA(()),
        ],
        input_output_aliases={6: 0},
        compiler_params=params(12),
        name="early",
    )(turn, edge_turn, back, near, came, held, updates)
    updates, rest_base = pl.pallas_call(
        functools.partial(window_kernel, cols, evens),
        out_shape=(shape, base),
        in_specs=[VMEM] * 5 + [HBM],
        out_specs=(HBM, VMEM),
        scratch_shapes=[*tiles_for(len(evens)), *tiles_for(1)],
        input_output_aliases={5: 0},
        compiler_params=params(12),
        name="window",
    )(turn, edge_turn, rest, near_edge, near_base, updates)
    updates, far_base = pl.pallas_call(
        functools.partial(middle_kernel, cols, odds, evens),
        out_shape=(shape, base),
        in_specs=[VMEM] * 5 + [HBM],
        out_specs=(HBM, VMEM),
        scratch_shapes=tiles_for(len(evens)) * 2,
        input_output_aliases={5: 0},
        compiler_params=params(12),
        name="middle",
    )(turn, edge_turn, far, rest_edge, rest_base, updates)
    updates = pl.pallas_call(
        functools.partial(end_kernel, cols, odds),
        out_shape=shape,
        in_specs=[VMEM] * 4 + [HBM],
        out_specs=HBM,
        scratch_shapes=tiles_for(len(odds)),
        input_output_aliases={4: 0},
        compiler_params=params(12),
        name="end",
    )(turn, edge_turn, far_edge, far_base, updates)
    return grids, updates


def solution(mesh):
    in_specs = (
        P(None, "facet", None, None, "col"),
        P("facet", None),
        P(),
        P(None, "col"),
        P(None, "col", "facet", None),
    )
    out_specs = (P(None, "col", None, "facet", None), P(None, "facet", None, None, "col"))
    return jax.shard_map(
        computed, mesh=mesh, in_specs=in_specs, out_specs=out_specs, check_vma=False
    )
```

```python
import functools
import math

import jax
import jax.numpy as jnp
from jax import lax
from jax.experimental import pallas as pl
from jax.experimental.pallas import tpu as pltpu
from jax.sharding import PartitionSpec as P


IMAGE = 65536
XM = 512
WM = 128
XA = 448
LANES = 128
HALF = WM // 2

TAU = 2.0 * math.pi
BF16 = jnp.bfloat16
F32 = jnp.float32

VMEM = pl.BlockSpec(memory_space=pltpu.VMEM)
SMEM = pl.BlockSpec(memory_space=pltpu.SMEM)
HBM = pl.BlockSpec(memory_space=pltpu.HBM)


def remainder(value, modulus):
    if modulus & (modulus - 1) == 0:
        return value & (modulus - 1)
    return lax.rem(value, jnp.int32(modulus))


def modular(first, second, image):
    upper = second // 256
    lower = remainder(second, 256)
    return remainder(remainder(first * upper, image // 256) * 256 + first * lower, image)


def place_of(subgrid_offset, here, shard, length):
    start = subgrid_offset // (IMAGE // length) - here * shard - HALF + LANES
    return lax.div(start, jnp.int32(LANES)) - 1, remainder(start, LANES)


def lanes_of(shape):
    return lax.broadcasted_iota(jnp.int32, shape, len(shape) - 1)


def turns_of(turn, index, firsts, second, length):
    rows = lax.broadcasted_iota(jnp.int32, (8, LANES), 0)
    first = jnp.zeros((8, LANES), F32)
    for c, value in enumerate(firsts):
        first = jnp.where(rows == c, value.astype(F32), first)
    steps = remainder(index * second, length).astype(F32)
    angle = TAU * (first / IMAGE + steps / length)
    turn[0:8, :] = jnp.cos(angle)
    turn[8:16, :] = jnp.sin(angle)


def firsts_of(cols, offsets, column):
    return [modular(column[c] * XA, offsets[0, 0], IMAGE) for c in range(cols)]


def rows_of(facet, s, block):
    return pl.ds(pl.multiple_of((facet ^ s) * block, block), block)


def fetched(spectra, buf, sems, c, s, rows, places):
    copies = []
    for slot, at in enumerate(places):
        copy = pltpu.make_async_copy(
            spectra.at[c, 0, :, rows, pl.ds(at, LANES)],
            buf.at[c, slot, :, rows, :],
            sems.at[c, slot, s],
        )
        copy.start()
        copies.append(copy)
    return copies


def turned(parts, cosine, sine):
    return parts[0] * cosine + parts[1] * sine, parts[1] * cosine - parts[0] * sine


def places_of(turn, cols):
    tiles = [jnp.min(turn[16 + c : 17 + c, :]).astype(jnp.int32) for c in range(cols)]
    lanes = [jnp.max(turn[24 + c : 25 + c, :]).astype(jnp.int32) for c in range(cols)]
    return tiles, lanes


def edges_of(target, buf, copies, turn, order, cols, block, facet):
    left = lanes_of((1, LANES)) < HALF
    for c in range(cols):
        cosine = turn[c : c + 1, :]
        sine = turn[8 + c : 9 + c, :]
        for i, s in enumerate(order):
            for copy in copies[c, s]:
                copy.wait()
            rows = rows_of(facet, s, block)
            parts = [
                jnp.where(
                    left,
                    buf[c, 0, part, rows, :].astype(F32),
                    buf[c, 1, part, rows, :].astype(F32),
                )
                for part in range(2)
            ]
            real, imag = turned(parts, cosine, sine)
            low = jnp.where(left, real, pltpu.roll(imag, HALF, 1))
            high = jnp.where(left, pltpu.roll(real, HALF, 1), imag)
            target[0, i, c] = low.astype(BF16)
            target[1, i, c] = high.astype(BF16)


def edge_kernel(
    cols, facets, length, offsets, column, spectra, send, turn, buf, sems, own, held, small
):
    shard = spectra.shape[4]
    block = XM // facets
    here = lax.axis_index("col")
    facet = lax.axis_index("facet")
    scalars = [
        pltpu.make_async_copy(offsets, own, small.at[0]),
        pltpu.make_async_copy(column, held, small.at[1]),
    ]
    for copy in scalars:
        copy.start()
    copies = {}
    order = range(3, facets, 2)
    for c in range(cols):
        for s in order:
            rows = rows_of(facet, s, block)
            copies[c, s] = fetched(spectra, buf, sems, c, s, rows, (0, shard - LANES))
    for copy in scalars:
        copy.wait()
    lanes = lanes_of((8, LANES))
    index = here * shard + lanes + jnp.where(lanes < HALF, 0, shard - LANES)
    turns_of(turn, index, firsts_of(cols, own, held), own[0, 1], length)
    edges_of(send, buf, copies, turn, order, cols, block, facet)


def hold_kernel(
    cols,
    facets,
    length,
    offsets,
    column,
    subgrid,
    spectra,
    edge_turn,
    keep,
    turn,
    buf,
    sems,
    own,
    held,
    spots,
    small,
):
    shard = spectra.shape[4]
    block = XM // facets
    here = lax.axis_index("col")
    facet = lax.axis_index("facet")
    scalars = [
        pltpu.make_async_copy(offsets, own, small.at[0]),
        pltpu.make_async_copy(column, held, small.at[1]),
        pltpu.make_async_copy(subgrid, spots, small.at[2]),
    ]
    for copy in scalars:
        copy.start()
    copies = {}
    order = range(2, facets, 2)
    for c in range(cols):
        for s in order:
            rows = rows_of(facet, s, block)
            copies[c, s] = fetched(spectra, buf, sems, c, s, rows, (0, shard - LANES))
    for copy in scalars:
        copy.wait()
    lanes = lanes_of((8, LANES))
    rows = lax.broadcasted_iota(jnp.int32, (8, LANES), 0)
    tile_at = jnp.zeros((8, LANES), jnp.int32)
    begins = jnp.zeros((8, LANES), jnp.int32)
    for c in range(cols):
        tile, lane = place_of(spots[0, c], here, shard, length)
        tile_at = jnp.where(rows == c, jnp.where(lanes >= lane, tile, tile + 1), tile_at)
        begins = jnp.where(rows == c, lane, begins)
    index = remainder(here * shard + lanes + tile_at * LANES + length, length)
    turns_of(turn, index, firsts_of(cols, own, held), own[0, 1], length)
    turn[16:24, :] = tile_at.astype(F32)
    turn[24:32, :] = begins.astype(F32)
    edges_of(keep, buf, copies, edge_turn, order, cols, block, facet)


def main_kernel(
    cols,
    facets,
    spectra,
    turn,
    edge_turn,
    send,
    keep,
    near_send,
    near_keep,
    buf,
    sems,
    edge_buf,
    edge_sems,
):
    shard = spectra.shape[4]
    tiles = shard // LANES
    block = XM // facets
    facet = lax.axis_index("facet")
    near = {}
    for c in range(cols):
        for s in range(2):
            rows = rows_of(facet, s, block)
            near[c, s] = fetched(spectra, edge_buf, edge_sems, c, s, rows, (0, shard - LANES))
    copies = {}
    first_tiles, _ = places_of(turn, cols)
    for c in range(cols):
        tile = first_tiles[c]
        low = pl.multiple_of(jnp.maximum(tile, 0) * LANES, LANES)
        high = pl.multiple_of(jnp.minimum(tile + 1, tiles - 1) * LANES, LANES)
        for s in range(facets):
            rows = rows_of(facet, s, block)
            copies[c, s] = fetched(spectra, buf, sems, c, s, rows, (low, high))
    edges_of(near_send, edge_buf, near, edge_turn, (1,), cols, block, facet)
    edges_of(near_keep, edge_buf, near, edge_turn, (0,), cols, block, facet)
    zero = jnp.zeros((1, LANES), F32)
    for c in range(cols):
        tile_at = turn[16 + c : 17 + c, :]
        is_low = lanes_of((1, LANES)).astype(F32) >= turn[24 + c : 25 + c, :]
        inside = jnp.logical_and(tile_at >= 0, tile_at <= tiles - 1)
        cosine = jnp.where(inside, turn[c : c + 1, :], zero)
        sine = jnp.where(inside, turn[8 + c : 9 + c, :], zero)
        for s in range(facets):
            for copy in copies[c, s]:
                copy.wait()
            rows = rows_of(facet, s, block)
            target = send if s % 2 else keep
            parts = [
                jnp.where(
                    is_low,
                    buf[c, 0, part, rows, :].astype(F32),
                    buf[c, 1, part, rows, :].astype(F32),
                )
                for part in range(2)
            ]
            real, imag = turned(parts, cosine, sine)
            target[0, s // 2, c] = real.astype(BF16)
            target[1, s // 2, c] = imag.astype(BF16)


def table_kernel(facets, after, table):
    del after
    place = lax.broadcasted_iota(jnp.int32, (WM, LANES), 0)
    cell = lanes_of((WM, LANES))
    angle = TAU * remainder((place - HALF) * cell + HALF * XM, XM).astype(F32) / XM
    relative = (place.astype(F32) + 0.5 - WM / 2.0) / (WM / 2.0)
    taper = (0.3 + 0.7 * (1.0 - relative * relative)) / jnp.sqrt(
        jnp.full((1, LANES), WM * facets, F32)
    )
    cosine = taper * jnp.cos(angle)
    sine = taper * jnp.sin(angle)
    for tile in range(XM // LANES):
        first = tile * LANES - XM // 2
        quarter = remainder((place - HALF) * (first * 4 // XM) + HALF * 4, 4)
        odd = remainder(quarter, 2) == 1
        real = jnp.where(odd, sine, cosine)
        imag = jnp.where(odd, cosine, sine)
        real = jnp.where(jnp.logical_or(quarter == 1, quarter == 2), -real, real).astype(BF16)
        imag = jnp.where(quarter >= 2, -imag, imag)
        span = slice(tile * LANES, (tile + 1) * LANES)
        other = slice(XM + tile * LANES, XM + (tile + 1) * LANES)
        table[:WM, span] = real
        table[WM:, other] = real
        table[:WM, other] = imag.astype(BF16)
        table[WM:, span] = (-imag).astype(BF16)


def zero_kernel(after, out, buf, sems):
    del after
    cols, _, _, height, _ = out.shape
    block = buf.shape[0]
    buf[...] = jnp.zeros(buf.shape, BF16)
    copies = []
    for c in range(cols):
        for part in range(2):
            for i in range(height // block):
                rows = pl.ds(i * block, block)
                copies.append(
                    pltpu.make_async_copy(buf, out.at[c, 0, part, rows, :], sems.at[c, part, i])
                )
    for copy in copies:
        copy.start()
    for copy in copies:
        copy.wait()


def subgrid_kernel(
    cols,
    shard,
    turn,
    kept,
    received,
    from_prev,
    from_next,
    table,
    weights,
    grids,
    back,
    to_prev,
    to_next,
    stack,
    scaled,
):
    tiles = shard // LANES
    block = kept.shape[3]
    zero = jnp.zeros((1, LANES), F32)
    _, begins = places_of(turn, cols)
    for c in range(cols):
        held = turn[16 + c : 17 + c, :]
        low = held < 0
        high = held > tiles - 1
        prev = from_prev[0, c].astype(F32)
        nxt = from_next[0, c].astype(F32)
        shift = remainder(LANES - begins[c], LANES)
        real = kept[0, 0, c].astype(F32) + received[0, 0, c].astype(F32)
        real = real + jnp.where(low, pltpu.roll(prev, HALF, 1), jnp.where(high, nxt, zero))
        imag = kept[1, 0, c].astype(F32) + received[1, 0, c].astype(F32)
        imag = imag + jnp.where(low, prev, jnp.where(high, pltpu.roll(nxt, HALF, 1), zero))
        rows = slice(c * block, (c + 1) * block)
        stack[rows, :WM] = pltpu.roll(real, shift, 1).astype(BF16)
        stack[rows, WM:] = pltpu.roll(imag, shift, 1).astype(BF16)
    for part in range(2):
        span = slice(part * XM, (part + 1) * XM)
        product = jnp.dot(stack[...], table[:, span], preferred_element_type=F32)
        rounded = product.astype(BF16)
        for c in range(cols):
            rows = slice(c * block, (c + 1) * block)
            piece = rounded[rows]
            grids[c, 0, part] = piece
            scaled[rows, span] = (piece.astype(F32) * weights[c, 0].astype(F32)).astype(BF16)
    result = lax.dot_general(
        scaled[...],
        table[...],
        (((1,), (1,)), ((), ())),
        preferred_element_type=F32,
    )
    for c in range(cols):
        held = turn[16 + c : 17 + c, :]
        rows = slice(c * block, (c + 1) * block)
        low = held < 0
        high = held > tiles - 1
        real = pltpu.roll(result[rows, :WM], begins[c], 1)
        imag = pltpu.roll(result[rows, WM:], begins[c], 1)
        back[0, 0, c] = real.astype(BF16)
        back[1, 0, c] = imag.astype(BF16)
        real_low = jnp.where(low, real, zero)
        imag_low = jnp.where(low, imag, zero)
        real_high = jnp.where(high, real, zero)
        imag_high = jnp.where(high, imag, zero)
        to_prev[0, c] = (pltpu.roll(real_low, HALF, 1) + imag_low).astype(BF16)
        to_next[0, c] = (real_high + pltpu.roll(imag_high, HALF, 1)).astype(BF16)


def window_of(main, i, c, turn):
    cosine = turn[c : c + 1, :]
    sine = turn[8 + c : 9 + c, :]
    real = main[0, i, c].astype(F32)
    imag = main[1, i, c].astype(F32)
    return real * cosine - imag * sine, imag * cosine + real * sine


def windows_of(mains, slots, base, turn, out, buf, sems, cols, block):
    tiles = out.shape[4] // LANES
    facet = lax.axis_index("facet")
    zero = jnp.zeros((1, LANES), F32)
    first_tiles, _ = places_of(turn, cols)
    copies = []
    for c in range(cols):
        is_low = lanes_of((1, LANES)).astype(F32) >= turn[24 + c : 25 + c, :]
        for i, slot in enumerate(slots):
            rows = rows_of(facet, slot, block)
            main, at_main = mains[i]
            values = window_of(main, at_main, c, turn)
            for part in range(2):
                base[part, i, c] = values[part]
                buf[c, 0, part, i] = jnp.where(is_low, values[part], zero).astype(BF16)
                buf[c, 1, part, i] = jnp.where(is_low, zero, values[part]).astype(BF16)
            for side in range(2):
                which = first_tiles[c] + side
                at = pl.multiple_of(jnp.clip(which, 0, tiles - 1) * LANES, LANES)
                copy = pltpu.make_async_copy(
                    buf.at[c, side, :, i],
                    out.at[c, 0, :, rows, pl.ds(at, LANES)],
                    sems.at[c, side, i],
                )
                inside = jnp.logical_and(which > 0, which < tiles - 1)
                pl.when(inside)(copy.start)
                copies.append((inside, copy))
    return copies


def ends_of(edges, slots, base, turn, edge_turn, out, buf, sems, cols, block):
    shard = out.shape[4]
    tiles = shard // LANES
    facet = lax.axis_index("facet")
    left = lanes_of((1, LANES)) < HALF
    zero = jnp.zeros((1, LANES), F32)
    copies = []
    for c in range(cols):
        edge_cosine = edge_turn[c : c + 1, :]
        edge_sine = edge_turn[8 + c : 9 + c, :]
        tile_at = turn[16 + c : 17 + c, :]
        in_first = tile_at == 0
        in_last = tile_at == tiles - 1
        for i, slot in enumerate(slots):
            rows = rows_of(facet, slot, block)
            edge, at_edge = edges[i]
            prev = edge[0, at_edge, c].astype(F32)
            nxt = edge[1, at_edge, c].astype(F32)
            real = jnp.where(left, prev, pltpu.roll(nxt, HALF, 1))
            imag = jnp.where(left, pltpu.roll(prev, HALF, 1), nxt)
            ends = (
                real * edge_cosine - imag * edge_sine,
                imag * edge_cosine + real * edge_sine,
            )
            for part in range(2):
                value = base[part, i, c]
                end = ends[part]
                buf[c, 0, part, i] = (
                    jnp.where(left, end, zero) + jnp.where(in_first, value, zero)
                ).astype(BF16)
                buf[c, 1, part, i] = (
                    jnp.where(left, zero, end) + jnp.where(in_last, value, zero)
                ).astype(BF16)
            for side, start in enumerate((0, shard - LANES)):
                copy = pltpu.make_async_copy(
                    buf.at[c, side, :, i],
                    out.at[c, 0, :, rows, pl.ds(start, LANES)],
                    sems.at[c, side, i],
                )
                copy.start()
                copies.append(copy)
    return copies


def finish(windows, ends):
    for inside, copy in windows:
        pl.when(inside)(copy.wait)
    for copy in ends:
        copy.wait()


def each(array, count):
    return [(array, i) for i in range(count)]


def early_kernel(
    cols,
    turn,
    edge_turn,
    own,
    near,
    own_edge,
    held,
    whole,
    out,
    grids,
    near_base,
    base,
    buf,
    sems,
    end_buf,
    end_sems,
    grid_sem,
):
    block = own.shape[3]
    store = pltpu.make_async_copy(held, grids, grid_sem)
    store.start()
    first = buf.at[:, :, :, 0:1], sems.at[:, :, 0:1]
    second = buf.at[:, :, :, 1:2], sems.at[:, :, 1:2]
    windows = windows_of(((own, 0),), (0,), base, turn, out, *first, cols, block)
    ends = ends_of(((own_edge, 0),), (0,), base, turn, edge_turn, out, end_buf, end_sems, cols, block)
    windows += windows_of(((near, 0),), (1,), near_base, turn, out, *second, cols, block)
    finish(windows, (*ends, store))


def window_kernel(
    cols,
    slots,
    turn,
    edge_turn,
    main,
    near_edge,
    near_base,
    whole,
    out,
    base,
    buf,
    sems,
    end_buf,
    end_sems,
):
    block = main.shape[3]
    mains = each(main, len(slots))
    windows = windows_of(mains, slots, base, turn, out, buf, sems, cols, block)
    edges = ((near_edge, 0),)
    ends = ends_of(edges, (1,), near_base, turn, edge_turn, out, end_buf, end_sems, cols, block)
    finish(windows, ends)


def middle_kernel(
    cols,
    slots,
    end_slots,
    turn,
    edge_turn,
    main,
    edge,
    edge_base,
    whole,
    out,
    base,
    buf,
    sems,
    end_buf,
    end_sems,
):
    block = main.shape[3]
    count = len(slots)
    windows = windows_of(each(main, count), slots, base, turn, out, buf, sems, cols, block)
    ends = ends_of(
        each(edge, count),
        end_slots,
        edge_base,
        turn,
        edge_turn,
        out,
        end_buf,
        end_sems,
        cols,
        block,
    )
    finish(windows, ends)


def end_kernel(cols, slots, turn, edge_turn, edge, base, whole, out, buf, sems):
    block = edge.shape[3]
    edges = each(edge, len(slots))
    finish((), ends_of(edges, slots, base, turn, edge_turn, out, buf, sems, cols, block))


def swapped(block, bit):
    facets = lax.axis_size("facet")
    return lax.ppermute(block, "facet", [(i, i ^ bit) for i in range(facets)])


def shifted(block, distance):
    count = lax.axis_size("col")
    return lax.ppermute(block, "col", [(i, (i + distance) % count) for i in range(count)])


def added(kept, received):
    return (kept.astype(F32) + received.astype(F32)).astype(BF16)


def reduced(kept, sent, facets):
    received = swapped(sent, 1)
    bit = 2
    while bit < facets:
        blocks = added(kept, received)
        kept, sent = blocks[:, 0::2], blocks[:, 1::2]
        received = swapped(sent, bit)
        bit *= 2
    return kept, received


def gathered(blocks, facets):
    bit = facets // 2
    while bit > 2:
        received = swapped(blocks, bit)
        shape = (blocks.shape[0], -1) + blocks.shape[2:]
        blocks = jnp.stack([blocks, received], axis=2).reshape(shape)
        bit //= 2
    received = swapped(blocks, bit)
    if blocks.shape[1] == 1:
        return received
    shape = (blocks.shape[0], -1) + blocks.shape[2:]
    return jnp.stack([blocks, received], axis=2).reshape(shape)[:, 1:]


def params(mib):
    return pltpu.CompilerParams(vmem_limit_bytes=mib * 1024 * 1024)


def computed(facet_spectra, facet_offsets, column_index, subgrid_offsets, weights):
    cols = facet_spectra.shape[0]
    shard = facet_spectra.shape[4]
    facets = lax.axis_size("facet")
    length = shard * lax.axis_size("col")
    block = XM // facets
    facet_spectra, facet_offsets, column_index, places = (
        pltpu.with_memory_space_constraint(array, pltpu.HBM)
        for array in (facet_spectra, facet_offsets, column_index, subgrid_offsets.T)
    )

    pieces = jax.ShapeDtypeStruct((2, facets // 2, cols, block, LANES), BF16)
    fewer = jax.ShapeDtypeStruct((2, facets // 2 - 1, cols, block, LANES), BF16)
    single = jax.ShapeDtypeStruct((2, 1, cols, block, LANES), BF16)
    tile_pair = pltpu.VMEM((cols, 2, 2, XM, LANES), BF16)
    pair_sems = pltpu.SemaphoreType.DMA((cols, 2, facets))
    whole_scalars = [
        pltpu.SMEM(facet_offsets.shape, jnp.int32),
        pltpu.SMEM(column_index.shape, jnp.int32),
    ]
    edge_send, edge_turn = pl.pallas_call(
        functools.partial(edge_kernel, cols, facets, length),
        out_shape=(fewer, jax.ShapeDtypeStruct((16, LANES), F32)),
        in_specs=[HBM, HBM, HBM],
        out_specs=(VMEM, VMEM),
        scratch_shapes=[tile_pair, pair_sems, *whole_scalars, pltpu.SemaphoreType.DMA((2,))],
        compiler_params=params(12),
        name="edge",
    )(facet_offsets, column_index, facet_spectra)
    edge_keep, turn = pl.pallas_call(
        functools.partial(hold_kernel, cols, facets, length),
        out_shape=(fewer, jax.ShapeDtypeStruct((32, LANES), F32)),
        in_specs=[HBM, HBM, HBM, HBM, VMEM],
        out_specs=(VMEM, VMEM),
        scratch_shapes=[
            tile_pair,
            pair_sems,
            *whole_scalars,
            pltpu.SMEM(places.shape, jnp.int32),
            pltpu.SemaphoreType.DMA((3,)),
        ],
        compiler_params=params(12),
        name="hold",
    )(facet_offsets, column_index, places, facet_spectra, edge_turn)
    rest = added(edge_keep, swapped(edge_send, 1))
    came = []
    bit = 2
    while bit < facets:
        received = swapped(rest[:, 0::2], bit)
        came.append(received[:, :1])
        if rest.shape[1] > 1:
            rest = added(rest[:, 1::2], received[:, 1:])
        bit *= 2

    main_send, main_keep, near_send, near_keep = pl.pallas_call(
        functools.partial(main_kernel, cols, facets),
        out_shape=(pieces, pieces, single, single),
        in_specs=[HBM, VMEM, VMEM],
        out_specs=(VMEM,) * 4,
        scratch_shapes=[tile_pair, pair_sems, tile_pair, pair_sems],
        compiler_params=params(12),
        name="main",
    )(facet_spectra, turn, edge_turn)
    came.append(swapped(near_send, 1))
    total = near_keep.astype(F32)
    for block_sum in came:
        total = total + block_sum.astype(F32)
    edges = total.astype(BF16)
    main_kept, main_received = reduced(main_keep, main_send, facets)
    from_prev = shifted(edges[1], 1)
    from_next = shifted(edges[0], -1)

    table = pl.pallas_call(
        functools.partial(table_kernel, facets),
        out_shape=jax.ShapeDtypeStruct((2 * WM, 2 * XM), BF16),
        in_specs=[VMEM],
        out_specs=VMEM,
        compiler_params=params(12),
        name="table",
    )(edge_turn)
    shape = jax.ShapeDtypeStruct((cols, 1, 2, XM, shard), BF16)
    updates = pl.pallas_call(
        zero_kernel,
        out_shape=shape,
        in_specs=[VMEM],
        out_specs=HBM,
        scratch_shapes=[
            pltpu.VMEM((LANES, shard), BF16),
            pltpu.SemaphoreType.DMA((cols, 2, XM // LANES)),
        ],
        compiler_params=params(12),
        name="zero",
    )(turn)

    edge = jax.ShapeDtypeStruct((1, cols, block, LANES), BF16)
    grid_shape = jax.ShapeDtypeStruct((cols, 1, 2, block, XM), BF16)
    held, back, to_prev, to_next = pl.pallas_call(
        functools.partial(subgrid_kernel, cols, shard),
        out_shape=(
            grid_shape,
            jax.ShapeDtypeStruct((2, 1, cols, block, LANES), BF16),
            edge,
            edge,
        ),
        in_specs=[VMEM] * 7,
        out_specs=(VMEM, VMEM, VMEM, VMEM),
        scratch_shapes=[
            pltpu.VMEM((cols * block, 2 * WM), BF16),
            pltpu.VMEM((cols * block, 2 * XM), BF16),
        ],
        compiler_params=params(12),
        name="subgrid",
    )(turn, main_kept, main_received, from_prev, from_next, table, weights)

    came_prev = shifted(to_next, 1)
    came_next = shifted(to_prev, -1)
    near = swapped(back, 1)
    far_half = gathered(back, facets)
    far = swapped(far_half, 1)
    own_edge = jnp.stack([came_prev, came_next])
    near_edge = swapped(own_edge, 1)
    rest_edge = gathered(own_edge, facets)
    far_edge = swapped(rest_edge, 1)
    evens = tuple(range(2, facets, 2))
    odds = tuple(range(3, facets, 2))

    def tiles_for(count):
        return [
            pltpu.VMEM((cols, 2, 2, count, block, LANES), BF16),
            pltpu.SemaphoreType.DMA((cols, 2, count)),
        ]

    base = jax.ShapeDtypeStruct((2, len(evens), cols, block, LANES), F32)
    near_shape = jax.ShapeDtypeStruct((2, 1, cols, block, LANES), F32)
    updates, grids, near_base = pl.pallas_call(
        functools.partial(early_kernel, cols),
        out_shape=(shape, grid_shape, near_shape),
        in_specs=[VMEM] * 6 + [HBM],
        out_specs=(HBM, HBM, VMEM),
        scratch_shapes=[
            pltpu.VMEM(near_shape.shape, F32),
            *tiles_for(2),
            *tiles_for(1),
            pltpu.SemaphoreType.DMA(()),
        ],
        input_output_aliases={6: 0},
        compiler_params=params(12),
        name="early",
    )(turn, edge_turn, back, near, own_edge, held, updates)
    updates, rest_base = pl.pallas_call(
        functools.partial(window_kernel, cols, evens),
        out_shape=(shape, base),
        in_specs=[VMEM] * 5 + [HBM],
        out_specs=(HBM, VMEM),
        scratch_shapes=[*tiles_for(len(evens)), *tiles_for(1)],
        input_output_aliases={5: 0},
        compiler_params=params(12),
        name="window",
    )(turn, edge_turn, far_half, near_edge, near_base, updates)
    updates, far_base = pl.pallas_call(
        functools.partial(middle_kernel, cols, odds, evens),
        out_shape=(shape, base),
        in_specs=[VMEM] * 5 + [HBM],
        out_specs=(HBM, VMEM),
        scratch_shapes=tiles_for(len(evens)) * 2,
        input_output_aliases={5: 0},
        compiler_params=params(12),
        name="middle",
    )(turn, edge_turn, far, rest_edge, rest_base, updates)
    updates = pl.pallas_call(
        functools.partial(end_kernel, cols, odds),
        out_shape=shape,
        in_specs=[VMEM] * 4 + [HBM],
        out_specs=HBM,
        scratch_shapes=tiles_for(len(odds)),
        input_output_aliases={4: 0},
        compiler_params=params(12),
        name="end",
    )(turn, edge_turn, far_edge, far_base, updates)
    return grids, updates


def solution(mesh):
    in_specs = (
        P(None, "facet", None, None, "col"),
        P("facet", None),
        P(),
        P(None, "col"),
        P(None, "col", "facet", None),
    )
    out_specs = (P(None, "col", None, "facet", None), P(None, "facet", None, None, "col"))
    return jax.shard_map(
        computed, mesh=mesh, in_specs=in_specs, out_specs=out_specs, check_vma=False
    )
```

```python
import functools
import math

import jax
import jax.numpy as jnp
from jax import lax
from jax.experimental import pallas as pl
from jax.experimental.pallas import tpu as pltpu
from jax.sharding import PartitionSpec as P


IMAGE = 65536
XM = 512
WM = 128
XA = 448
LANES = 128
HALF = WM // 2

TAU = 2.0 * math.pi
BF16 = jnp.bfloat16
F32 = jnp.float32

VMEM = pl.BlockSpec(memory_space=pltpu.VMEM)
SMEM = pl.BlockSpec(memory_space=pltpu.SMEM)
HBM = pl.BlockSpec(memory_space=pltpu.HBM)


def remainder(value, modulus):
    if modulus & (modulus - 1) == 0:
        return value & (modulus - 1)
    return lax.rem(value, jnp.int32(modulus))


def modular(first, second, image):
    upper = second // 256
    lower = remainder(second, 256)
    return remainder(remainder(first * upper, image // 256) * 256 + first * lower, image)


def place_of(subgrid_offset, here, shard, length):
    start = subgrid_offset // (IMAGE // length) - here * shard - HALF + LANES
    return lax.div(start, jnp.int32(LANES)) - 1, remainder(start, LANES)


def lanes_of(shape):
    return lax.broadcasted_iota(jnp.int32, shape, len(shape) - 1)


def turns_of(turn, index, firsts, second, length):
    rows = lax.broadcasted_iota(jnp.int32, (8, LANES), 0)
    first = jnp.zeros((8, LANES), F32)
    for c, value in enumerate(firsts):
        first = jnp.where(rows == c, value.astype(F32), first)
    steps = remainder(index * second, length).astype(F32)
    angle = TAU * (first / IMAGE + steps / length)
    turn[0:8, :] = jnp.cos(angle)
    turn[8:16, :] = jnp.sin(angle)


def firsts_of(cols, offsets, column):
    return [modular(column[c] * XA, offsets[0, 0], IMAGE) for c in range(cols)]


def rows_of(facet, s, block):
    return pl.ds(pl.multiple_of((facet ^ s) * block, block), block)


def fetched(spectra, buf, sems, c, s, rows, places):
    copies = []
    for slot, at in enumerate(places):
        copy = pltpu.make_async_copy(
            spectra.at[c, 0, :, rows, pl.ds(at, LANES)],
            buf.at[c, slot, :, rows, :],
            sems.at[c, slot, s],
        )
        copy.start()
        copies.append(copy)
    return copies


def turned(parts, cosine, sine):
    return parts[0] * cosine + parts[1] * sine, parts[1] * cosine - parts[0] * sine


def places_of(turn, cols):
    tiles = [jnp.min(turn[16 + c : 17 + c, :]).astype(jnp.int32) for c in range(cols)]
    lanes = [jnp.max(turn[24 + c : 25 + c, :]).astype(jnp.int32) for c in range(cols)]
    return tiles, lanes


def edges_of(target, buf, copies, turn, order, cols, block, facet):
    left = lanes_of((1, LANES)) < HALF
    for c in range(cols):
        cosine = turn[c : c + 1, :]
        sine = turn[8 + c : 9 + c, :]
        for i, s in enumerate(order):
            for copy in copies[c, s]:
                copy.wait()
            rows = rows_of(facet, s, block)
            parts = [
                jnp.where(
                    left,
                    buf[c, 0, part, rows, :].astype(F32),
                    buf[c, 1, part, rows, :].astype(F32),
                )
                for part in range(2)
            ]
            real, imag = turned(parts, cosine, sine)
            low = jnp.where(left, real, pltpu.roll(imag, HALF, 1))
            high = jnp.where(left, pltpu.roll(real, HALF, 1), imag)
            target[0, i, c] = low.astype(BF16)
            target[1, i, c] = high.astype(BF16)


def edge_kernel(
    cols, facets, length, offsets, column, spectra, send, turn, buf, sems, own, held, small
):
    shard = spectra.shape[4]
    block = XM // facets
    here = lax.axis_index("col")
    facet = lax.axis_index("facet")
    scalars = [
        pltpu.make_async_copy(offsets, own, small.at[0]),
        pltpu.make_async_copy(column, held, small.at[1]),
    ]
    for copy in scalars:
        copy.start()
    copies = {}
    order = range(3, facets, 2)
    for c in range(cols):
        for s in order:
            rows = rows_of(facet, s, block)
            copies[c, s] = fetched(spectra, buf, sems, c, s, rows, (0, shard - LANES))
    for copy in scalars:
        copy.wait()
    lanes = lanes_of((8, LANES))
    index = here * shard + lanes + jnp.where(lanes < HALF, 0, shard - LANES)
    turns_of(turn, index, firsts_of(cols, own, held), own[0, 1], length)
    edges_of(send, buf, copies, turn, order, cols, block, facet)


def hold_kernel(
    cols,
    facets,
    length,
    offsets,
    column,
    subgrid,
    spectra,
    edge_turn,
    keep,
    turn,
    buf,
    sems,
    own,
    held,
    spots,
    small,
):
    shard = spectra.shape[4]
    block = XM // facets
    here = lax.axis_index("col")
    facet = lax.axis_index("facet")
    scalars = [
        pltpu.make_async_copy(offsets, own, small.at[0]),
        pltpu.make_async_copy(column, held, small.at[1]),
        pltpu.make_async_copy(subgrid, spots, small.at[2]),
    ]
    for copy in scalars:
        copy.start()
    copies = {}
    order = range(2, facets, 2)
    for c in range(cols):
        for s in order:
            rows = rows_of(facet, s, block)
            copies[c, s] = fetched(spectra, buf, sems, c, s, rows, (0, shard - LANES))
    for copy in scalars:
        copy.wait()
    lanes = lanes_of((8, LANES))
    rows = lax.broadcasted_iota(jnp.int32, (8, LANES), 0)
    tile_at = jnp.zeros((8, LANES), jnp.int32)
    begins = jnp.zeros((8, LANES), jnp.int32)
    for c in range(cols):
        tile, lane = place_of(spots[0, c], here, shard, length)
        tile_at = jnp.where(rows == c, jnp.where(lanes >= lane, tile, tile + 1), tile_at)
        begins = jnp.where(rows == c, lane, begins)
    index = remainder(here * shard + lanes + tile_at * LANES + length, length)
    turns_of(turn, index, firsts_of(cols, own, held), own[0, 1], length)
    turn[16:24, :] = tile_at.astype(F32)
    turn[24:32, :] = begins.astype(F32)
    edges_of(keep, buf, copies, edge_turn, order, cols, block, facet)


def main_kernel(
    cols,
    facets,
    spectra,
    turn,
    edge_turn,
    send,
    keep,
    main_send,
    main_keep,
    near_send,
    near_keep,
    buf,
    sems,
    edge_buf,
    edge_sems,
):
    shard = spectra.shape[4]
    tiles = shard // LANES
    block = XM // facets
    facet = lax.axis_index("facet")
    near = {}
    for c in range(cols):
        for s in range(2):
            rows = rows_of(facet, s, block)
            near[c, s] = fetched(spectra, edge_buf, edge_sems, c, s, rows, (0, shard - LANES))
    copies = {}
    first_tiles, _ = places_of(turn, cols)
    for c in range(cols):
        tile = first_tiles[c]
        low = pl.multiple_of(jnp.maximum(tile, 0) * LANES, LANES)
        high = pl.multiple_of(jnp.minimum(tile + 1, tiles - 1) * LANES, LANES)
        for s in range(facets):
            rows = rows_of(facet, s, block)
            copies[c, s] = fetched(spectra, buf, sems, c, s, rows, (low, high))
    edges_of(near_send, edge_buf, near, edge_turn, (1,), cols, block, facet)
    edges_of(near_keep, edge_buf, near, edge_turn, (0,), cols, block, facet)
    zero = jnp.zeros((1, LANES), F32)
    for c in range(cols):
        tile_at = turn[16 + c : 17 + c, :]
        is_low = lanes_of((1, LANES)).astype(F32) >= turn[24 + c : 25 + c, :]
        inside = jnp.logical_and(tile_at >= 0, tile_at <= tiles - 1)
        cosine = jnp.where(inside, turn[c : c + 1, :], zero)
        sine = jnp.where(inside, turn[8 + c : 9 + c, :], zero)
        for s in range(facets):
            for copy in copies[c, s]:
                copy.wait()
            rows = rows_of(facet, s, block)
            if s < 2:
                target, at = (main_send if s else main_keep), 0
            else:
                target, at = (send if s % 2 else keep), s // 2 - 1
            parts = [
                jnp.where(
                    is_low,
                    buf[c, 0, part, rows, :].astype(F32),
                    buf[c, 1, part, rows, :].astype(F32),
                )
                for part in range(2)
            ]
            real, imag = turned(parts, cosine, sine)
            target[0, at, c] = real.astype(BF16)
            target[1, at, c] = imag.astype(BF16)


def table_kernel(facets, after, table):
    del after
    place = lax.broadcasted_iota(jnp.int32, (WM, LANES), 0)
    cell = lanes_of((WM, LANES))
    angle = TAU * remainder((place - HALF) * cell + HALF * XM, XM).astype(F32) / XM
    relative = (place.astype(F32) + 0.5 - WM / 2.0) / (WM / 2.0)
    taper = (0.3 + 0.7 * (1.0 - relative * relative)) / jnp.sqrt(
        jnp.full((1, LANES), WM * facets, F32)
    )
    cosine = taper * jnp.cos(angle)
    sine = taper * jnp.sin(angle)
    for tile in range(XM // LANES):
        first = tile * LANES - XM // 2
        quarter = remainder((place - HALF) * (first * 4 // XM) + HALF * 4, 4)
        odd = remainder(quarter, 2) == 1
        real = jnp.where(odd, sine, cosine)
        imag = jnp.where(odd, cosine, sine)
        real = jnp.where(jnp.logical_or(quarter == 1, quarter == 2), -real, real).astype(BF16)
        imag = jnp.where(quarter >= 2, -imag, imag)
        span = slice(tile * LANES, (tile + 1) * LANES)
        other = slice(XM + tile * LANES, XM + (tile + 1) * LANES)
        table[:WM, span] = real
        table[WM:, other] = real
        table[:WM, other] = imag.astype(BF16)
        table[WM:, span] = (-imag).astype(BF16)


def zero_kernel(after, out, buf, sems):
    del after
    cols, _, _, height, _ = out.shape
    block, width = buf.shape
    buf[...] = jnp.zeros(buf.shape, BF16)
    copies = []
    for c in range(cols):
        for part in range(2):
            for i in range(height // block):
                place = out.at[c, 0, part, pl.ds(i * block, block), pl.ds(LANES, width)]
                copies.append(pltpu.make_async_copy(buf, place, sems.at[c, part, i]))
    for copy in copies:
        copy.start()
    for copy in copies:
        copy.wait()


def subgrid_kernel(
    cols,
    shard,
    turn,
    kept,
    near,
    received,
    from_prev,
    from_next,
    table,
    weights,
    grids,
    back,
    to_prev,
    to_next,
    stack,
    scaled,
):
    tiles = shard // LANES
    block = kept.shape[3]
    zero = jnp.zeros((1, LANES), F32)
    _, begins = places_of(turn, cols)
    for c in range(cols):
        held = turn[16 + c : 17 + c, :]
        low = held < 0
        high = held > tiles - 1
        prev = from_prev[0, c].astype(F32)
        nxt = from_next[0, c].astype(F32)
        shift = remainder(LANES - begins[c], LANES)
        real, imag = (
            kept[part, 0, c].astype(F32)
            + near[part, 0, c].astype(F32)
            + received[part, 0, c].astype(F32)
            for part in range(2)
        )
        real = real + jnp.where(low, pltpu.roll(prev, HALF, 1), jnp.where(high, nxt, zero))
        imag = imag + jnp.where(low, prev, jnp.where(high, pltpu.roll(nxt, HALF, 1), zero))
        rows = slice(c * block, (c + 1) * block)
        stack[rows, :WM] = pltpu.roll(real, shift, 1).astype(BF16)
        stack[rows, WM:] = pltpu.roll(imag, shift, 1).astype(BF16)
    for part in range(2):
        span = slice(part * XM, (part + 1) * XM)
        product = jnp.dot(stack[...], table[:, span], preferred_element_type=F32)
        rounded = product.astype(BF16)
        for c in range(cols):
            rows = slice(c * block, (c + 1) * block)
            piece = rounded[rows]
            grids[c, 0, part] = piece
            scaled[rows, span] = (piece.astype(F32) * weights[c, 0].astype(F32)).astype(BF16)
    result = lax.dot_general(
        scaled[...],
        table[...],
        (((1,), (1,)), ((), ())),
        preferred_element_type=F32,
    )
    for c in range(cols):
        held = turn[16 + c : 17 + c, :]
        rows = slice(c * block, (c + 1) * block)
        low = held < 0
        high = held > tiles - 1
        real = pltpu.roll(result[rows, :WM], begins[c], 1)
        imag = pltpu.roll(result[rows, WM:], begins[c], 1)
        back[0, 0, c] = real.astype(BF16)
        back[1, 0, c] = imag.astype(BF16)
        real_low = jnp.where(low, real, zero)
        imag_low = jnp.where(low, imag, zero)
        real_high = jnp.where(high, real, zero)
        imag_high = jnp.where(high, imag, zero)
        to_prev[0, c] = (pltpu.roll(real_low, HALF, 1) + imag_low).astype(BF16)
        to_next[0, c] = (real_high + pltpu.roll(imag_high, HALF, 1)).astype(BF16)


def window_of(main, i, c, turn):
    cosine = turn[c : c + 1, :]
    sine = turn[8 + c : 9 + c, :]
    real = main[0, i, c].astype(F32)
    imag = main[1, i, c].astype(F32)
    return real * cosine - imag * sine, imag * cosine + real * sine


def windows_of(mains, slots, base, turn, out, buf, sems, cols, block):
    tiles = out.shape[4] // LANES
    facet = lax.axis_index("facet")
    zero = jnp.zeros((1, LANES), F32)
    first_tiles, _ = places_of(turn, cols)
    copies = []
    for c in range(cols):
        is_low = lanes_of((1, LANES)).astype(F32) >= turn[24 + c : 25 + c, :]
        for i, slot in enumerate(slots):
            rows = rows_of(facet, slot, block)
            main, at_main = mains[i]
            values = window_of(main, at_main, c, turn)
            for part in range(2):
                base[part, i, c] = values[part]
                buf[c, 0, part, i] = jnp.where(is_low, values[part], zero).astype(BF16)
                buf[c, 1, part, i] = jnp.where(is_low, zero, values[part]).astype(BF16)
            for side in range(2):
                which = first_tiles[c] + side
                at = pl.multiple_of(jnp.clip(which, 0, tiles - 1) * LANES, LANES)
                copy = pltpu.make_async_copy(
                    buf.at[c, side, :, i],
                    out.at[c, 0, :, rows, pl.ds(at, LANES)],
                    sems.at[c, side, i],
                )
                inside = jnp.logical_and(which > 0, which < tiles - 1)
                pl.when(inside)(copy.start)
                copies.append((inside, copy))
    return copies


def ends_of(edges, slots, base, turn, edge_turn, out, buf, sems, cols, block):
    shard = out.shape[4]
    tiles = shard // LANES
    facet = lax.axis_index("facet")
    left = lanes_of((1, LANES)) < HALF
    zero = jnp.zeros((1, LANES), F32)
    copies = []
    for c in range(cols):
        edge_cosine = edge_turn[c : c + 1, :]
        edge_sine = edge_turn[8 + c : 9 + c, :]
        tile_at = turn[16 + c : 17 + c, :]
        in_first = tile_at == 0
        in_last = tile_at == tiles - 1
        for i, slot in enumerate(slots):
            rows = rows_of(facet, slot, block)
            edge, at_edge = edges[i]
            prev = edge[0, at_edge, c].astype(F32)
            nxt = edge[1, at_edge, c].astype(F32)
            real = jnp.where(left, prev, pltpu.roll(nxt, HALF, 1))
            imag = jnp.where(left, pltpu.roll(prev, HALF, 1), nxt)
            ends = (
                real * edge_cosine - imag * edge_sine,
                imag * edge_cosine + real * edge_sine,
            )
            for part in range(2):
                value = base[part, i, c]
                end = ends[part]
                buf[c, 0, part, i] = (
                    jnp.where(left, end, zero) + jnp.where(in_first, value, zero)
                ).astype(BF16)
                buf[c, 1, part, i] = (
                    jnp.where(left, zero, end) + jnp.where(in_last, value, zero)
                ).astype(BF16)
            for side, start in enumerate((0, shard - LANES)):
                copy = pltpu.make_async_copy(
                    buf.at[c, side, :, i],
                    out.at[c, 0, :, rows, pl.ds(start, LANES)],
                    sems.at[c, side, i],
                )
                copy.start()
                copies.append(copy)
    return copies


def finish(windows, ends):
    for inside, copy in windows:
        pl.when(inside)(copy.wait)
    for copy in ends:
        copy.wait()


def each(array, count):
    return [(array, i) for i in range(count)]


def early_kernel(
    cols,
    turn,
    edge_turn,
    own,
    near,
    own_edge,
    held,
    whole,
    out,
    grids,
    near_base,
    base,
    buf,
    sems,
    end_buf,
    end_sems,
    grid_sem,
):
    block = own.shape[3]
    store = pltpu.make_async_copy(held, grids, grid_sem)
    store.start()
    first = buf.at[:, :, :, 0:1], sems.at[:, :, 0:1]
    second = buf.at[:, :, :, 1:2], sems.at[:, :, 1:2]
    windows = windows_of(((own, 0),), (0,), base, turn, out, *first, cols, block)
    ends = ends_of(((own_edge, 0),), (0,), base, turn, edge_turn, out, end_buf, end_sems, cols, block)
    windows += windows_of(((near, 0),), (1,), near_base, turn, out, *second, cols, block)
    finish(windows, (*ends, store))


def window_kernel(
    cols,
    slots,
    turn,
    edge_turn,
    main,
    near_edge,
    near_base,
    whole,
    out,
    base,
    buf,
    sems,
    end_buf,
    end_sems,
):
    block = main.shape[3]
    mains = each(main, len(slots))
    windows = windows_of(mains, slots, base, turn, out, buf, sems, cols, block)
    edges = ((near_edge, 0),)
    ends = ends_of(edges, (1,), near_base, turn, edge_turn, out, end_buf, end_sems, cols, block)
    finish(windows, ends)


def middle_kernel(
    cols,
    slots,
    end_slots,
    turn,
    edge_turn,
    main,
    edge,
    edge_base,
    whole,
    out,
    base,
    buf,
    sems,
    end_buf,
    end_sems,
):
    block = main.shape[3]
    count = len(slots)
    windows = windows_of(each(main, count), slots, base, turn, out, buf, sems, cols, block)
    ends = ends_of(
        each(edge, count),
        end_slots,
        edge_base,
        turn,
        edge_turn,
        out,
        end_buf,
        end_sems,
        cols,
        block,
    )
    finish(windows, ends)


def end_kernel(cols, slots, turn, edge_turn, edge, base, whole, out, buf, sems):
    block = edge.shape[3]
    edges = each(edge, len(slots))
    finish((), ends_of(edges, slots, base, turn, edge_turn, out, buf, sems, cols, block))


def swapped(block, bit):
    facets = lax.axis_size("facet")
    return lax.ppermute(block, "facet", [(i, i ^ bit) for i in range(facets)])


def shifted(block, distance):
    count = lax.axis_size("col")
    return lax.ppermute(block, "col", [(i, (i + distance) % count) for i in range(count)])


def added(kept, received):
    return (kept.astype(F32) + received.astype(F32)).astype(BF16)


def reduced(kept, sent, facets):
    rest = added(kept, swapped(sent, 1))
    came = []
    bit = 2
    while bit < facets:
        received = swapped(rest[:, 0::2], bit)
        came.append(received[:, :1])
        if rest.shape[1] > 1:
            rest = added(rest[:, 1::2], received[:, 1:])
        bit *= 2
    return came


def gathered(blocks, facets):
    bit = facets // 2
    while bit > 2:
        received = swapped(blocks, bit)
        shape = (blocks.shape[0], -1) + blocks.shape[2:]
        blocks = jnp.stack([blocks, received], axis=2).reshape(shape)
        bit //= 2
    received = swapped(blocks, bit)
    if blocks.shape[1] == 1:
        return received
    shape = (blocks.shape[0], -1) + blocks.shape[2:]
    return jnp.stack([blocks, received], axis=2).reshape(shape)[:, 1:]


def params(mib):
    return pltpu.CompilerParams(vmem_limit_bytes=mib * 1024 * 1024)


def computed(facet_spectra, facet_offsets, column_index, subgrid_offsets, weights):
    cols = facet_spectra.shape[0]
    shard = facet_spectra.shape[4]
    facets = lax.axis_size("facet")
    length = shard * lax.axis_size("col")
    block = XM // facets
    facet_spectra, facet_offsets, column_index, places = (
        pltpu.with_memory_space_constraint(array, pltpu.HBM)
        for array in (facet_spectra, facet_offsets, column_index, subgrid_offsets.T)
    )

    fewer = jax.ShapeDtypeStruct((2, facets // 2 - 1, cols, block, LANES), BF16)
    single = jax.ShapeDtypeStruct((2, 1, cols, block, LANES), BF16)
    tile_pair = pltpu.VMEM((cols, 2, 2, XM, LANES), BF16)
    pair_sems = pltpu.SemaphoreType.DMA((cols, 2, facets))
    whole_scalars = [
        pltpu.SMEM(facet_offsets.shape, jnp.int32),
        pltpu.SMEM(column_index.shape, jnp.int32),
    ]
    edge_send, edge_turn = pl.pallas_call(
        functools.partial(edge_kernel, cols, facets, length),
        out_shape=(fewer, jax.ShapeDtypeStruct((16, LANES), F32)),
        in_specs=[HBM, HBM, HBM],
        out_specs=(VMEM, VMEM),
        scratch_shapes=[tile_pair, pair_sems, *whole_scalars, pltpu.SemaphoreType.DMA((2,))],
        compiler_params=params(12),
        name="edge",
    )(facet_offsets, column_index, facet_spectra)
    edge_keep, turn = pl.pallas_call(
        functools.partial(hold_kernel, cols, facets, length),
        out_shape=(fewer, jax.ShapeDtypeStruct((32, LANES), F32)),
        in_specs=[HBM, HBM, HBM, HBM, VMEM],
        out_specs=(VMEM, VMEM),
        scratch_shapes=[
            tile_pair,
            pair_sems,
            *whole_scalars,
            pltpu.SMEM(places.shape, jnp.int32),
            pltpu.SemaphoreType.DMA((3,)),
        ],
        compiler_params=params(12),
        name="hold",
    )(facet_offsets, column_index, places, facet_spectra, edge_turn)
    came = reduced(edge_keep, edge_send, facets)

    main_far, main_rest, main_send, main_keep, near_send, near_keep = pl.pallas_call(
        functools.partial(main_kernel, cols, facets),
        out_shape=(fewer, fewer, single, single, single, single),
        in_specs=[HBM, VMEM, VMEM],
        out_specs=(VMEM,) * 6,
        scratch_shapes=[tile_pair, pair_sems, tile_pair, pair_sems],
        compiler_params=params(12),
        name="main",
    )(facet_spectra, turn, edge_turn)
    came.append(swapped(near_send, 1))
    total = near_keep.astype(F32)
    for block_sum in came:
        total = total + block_sum.astype(F32)
    edges = total.astype(BF16)
    *more, main_received = reduced(main_rest, main_far, facets)
    for block_sum in more:
        main_keep = added(main_keep, block_sum)
    main_near = swapped(main_send, 1)
    from_prev = shifted(edges[1], 1)
    from_next = shifted(edges[0], -1)

    table = pl.pallas_call(
        functools.partial(table_kernel, facets),
        out_shape=jax.ShapeDtypeStruct((2 * WM, 2 * XM), BF16),
        in_specs=[VMEM],
        out_specs=VMEM,
        compiler_params=params(12),
        name="table",
    )(edge_turn)
    shape = jax.ShapeDtypeStruct((cols, 1, 2, XM, shard), BF16)
    updates = pl.pallas_call(
        zero_kernel,
        out_shape=shape,
        in_specs=[VMEM],
        out_specs=HBM,
        scratch_shapes=[
            pltpu.VMEM((LANES, shard - 2 * LANES), BF16),
            pltpu.SemaphoreType.DMA((cols, 2, XM // LANES)),
        ],
        compiler_params=params(12),
        name="zero",
    )(turn)

    edge = jax.ShapeDtypeStruct((1, cols, block, LANES), BF16)
    grid_shape = jax.ShapeDtypeStruct((cols, 1, 2, block, XM), BF16)
    held, back, to_prev, to_next = pl.pallas_call(
        functools.partial(subgrid_kernel, cols, shard),
        out_shape=(
            grid_shape,
            jax.ShapeDtypeStruct((2, 1, cols, block, LANES), BF16),
            edge,
            edge,
        ),
        in_specs=[VMEM] * 8,
        out_specs=(VMEM, VMEM, VMEM, VMEM),
        scratch_shapes=[
            pltpu.VMEM((cols * block, 2 * WM), BF16),
            pltpu.VMEM((cols * block, 2 * XM), BF16),
        ],
        compiler_params=params(12),
        name="subgrid",
    )(turn, main_keep, main_near, main_received, from_prev, from_next, table, weights)

    came_prev = shifted(to_next, 1)
    came_next = shifted(to_prev, -1)
    near = swapped(back, 1)
    far_half = gathered(back, facets)
    far = swapped(far_half, 1)
    own_edge = jnp.stack([came_prev, came_next])
    near_edge = swapped(own_edge, 1)
    rest_edge = gathered(own_edge, facets)
    far_edge = swapped(rest_edge, 1)
    evens = tuple(range(2, facets, 2))
    odds = tuple(range(3, facets, 2))

    def tiles_for(count):
        return [
            pltpu.VMEM((cols, 2, 2, count, block, LANES), BF16),
            pltpu.SemaphoreType.DMA((cols, 2, count)),
        ]

    base = jax.ShapeDtypeStruct((2, len(evens), cols, block, LANES), F32)
    near_shape = jax.ShapeDtypeStruct((2, 1, cols, block, LANES), F32)
    updates, grids, near_base = pl.pallas_call(
        functools.partial(early_kernel, cols),
        out_shape=(shape, grid_shape, near_shape),
        in_specs=[VMEM] * 6 + [HBM],
        out_specs=(HBM, HBM, VMEM),
        scratch_shapes=[
            pltpu.VMEM(near_shape.shape, F32),
            *tiles_for(2),
            *tiles_for(1),
            pltpu.SemaphoreType.DMA(()),
        ],
        input_output_aliases={6: 0},
        compiler_params=params(12),
        name="early",
    )(turn, edge_turn, back, near, own_edge, held, updates)
    updates, rest_base = pl.pallas_call(
        functools.partial(window_kernel, cols, evens),
        out_shape=(shape, base),
        in_specs=[VMEM] * 5 + [HBM],
        out_specs=(HBM, VMEM),
        scratch_shapes=[*tiles_for(len(evens)), *tiles_for(1)],
        input_output_aliases={5: 0},
        compiler_params=params(12),
        name="window",
    )(turn, edge_turn, far_half, near_edge, near_base, updates)
    updates, far_base = pl.pallas_call(
        functools.partial(middle_kernel, cols, odds, evens),
        out_shape=(shape, base),
        in_specs=[VMEM] * 5 + [HBM],
        out_specs=(HBM, VMEM),
        scratch_shapes=tiles_for(len(evens)) * 2,
        input_output_aliases={5: 0},
        compiler_params=params(12),
        name="middle",
    )(turn, edge_turn, far, rest_edge, rest_base, updates)
    updates = pl.pallas_call(
        functools.partial(end_kernel, cols, odds),
        out_shape=shape,
        in_specs=[VMEM] * 4 + [HBM],
        out_specs=HBM,
        scratch_shapes=tiles_for(len(odds)),
        input_output_aliases={4: 0},
        compiler_params=params(12),
        name="end",
    )(turn, edge_turn, far_edge, far_base, updates)
    return grids, updates


def solution(mesh):
    in_specs = (
        P(None, "facet", None, None, "col"),
        P("facet", None),
        P(),
        P(None, "col"),
        P(None, "col", "facet", None),
    )
    out_specs = (P(None, "col", None, "facet", None), P(None, "facet", None, None, "col"))
    return jax.shard_map(
        computed, mesh=mesh, in_specs=in_specs, out_specs=out_specs, check_vma=False
    )
```

```python
import functools
import math

import jax
import jax.numpy as jnp
from jax import lax
from jax.experimental import pallas as pl
from jax.experimental.pallas import tpu as pltpu
from jax.sharding import PartitionSpec as P


IMAGE = 65536
XM = 512
WM = 128
XA = 448
LANES = 128
HALF = WM // 2

TAU = 2.0 * math.pi
BF16 = jnp.bfloat16
F32 = jnp.float32

VMEM = pl.BlockSpec(memory_space=pltpu.VMEM)
SMEM = pl.BlockSpec(memory_space=pltpu.SMEM)
HBM = pl.BlockSpec(memory_space=pltpu.HBM)


def remainder(value, modulus):
    if modulus & (modulus - 1) == 0:
        return value & (modulus - 1)
    return lax.rem(value, jnp.int32(modulus))


def modular(first, second, image):
    upper = second // 256
    lower = remainder(second, 256)
    return remainder(remainder(first * upper, image // 256) * 256 + first * lower, image)


def place_of(subgrid_offset, here, shard, length):
    start = subgrid_offset // (IMAGE // length) - here * shard - HALF + LANES
    return lax.div(start, jnp.int32(LANES)) - 1, remainder(start, LANES)


def lanes_of(shape):
    return lax.broadcasted_iota(jnp.int32, shape, len(shape) - 1)


def turns_of(turn, index, firsts, second, length):
    rows = lax.broadcasted_iota(jnp.int32, (8, LANES), 0)
    first = jnp.zeros((8, LANES), F32)
    for c, value in enumerate(firsts):
        first = jnp.where(rows == c, value.astype(F32), first)
    steps = remainder(index * second, length).astype(F32)
    angle = TAU * (first / IMAGE + steps / length)
    turn[0:8, :] = jnp.cos(angle)
    turn[8:16, :] = jnp.sin(angle)


def firsts_of(cols, offsets, column):
    return [modular(column[c] * XA, offsets[0, 0], IMAGE) for c in range(cols)]


def rows_of(facet, s, block):
    return pl.ds(pl.multiple_of((facet ^ s) * block, block), block)


def fetched(spectra, buf, sems, c, s, rows, places):
    copies = []
    for slot, at in enumerate(places):
        copy = pltpu.make_async_copy(
            spectra.at[c, 0, :, rows, pl.ds(at, LANES)],
            buf.at[c, slot, :, rows, :],
            sems.at[c, slot, s],
        )
        copy.start()
        copies.append(copy)
    return copies


def turned(parts, cosine, sine):
    return parts[0] * cosine + parts[1] * sine, parts[1] * cosine - parts[0] * sine


def places_of(turn, cols):
    tiles = [jnp.min(turn[16 + c : 17 + c, :]).astype(jnp.int32) for c in range(cols)]
    lanes = [jnp.max(turn[24 + c : 25 + c, :]).astype(jnp.int32) for c in range(cols)]
    return tiles, lanes


def edges_of(target, buf, copies, turn, order, cols, block, facet):
    left = lanes_of((1, LANES)) < HALF
    for c in range(cols):
        cosine = turn[c : c + 1, :]
        sine = turn[8 + c : 9 + c, :]
        for i, s in enumerate(order):
            for copy in copies[c, s]:
                copy.wait()
            rows = rows_of(facet, s, block)
            parts = [
                jnp.where(
                    left,
                    buf[c, 0, part, rows, :].astype(F32),
                    buf[c, 1, part, rows, :].astype(F32),
                )
                for part in range(2)
            ]
            real, imag = turned(parts, cosine, sine)
            low = jnp.where(left, real, pltpu.roll(imag, HALF, 1))
            high = jnp.where(left, pltpu.roll(real, HALF, 1), imag)
            target[0, i, c] = low.astype(BF16)
            target[1, i, c] = high.astype(BF16)


def edge_kernel(
    cols, facets, length, offsets, column, spectra, send, turn, buf, sems, own, held, small
):
    shard = spectra.shape[4]
    block = XM // facets
    here = lax.axis_index("col")
    facet = lax.axis_index("facet")
    scalars = [
        pltpu.make_async_copy(offsets, own, small.at[0]),
        pltpu.make_async_copy(column, held, small.at[1]),
    ]
    for copy in scalars:
        copy.start()
    copies = {}
    order = range(3, facets, 2)
    for c in range(cols):
        for s in order:
            rows = rows_of(facet, s, block)
            copies[c, s] = fetched(spectra, buf, sems, c, s, rows, (0, shard - LANES))
    for copy in scalars:
        copy.wait()
    lanes = lanes_of((8, LANES))
    index = here * shard + lanes + jnp.where(lanes < HALF, 0, shard - LANES)
    turns_of(turn, index, firsts_of(cols, own, held), own[0, 1], length)
    edges_of(send, buf, copies, turn, order, cols, block, facet)


def hold_kernel(
    cols,
    facets,
    length,
    offsets,
    column,
    subgrid,
    spectra,
    edge_turn,
    keep,
    turn,
    buf,
    sems,
    own,
    held,
    spots,
    small,
):
    shard = spectra.shape[4]
    block = XM // facets
    here = lax.axis_index("col")
    facet = lax.axis_index("facet")
    scalars = [
        pltpu.make_async_copy(offsets, own, small.at[0]),
        pltpu.make_async_copy(column, held, small.at[1]),
        pltpu.make_async_copy(subgrid, spots, small.at[2]),
    ]
    for copy in scalars:
        copy.start()
    copies = {}
    order = range(2, facets, 2)
    for c in range(cols):
        for s in order:
            rows = rows_of(facet, s, block)
            copies[c, s] = fetched(spectra, buf, sems, c, s, rows, (0, shard - LANES))
    for copy in scalars:
        copy.wait()
    lanes = lanes_of((8, LANES))
    rows = lax.broadcasted_iota(jnp.int32, (8, LANES), 0)
    tile_at = jnp.zeros((8, LANES), jnp.int32)
    begins = jnp.zeros((8, LANES), jnp.int32)
    for c in range(cols):
        tile, lane = place_of(spots[0, c], here, shard, length)
        tile_at = jnp.where(rows == c, jnp.where(lanes >= lane, tile, tile + 1), tile_at)
        begins = jnp.where(rows == c, lane, begins)
    index = remainder(here * shard + lanes + tile_at * LANES + length, length)
    turns_of(turn, index, firsts_of(cols, own, held), own[0, 1], length)
    turn[16:24, :] = tile_at.astype(F32)
    turn[24:32, :] = begins.astype(F32)
    edges_of(keep, buf, copies, edge_turn, order, cols, block, facet)


def main_kernel(
    cols,
    facets,
    spectra,
    turn,
    edge_turn,
    send,
    keep,
    main_send,
    main_keep,
    near_send,
    near_keep,
    buf,
    sems,
    edge_buf,
    edge_sems,
):
    shard = spectra.shape[4]
    tiles = shard // LANES
    block = XM // facets
    facet = lax.axis_index("facet")
    near = {}
    for c in range(cols):
        for s in range(2):
            rows = rows_of(facet, s, block)
            near[c, s] = fetched(spectra, edge_buf, edge_sems, c, s, rows, (0, shard - LANES))
    copies = {}
    first_tiles, _ = places_of(turn, cols)
    for c in range(cols):
        tile = first_tiles[c]
        low = pl.multiple_of(jnp.maximum(tile, 0) * LANES, LANES)
        high = pl.multiple_of(jnp.minimum(tile + 1, tiles - 1) * LANES, LANES)
        for s in range(facets):
            rows = rows_of(facet, s, block)
            copies[c, s] = fetched(spectra, buf, sems, c, s, rows, (low, high))
    edges_of(near_send, edge_buf, near, edge_turn, (1,), cols, block, facet)
    edges_of(near_keep, edge_buf, near, edge_turn, (0,), cols, block, facet)
    zero = jnp.zeros((1, LANES), F32)
    for c in range(cols):
        tile_at = turn[16 + c : 17 + c, :]
        is_low = lanes_of((1, LANES)).astype(F32) >= turn[24 + c : 25 + c, :]
        inside = jnp.logical_and(tile_at >= 0, tile_at <= tiles - 1)
        cosine = jnp.where(inside, turn[c : c + 1, :], zero)
        sine = jnp.where(inside, turn[8 + c : 9 + c, :], zero)
        for s in range(facets):
            for copy in copies[c, s]:
                copy.wait()
            rows = rows_of(facet, s, block)
            if s < 2:
                target, at = (main_send if s else main_keep), 0
            else:
                target, at = (send if s % 2 else keep), s // 2 - 1
            parts = [
                jnp.where(
                    is_low,
                    buf[c, 0, part, rows, :].astype(F32),
                    buf[c, 1, part, rows, :].astype(F32),
                )
                for part in range(2)
            ]
            real, imag = turned(parts, cosine, sine)
            target[0, at, c] = real.astype(BF16)
            target[1, at, c] = imag.astype(BF16)


def table_kernel(facets, after, table):
    del after
    place = lax.broadcasted_iota(jnp.int32, (WM, LANES), 0)
    cell = lanes_of((WM, LANES))
    angle = TAU * remainder((place - HALF) * cell + HALF * XM, XM).astype(F32) / XM
    relative = (place.astype(F32) + 0.5 - WM / 2.0) / (WM / 2.0)
    taper = (0.3 + 0.7 * (1.0 - relative * relative)) / jnp.sqrt(
        jnp.full((1, LANES), WM * facets, F32)
    )
    cosine = taper * jnp.cos(angle)
    sine = taper * jnp.sin(angle)
    for tile in range(XM // LANES):
        first = tile * LANES - XM // 2
        quarter = remainder((place - HALF) * (first * 4 // XM) + HALF * 4, 4)
        odd = remainder(quarter, 2) == 1
        real = jnp.where(odd, sine, cosine)
        imag = jnp.where(odd, cosine, sine)
        real = jnp.where(jnp.logical_or(quarter == 1, quarter == 2), -real, real).astype(BF16)
        imag = jnp.where(quarter >= 2, -imag, imag)
        span = slice(tile * LANES, (tile + 1) * LANES)
        other = slice(XM + tile * LANES, XM + (tile + 1) * LANES)
        table[:WM, span] = real
        table[WM:, other] = real
        table[:WM, other] = imag.astype(BF16)
        table[WM:, span] = (-imag).astype(BF16)


def zero_kernel(after, out, buf, sems):
    del after
    cols, _, _, height, _ = out.shape
    block, width = buf.shape
    buf[...] = jnp.zeros(buf.shape, BF16)
    copies = []
    for c in range(cols):
        for part in range(2):
            for i in range(height // block):
                place = out.at[c, 0, part, pl.ds(i * block, block), pl.ds(LANES, width)]
                copies.append(pltpu.make_async_copy(buf, place, sems.at[c, part, i]))
    for copy in copies:
        copy.start()
    for copy in copies:
        copy.wait()


def subgrid_kernel(
    cols,
    shard,
    turn,
    kept,
    near,
    received,
    from_prev,
    from_next,
    table,
    weights,
    grids,
    back,
    to_prev,
    to_next,
    stack,
    scaled,
):
    tiles = shard // LANES
    block = kept.shape[3]
    zero = jnp.zeros((1, LANES), F32)
    _, begins = places_of(turn, cols)
    for c in range(cols):
        held = turn[16 + c : 17 + c, :]
        low = held < 0
        high = held > tiles - 1
        prev = from_prev[0, c].astype(F32)
        nxt = from_next[0, c].astype(F32)
        shift = remainder(LANES - begins[c], LANES)
        real, imag = (
            kept[part, 0, c].astype(F32)
            + near[part, 0, c].astype(F32)
            + received[part, 0, c].astype(F32)
            for part in range(2)
        )
        real = real + jnp.where(low, pltpu.roll(prev, HALF, 1), jnp.where(high, nxt, zero))
        imag = imag + jnp.where(low, prev, jnp.where(high, pltpu.roll(nxt, HALF, 1), zero))
        rows = slice(c * block, (c + 1) * block)
        stack[rows, :WM] = pltpu.roll(real, shift, 1).astype(BF16)
        stack[rows, WM:] = pltpu.roll(imag, shift, 1).astype(BF16)
    for part in range(2):
        span = slice(part * XM, (part + 1) * XM)
        product = jnp.dot(stack[...], table[:, span], preferred_element_type=F32)
        rounded = product.astype(BF16)
        for c in range(cols):
            rows = slice(c * block, (c + 1) * block)
            piece = rounded[rows]
            grids[c, 0, part] = piece
            scaled[rows, span] = (piece.astype(F32) * weights[c, 0].astype(F32)).astype(BF16)
    result = lax.dot_general(
        scaled[...],
        table[...],
        (((1,), (1,)), ((), ())),
        preferred_element_type=F32,
    )
    for c in range(cols):
        held = turn[16 + c : 17 + c, :]
        rows = slice(c * block, (c + 1) * block)
        low = held < 0
        high = held > tiles - 1
        real = pltpu.roll(result[rows, :WM], begins[c], 1)
        imag = pltpu.roll(result[rows, WM:], begins[c], 1)
        back[0, 0, c] = real.astype(BF16)
        back[1, 0, c] = imag.astype(BF16)
        real_low = jnp.where(low, real, zero)
        imag_low = jnp.where(low, imag, zero)
        real_high = jnp.where(high, real, zero)
        imag_high = jnp.where(high, imag, zero)
        to_prev[0, c] = (pltpu.roll(real_low, HALF, 1) + imag_low).astype(BF16)
        to_next[0, c] = (real_high + pltpu.roll(imag_high, HALF, 1)).astype(BF16)


def window_of(main, i, c, turn):
    cosine = turn[c : c + 1, :]
    sine = turn[8 + c : 9 + c, :]
    real = main[0, i, c].astype(F32)
    imag = main[1, i, c].astype(F32)
    return real * cosine - imag * sine, imag * cosine + real * sine


def windows_of(mains, slots, base, turn, out, buf, sems, cols, block):
    tiles = out.shape[4] // LANES
    facet = lax.axis_index("facet")
    zero = jnp.zeros((1, LANES), F32)
    first_tiles, _ = places_of(turn, cols)
    copies = []
    for c in range(cols):
        is_low = lanes_of((1, LANES)).astype(F32) >= turn[24 + c : 25 + c, :]
        for i, slot in enumerate(slots):
            rows = rows_of(facet, slot, block)
            main, at_main = mains[i]
            values = window_of(main, at_main, c, turn)
            for part in range(2):
                base[part, i, c] = values[part]
                buf[c, 0, part, i] = jnp.where(is_low, values[part], zero).astype(BF16)
                buf[c, 1, part, i] = jnp.where(is_low, zero, values[part]).astype(BF16)
            for side in range(2):
                which = first_tiles[c] + side
                at = pl.multiple_of(jnp.clip(which, 0, tiles - 1) * LANES, LANES)
                copy = pltpu.make_async_copy(
                    buf.at[c, side, :, i],
                    out.at[c, 0, :, rows, pl.ds(at, LANES)],
                    sems.at[c, side, i],
                )
                inside = jnp.logical_and(which > 0, which < tiles - 1)
                pl.when(inside)(copy.start)
                copies.append((inside, copy))
    return copies


def ends_of(edges, slots, base, turn, edge_turn, out, buf, sems, cols, block):
    shard = out.shape[4]
    tiles = shard // LANES
    facet = lax.axis_index("facet")
    left = lanes_of((1, LANES)) < HALF
    zero = jnp.zeros((1, LANES), F32)
    copies = []
    for c in range(cols):
        edge_cosine = edge_turn[c : c + 1, :]
        edge_sine = edge_turn[8 + c : 9 + c, :]
        tile_at = turn[16 + c : 17 + c, :]
        in_first = tile_at == 0
        in_last = tile_at == tiles - 1
        for i, slot in enumerate(slots):
            rows = rows_of(facet, slot, block)
            edge, at_edge = edges[i]
            prev = edge[0, at_edge, c].astype(F32)
            nxt = edge[1, at_edge, c].astype(F32)
            real = jnp.where(left, prev, pltpu.roll(nxt, HALF, 1))
            imag = jnp.where(left, pltpu.roll(prev, HALF, 1), nxt)
            ends = (
                real * edge_cosine - imag * edge_sine,
                imag * edge_cosine + real * edge_sine,
            )
            for side, start in enumerate((0, shard - LANES)):
                keep = left if side == 0 else jnp.logical_not(left)
                inside = in_last if side else in_first
                for part in range(2):
                    buf[c, side, part, i] = (
                        jnp.where(keep, ends[part], zero)
                        + jnp.where(inside, base[part, i, c], zero)
                    ).astype(BF16)
                copy = pltpu.make_async_copy(
                    buf.at[c, side, :, i],
                    out.at[c, 0, :, rows, pl.ds(start, LANES)],
                    sems.at[c, side, i],
                )
                copy.start()
                copies.append(copy)
    return copies


def finish(windows, ends):
    for inside, copy in windows:
        pl.when(inside)(copy.wait)
    for copy in ends:
        copy.wait()


def each(array, count):
    return [(array, i) for i in range(count)]


def early_kernel(
    cols,
    turn,
    edge_turn,
    own,
    near,
    own_edge,
    held,
    whole,
    out,
    grids,
    near_base,
    base,
    buf,
    sems,
    end_buf,
    end_sems,
    grid_sem,
):
    block = own.shape[3]
    store = pltpu.make_async_copy(held, grids, grid_sem)
    store.start()
    first = buf.at[:, :, :, 0:1], sems.at[:, :, 0:1]
    second = buf.at[:, :, :, 1:2], sems.at[:, :, 1:2]
    windows = windows_of(((own, 0),), (0,), base, turn, out, *first, cols, block)
    ends = ends_of(((own_edge, 0),), (0,), base, turn, edge_turn, out, end_buf, end_sems, cols, block)
    windows += windows_of(((near, 0),), (1,), near_base, turn, out, *second, cols, block)
    finish(windows, (*ends, store))


def window_kernel(
    cols,
    slots,
    turn,
    edge_turn,
    main,
    near_edge,
    near_base,
    whole,
    out,
    base,
    buf,
    sems,
    end_buf,
    end_sems,
):
    block = main.shape[3]
    mains = each(main, len(slots))
    windows = windows_of(mains, slots, base, turn, out, buf, sems, cols, block)
    edges = ((near_edge, 0),)
    ends = ends_of(edges, (1,), near_base, turn, edge_turn, out, end_buf, end_sems, cols, block)
    finish(windows, ends)


def middle_kernel(
    cols,
    slots,
    end_slots,
    turn,
    edge_turn,
    main,
    edge,
    edge_base,
    whole,
    out,
    base,
    buf,
    sems,
    end_buf,
    end_sems,
):
    block = main.shape[3]
    count = len(slots)
    windows = windows_of(each(main, count), slots, base, turn, out, buf, sems, cols, block)
    ends = ends_of(
        each(edge, count),
        end_slots,
        edge_base,
        turn,
        edge_turn,
        out,
        end_buf,
        end_sems,
        cols,
        block,
    )
    finish(windows, ends)


def end_kernel(cols, slots, turn, edge_turn, edge, base, whole, out, buf, sems):
    block = edge.shape[3]
    edges = each(edge, len(slots))
    finish((), ends_of(edges, slots, base, turn, edge_turn, out, buf, sems, cols, block))


def swapped(block, bit):
    facets = lax.axis_size("facet")
    return lax.ppermute(block, "facet", [(i, i ^ bit) for i in range(facets)])


def shifted(block, distance):
    count = lax.axis_size("col")
    return lax.ppermute(block, "col", [(i, (i + distance) % count) for i in range(count)])


def added(kept, received):
    return (kept.astype(F32) + received.astype(F32)).astype(BF16)


def reduced(kept, sent, facets):
    rest = added(kept, swapped(sent, 1))
    came = []
    bit = 2
    while bit < facets:
        received = swapped(rest[:, 0::2], bit)
        came.append(received[:, :1])
        if rest.shape[1] > 1:
            rest = added(rest[:, 1::2], received[:, 1:])
        bit *= 2
    return came


def gathered(blocks, facets):
    bit = facets // 2
    while bit > 2:
        received = swapped(blocks, bit)
        shape = (blocks.shape[0], -1) + blocks.shape[2:]
        blocks = jnp.stack([blocks, received], axis=2).reshape(shape)
        bit //= 2
    received = swapped(blocks, bit)
    if blocks.shape[1] == 1:
        return received
    shape = (blocks.shape[0], -1) + blocks.shape[2:]
    return jnp.stack([blocks, received], axis=2).reshape(shape)[:, 1:]


def params(mib):
    return pltpu.CompilerParams(vmem_limit_bytes=mib * 1024 * 1024)


def computed(facet_spectra, facet_offsets, column_index, subgrid_offsets, weights):
    cols = facet_spectra.shape[0]
    shard = facet_spectra.shape[4]
    facets = lax.axis_size("facet")
    length = shard * lax.axis_size("col")
    block = XM // facets
    facet_spectra, facet_offsets, column_index, places = (
        pltpu.with_memory_space_constraint(array, pltpu.HBM)
        for array in (facet_spectra, facet_offsets, column_index, subgrid_offsets.T)
    )

    fewer = jax.ShapeDtypeStruct((2, facets // 2 - 1, cols, block, LANES), BF16)
    single = jax.ShapeDtypeStruct((2, 1, cols, block, LANES), BF16)
    tile_pair = pltpu.VMEM((cols, 2, 2, XM, LANES), BF16)
    pair_sems = pltpu.SemaphoreType.DMA((cols, 2, facets))
    whole_scalars = [
        pltpu.SMEM(facet_offsets.shape, jnp.int32),
        pltpu.SMEM(column_index.shape, jnp.int32),
    ]
    edge_send, edge_turn = pl.pallas_call(
        functools.partial(edge_kernel, cols, facets, length),
        out_shape=(fewer, jax.ShapeDtypeStruct((16, LANES), F32)),
        in_specs=[HBM, HBM, HBM],
        out_specs=(VMEM, VMEM),
        scratch_shapes=[tile_pair, pair_sems, *whole_scalars, pltpu.SemaphoreType.DMA((2,))],
        compiler_params=params(12),
        name="edge",
    )(facet_offsets, column_index, facet_spectra)
    edge_keep, turn = pl.pallas_call(
        functools.partial(hold_kernel, cols, facets, length),
        out_shape=(fewer, jax.ShapeDtypeStruct((32, LANES), F32)),
        in_specs=[HBM, HBM, HBM, HBM, VMEM],
        out_specs=(VMEM, VMEM),
        scratch_shapes=[
            tile_pair,
            pair_sems,
            *whole_scalars,
            pltpu.SMEM(places.shape, jnp.int32),
            pltpu.SemaphoreType.DMA((3,)),
        ],
        compiler_params=params(12),
        name="hold",
    )(facet_offsets, column_index, places, facet_spectra, edge_turn)
    came = reduced(edge_keep, edge_send, facets)

    main_far, main_rest, main_send, main_keep, near_send, near_keep = pl.pallas_call(
        functools.partial(main_kernel, cols, facets),
        out_shape=(fewer, fewer, single, single, single, single),
        in_specs=[HBM, VMEM, VMEM],
        out_specs=(VMEM,) * 6,
        scratch_shapes=[tile_pair, pair_sems, tile_pair, pair_sems],
        compiler_params=params(12),
        name="main",
    )(facet_spectra, turn, edge_turn)
    came.append(swapped(near_send, 1))
    total = near_keep.astype(F32)
    for block_sum in came:
        total = total + block_sum.astype(F32)
    edges = total.astype(BF16)
    *more, main_received = reduced(main_rest, main_far, facets)
    for block_sum in more:
        main_keep = added(main_keep, block_sum)
    main_near = swapped(main_send, 1)
    from_prev = shifted(edges[1], 1)
    from_next = shifted(edges[0], -1)

    table = pl.pallas_call(
        functools.partial(table_kernel, facets),
        out_shape=jax.ShapeDtypeStruct((2 * WM, 2 * XM), BF16),
        in_specs=[VMEM],
        out_specs=VMEM,
        compiler_params=params(12),
        name="table",
    )(edge_turn)
    shape = jax.ShapeDtypeStruct((cols, 1, 2, XM, shard), BF16)
    updates = pl.pallas_call(
        zero_kernel,
        out_shape=shape,
        in_specs=[VMEM],
        out_specs=HBM,
        scratch_shapes=[
            pltpu.VMEM((LANES, shard - 2 * LANES), BF16),
            pltpu.SemaphoreType.DMA((cols, 2, XM // LANES)),
        ],
        compiler_params=params(12),
        name="zero",
    )(turn)

    edge = jax.ShapeDtypeStruct((1, cols, block, LANES), BF16)
    grid_shape = jax.ShapeDtypeStruct((cols, 1, 2, block, XM), BF16)
    held, back, to_prev, to_next = pl.pallas_call(
        functools.partial(subgrid_kernel, cols, shard),
        out_shape=(
            grid_shape,
            jax.ShapeDtypeStruct((2, 1, cols, block, LANES), BF16),
            edge,
            edge,
        ),
        in_specs=[VMEM] * 8,
        out_specs=(VMEM, VMEM, VMEM, VMEM),
        scratch_shapes=[
            pltpu.VMEM((cols * block, 2 * WM), BF16),
            pltpu.VMEM((cols * block, 2 * XM), BF16),
        ],
        compiler_params=params(12),
        name="subgrid",
    )(turn, main_keep, main_near, main_received, from_prev, from_next, table, weights)

    came_prev = shifted(to_next, 1)
    came_next = shifted(to_prev, -1)
    near = swapped(back, 1)
    far_half = gathered(back, facets)
    far = swapped(far_half, 1)
    own_edge = jnp.stack([came_prev, came_next])
    near_edge = swapped(own_edge, 1)
    rest_edge = gathered(own_edge, facets)
    far_edge = swapped(rest_edge, 1)
    evens = tuple(range(2, facets, 2))
    odds = tuple(range(3, facets, 2))

    def tiles_for(count):
        return [
            pltpu.VMEM((cols, 2, 2, count, block, LANES), BF16),
            pltpu.SemaphoreType.DMA((cols, 2, count)),
        ]

    base = jax.ShapeDtypeStruct((2, len(evens), cols, block, LANES), F32)
    near_shape = jax.ShapeDtypeStruct((2, 1, cols, block, LANES), F32)
    updates, grids, near_base = pl.pallas_call(
        functools.partial(early_kernel, cols),
        out_shape=(shape, grid_shape, near_shape),
        in_specs=[VMEM] * 6 + [HBM],
        out_specs=(HBM, HBM, VMEM),
        scratch_shapes=[
            pltpu.VMEM(near_shape.shape, F32),
            *tiles_for(2),
            *tiles_for(1),
            pltpu.SemaphoreType.DMA(()),
        ],
        input_output_aliases={6: 0},
        compiler_params=params(12),
        name="early",
    )(turn, edge_turn, back, near, own_edge, held, updates)
    updates, rest_base = pl.pallas_call(
        functools.partial(window_kernel, cols, evens),
        out_shape=(shape, base),
        in_specs=[VMEM] * 5 + [HBM],
        out_specs=(HBM, VMEM),
        scratch_shapes=[*tiles_for(len(evens)), *tiles_for(1)],
        input_output_aliases={5: 0},
        compiler_params=params(12),
        name="window",
    )(turn, edge_turn, far_half, near_edge, near_base, updates)
    updates, far_base = pl.pallas_call(
        functools.partial(middle_kernel, cols, odds, evens),
        out_shape=(shape, base),
        in_specs=[VMEM] * 5 + [HBM],
        out_specs=(HBM, VMEM),
        scratch_shapes=tiles_for(len(evens)) * 2,
        input_output_aliases={5: 0},
        compiler_params=params(12),
        name="middle",
    )(turn, edge_turn, far, rest_edge, rest_base, updates)
    updates = pl.pallas_call(
        functools.partial(end_kernel, cols, odds),
        out_shape=shape,
        in_specs=[VMEM] * 4 + [HBM],
        out_specs=HBM,
        scratch_shapes=tiles_for(len(odds)),
        input_output_aliases={4: 0},
        compiler_params=params(12),
        name="end",
    )(turn, edge_turn, far_edge, far_base, updates)
    return grids, updates


def solution(mesh):
    in_specs = (
        P(None, "facet", None, None, "col"),
        P("facet", None),
        P(),
        P(None, "col"),
        P(None, "col", "facet", None),
    )
    out_specs = (P(None, "col", None, "facet", None), P(None, "facet", None, None, "col"))
    return jax.shard_map(
        computed, mesh=mesh, in_specs=in_specs, out_specs=out_specs, check_vma=False
    )
```
